32 devices in a mesh: wide: 16 (over z, y, x), narrow: 2 (over core).
Axes of the slice: x: 2, y: 2, z: 4, core: 2. Of those that a mesh axis runs over, the one named last changes fastest.
Arguments:
- tokens: bfloat16 [16384, 1024], P(('wide', 'narrow')), may hold values from -6 to 6
- window_span: int32 [32], P('wide'), may hold values from 1 to 2, as said below
- valid_len: int32 [32], P('wide'), may hold values from 384 to 512, as said below
- norm1_gain: float32 [1024], replicated, may hold values from 0.5 to 1.5
- norm1_shift: float32 [1024], replicated, may hold values from -1.8 to 1.8
- w_query: bfloat16 [1024, 1024], P(None, 'narrow'), may hold values from -0.25 to 0.25
- w_key: bfloat16 [1024, 1024], P(None, 'narrow'), may hold values from -0.25 to 0.25
- w_value: bfloat16 [1024, 1024], P(None, 'narrow'), may hold values from -0.1875 to 0.1875
- w_out: bfloat16 [1024, 1024], P('narrow'), may hold values from -1.5 to 1.5
- norm2_gain: float32 [1024], replicated, may hold values from 0.5 to 1.5
- norm2_shift: float32 [1024], replicated, may hold values from -1.8 to 1.8
- w_gate: bfloat16 [1024, 4096], P(None, 'narrow'), may hold values from -0.1875 to 0.1875
- w_up: bfloat16 [1024, 4096], P(None, 'narrow'), may hold values from -0.1875 to 0.1875
- w_down: bfloat16 [4096, 1024], P('narrow'), may hold values from -0.09375 to 0.09375
- cotangent: bfloat16 [16384, 1024], P(('wide', 'narrow')), may hold values from -6 to 6
Outputs:
- out: float32 [16384, 1024], P(('wide', 'narrow'))
- token_grad: float32 [16384, 1024], P(('wide', 'narrow'))
- norm1_gain_grad: float32 [1024], replicated
- norm1_shift_grad: float32 [1024], replicated
- w_query_grad: float32 [1024, 1024], P(None, 'narrow')
- w_key_grad: float32 [1024, 1024], P(None, 'narrow')
- w_value_grad: float32 [1024, 1024], P(None, 'narrow')
- w_out_grad: float32 [1024, 1024], P('narrow')
- norm2_gain_grad: float32 [1024], replicated
- norm2_shift_grad: float32 [1024], replicated
- w_gate_grad: float32 [1024, 4096], P(None, 'narrow')
- w_up_grad: float32 [1024, 4096], P(None, 'narrow')
- w_down_grad: float32 [4096, 1024], P('narrow')
The draws below stay inside these ranges and needn't reach their ends.
Inputs may be any that keep to these rules, and one draw needn't show every extreme that they name: `window_span`: within each group, blocks 2k and 2k+1 hold the same value: 2 where one window fills both blocks, 1 where each block holds a window of its own. `valid_len`: blocks whose window_span is 2 hold 512.
All inputs are finite; a program needn't handle non-finite values.
Results may differ from the reference program's by a relative error of at most 0.019.
Values may be sent and summed in bfloat16 or wider, within the bound.
A program may use at most 256 MiB of HBM per device.

```python
import jax
import jax.numpy as jnp
from jax import lax

D = 1024
H = 16
HD = 64
FF = 4096
BLOCK = 512
BLOCKS = 2
TOKENS = 16384
N_WIDE = 16


def span_table_draw(key):
    pair_count = N_WIDE * BLOCKS // 2
    pair_long = jax.random.randint(jax.random.fold_in(key, 11), (pair_count,), 0, 2)
    forced = jnp.arange(pair_count)
    pair_long = jnp.where(forced == 0, 1, jnp.where(forced == 1, 0, pair_long))
    return 1 + jnp.repeat(pair_long, 2)


def draw_window_span(key, part):
    return span_table_draw(key).astype(jnp.int32)


def draw_valid_len(key, part):
    span_table = span_table_draw(key)
    short_len = jax.random.randint(jax.random.fold_in(key, 12), (N_WIDE * BLOCKS,), 3 * BLOCK // 4, BLOCK + 1)
    position = jnp.arange(N_WIDE * BLOCKS)
    short_len = jnp.where(position == 2, 3 * BLOCK // 4, short_len)
    return jnp.where(span_table == 2, BLOCK, short_len).astype(jnp.int32)


def shard_levels(rng, dims, split, least, largest):
    factor_of, own = 1.0, jax.random.fold_in(rng, 6)
    for dim, blocks in split:
        draws = jnp.exp(jax.random.uniform(jax.random.fold_in(own, dim), (blocks,), jnp.float32, least / len(split), largest / len(split)))
        factor_of = factor_of * jnp.repeat(draws, dims[dim] // blocks).reshape([-1 if axis == dim else 1 for axis in range(len(dims))])
    return factor_of


def gaussian(key, shape, scale, most, shards=(), held_as=jnp.bfloat16):
    entries = jax.random.normal(key, shape, jnp.float32) * scale
    if len(shards) > 0:
        entries = shard_levels(key, shape, shards, -0.22, 0.18) * entries
    return jnp.clip(entries, min=-most, max=most).astype(held_as)


def setup_inputs(seed: int = 0) -> dict:
    key_of = jax.random.split(jax.random.key(seed), 16)
    return {
        "tokens": gaussian(key_of[0], (TOKENS, D), 1.0, 6.0, ((0, 32),)),
        "window_span": draw_window_span(jax.random.fold_in(key_of[15], 71), 0),
        "valid_len": draw_valid_len(jax.random.fold_in(key_of[15], 71), 0),
        "norm1_gain": jnp.clip(1.0 + 0.1 * jax.random.normal(key_of[3], (D,), jnp.float32), 0.5, 1.5),
        "norm1_shift": gaussian(key_of[4], (D,), 0.3, 1.8, (), jnp.float32),
        "w_query": gaussian(key_of[5], (D, D), (D // 2) ** -0.5, 0.25, ((1, 2),)),
        "w_key": gaussian(key_of[6], (D, D), (D // 2) ** -0.5, 0.25, ((1, 2),)),
        "w_value": gaussian(key_of[7], (D, D), D ** -0.5, 0.1875, ((1, 2),)),
        "w_out": gaussian(key_of[8], (D, D), (D // 64) ** -0.5, 1.5, ((0, 2),)),
        "norm2_gain": jnp.clip(1.0 + 0.1 * jax.random.normal(key_of[9], (D,), jnp.float32), 0.5, 1.5),
        "norm2_shift": gaussian(key_of[10], (D,), 0.3, 1.8, (), jnp.float32),
        "w_gate": gaussian(key_of[11], (D, FF), D ** -0.5, 0.1875, ((1, 2),)),
        "w_up": gaussian(key_of[12], (D, FF), D ** -0.5, 0.1875, ((1, 2),)),
        "w_down": gaussian(key_of[13], (FF, D), FF ** -0.5, 0.09375, ((0, 2),)),
        "cotangent": gaussian(key_of[14], (TOKENS, D), 1.0, 6.0, ((0, 32),)),
    }


EPSILON = 1e-05
MASKED = -1e+30
ROPE_BASE = 10000.0
HIGHEST = lax.Precision.HIGHEST

@jax.custom_vjp
def low(v):
    return lax.optimization_barrier(v.astype(jnp.bfloat16)).astype(jnp.float32)

@jax.custom_vjp
def low_back(v):
    return v

def low_keep(v):
    return (low(v), None)

def low_pass(kept, grad):
    return (grad,)

def back_keep(v):
    return (v, None)

def back_low(kept, grad):
    return (low(grad),)
low.defvjp(low_keep, low_pass)
low_back.defvjp(back_keep, back_low)

def layer_norm(values, norm_gain, norm_shift):
    average = lax.optimization_barrier(jnp.mean(values, axis=-1, keepdims=True))
    centred = values - average
    variance = lax.optimization_barrier(jnp.mean(centred * centred, axis=-1, keepdims=True))
    return centred * lax.rsqrt(variance + EPSILON) * norm_gain + norm_shift

def rotary_tables(span_table):
    row_count = BLOCKS * BLOCK
    row_ids = jnp.arange(row_count)
    block_ids = row_ids // BLOCK
    span_rows = jnp.repeat(span_table, BLOCK)
    position = (row_ids % BLOCK + BLOCK * (block_ids % 2) * (span_rows == 2)).astype(jnp.float32)
    columns = jnp.arange(D) % HD
    half_dim = HD // 2
    freq_index = (columns % half_dim).astype(jnp.float32)
    frequency = ROPE_BASE ** (-2.0 * freq_index / HD)
    angles = position[:, None] * frequency[None, :]
    signs = jnp.where(columns < half_dim, -1.0, 1.0).astype(jnp.float32)
    return (jnp.cos(angles), jnp.sin(angles) * signs)

def swap_halves(values):
    row_count = values.shape[0]
    width = values.shape[1]
    parts = values.reshape(row_count, width // HD, 2, HD // 2)
    return jnp.flip(parts, axis=2).reshape(row_count, width)

def rotate(values, cosine, sine_signed):
    return values * cosine + swap_halves(values) * sine_signed

def key_masks(span_table, valid_table):
    block_ids = jnp.arange(BLOCKS)
    pair_first = block_ids // 2 * 2
    offsets = jnp.arange(2 * BLOCK)
    key_block = pair_first[:, None] + offsets[None, :] // BLOCK
    within = offsets[None, :] % BLOCK
    length_bound = valid_table[key_block]
    own_block = key_block == block_ids[:, None]
    return (within < length_bound) & ((span_table[:, None] == 2) | own_block)

def attend(query_rows, key_rows, value_rows, mask_table):
    query_blocks = query_rows.reshape(BLOCKS, BLOCK, H, HD)
    key_pairs = jnp.repeat(key_rows.reshape(BLOCKS // 2, 2 * BLOCK, H, HD), 2, axis=0)
    value_pairs = jnp.repeat(value_rows.reshape(BLOCKS // 2, 2 * BLOCK, H, HD), 2, axis=0)

    def one_block(inputs):
        query_block, key_pair, value_pair, key_mask = inputs
        scores = low_back(jnp.einsum('qhd,khd->hqk', query_block, key_pair, precision=HIGHEST))
        scores = jnp.where(key_mask[None, None, :], scores, MASKED)
        attention_probs = low(jax.nn.softmax(scores, axis=-1))
        return jnp.einsum('hqk,khd->qhd', attention_probs, value_pair, precision=HIGHEST)
    mixed_blocks = lax.map(jax.checkpoint(one_block), (query_blocks, key_pairs, value_pairs, mask_table))
    return mixed_blocks.reshape(BLOCKS * BLOCK, D)

def layer_forward(token_values, norm1_gain, norm1_shift, w_query, w_key, w_value, w_out, norm2_gain, norm2_shift, w_gate, w_up, w_down, cosine, sine_signed, mask_table):
    normed_one = low(layer_norm(token_values, norm1_gain, norm1_shift))
    query_raw = low_back(jnp.dot(normed_one, w_query, precision=HIGHEST))
    key_raw = low_back(jnp.dot(normed_one, w_key, precision=HIGHEST))
    value_rows = low_back(low(jnp.dot(normed_one, w_value, precision=HIGHEST)))
    query_rows = low(rotate(query_raw, cosine, sine_signed) * HD ** (-0.5))
    key_rows = low(rotate(key_raw, cosine, sine_signed))
    mixed_rows = low_back(low(attend(query_rows, key_rows, value_rows, mask_table)))
    resid_values = token_values + low_back(jnp.dot(mixed_rows, w_out, precision=HIGHEST))
    normed_two = low(layer_norm(resid_values, norm2_gain, norm2_shift))
    gate_values = low_back(jnp.dot(normed_two, w_gate, precision=HIGHEST))
    up_values = low_back(jnp.dot(normed_two, w_up, precision=HIGHEST))
    hidden_rows = low(jax.nn.silu(gate_values) * up_values)
    return resid_values + low_back(jnp.dot(hidden_rows, w_down, precision=HIGHEST))

def add_terms(first_term, second_term):
    return first_term + second_term

def reference(tokens, window_span, valid_len, norm1_gain, norm1_shift, w_query, w_key, w_value, w_out, norm2_gain, norm2_shift, w_gate, w_up, w_down, cotangent):
    group_rows = BLOCKS * BLOCK
    params = (norm1_gain.astype(jnp.float32), norm1_shift.astype(jnp.float32), w_query.astype(jnp.float32), w_key.astype(jnp.float32), w_value.astype(jnp.float32), w_out.astype(jnp.float32), norm2_gain.astype(jnp.float32), norm2_shift.astype(jnp.float32), w_gate.astype(jnp.float32), w_up.astype(jnp.float32), w_down.astype(jnp.float32))
    token_groups = tokens.astype(jnp.float32).reshape(N_WIDE, group_rows, D)
    cot_groups = cotangent.astype(jnp.float32).reshape(N_WIDE, group_rows, D)
    span_groups = window_span.reshape(N_WIDE, BLOCKS)
    valid_groups = valid_len.reshape(N_WIDE, BLOCKS)

    def group_step(running, inputs):
        token_rows, cot_rows, span_table, valid_table = inputs
        cosine, sine_signed = rotary_tables(span_table)
        mask_table = key_masks(span_table, valid_table)

        def forward(token_values, *weights):
            return layer_forward(token_values, *weights, cosine, sine_signed, mask_table)
        out_rows, pullback = jax.vjp(forward, token_rows, *params)
        gradients = pullback(cot_rows)
        running = jax.tree.map(add_terms, running, tuple(gradients[1:]))
        return (running, (out_rows, gradients[0]))
    zero_sums = jax.tree.map(jnp.zeros_like, params)
    running, outputs = lax.scan(group_step, zero_sums, (token_groups, cot_groups, span_groups, valid_groups))
    out_groups, grad_groups = outputs
    return (out_groups.reshape(TOKENS, D), grad_groups.reshape(TOKENS, D), running[0], running[1], running[2], running[3], running[4], running[5], running[6], running[7], running[8], running[9], running[10])
```

```python
import jax
import jax.numpy as jnp
from jax import lax
from jax.sharding import PartitionSpec as P

HD = 64


EPSILON = 1e-05
MASKED = -1e30
ROPE_BASE = 10000.0


def times_transpose(left, right):
    return lax.dot_general(
        left, right, (((1,), (1,)), ((), ())), preferred_element_type=jnp.float32
    )


def transpose_times(left, right):
    return lax.dot_general(
        left, right, (((0,), (0,)), ((), ())), preferred_element_type=jnp.float32
    )


def norm_forward(values, norm_gain, norm_shift):
    average = jnp.mean(values, axis=-1, keepdims=True)
    centred = values - average
    inverse = lax.rsqrt(jnp.mean(centred * centred, axis=-1, keepdims=True) + EPSILON)
    scaled = centred * inverse
    return (scaled * norm_gain + norm_shift, scaled, inverse)


def norm_backward(grad_out, scaled, inverse, norm_gain):
    grad_scaled = grad_out * norm_gain
    first_term = jnp.mean(grad_scaled, axis=-1, keepdims=True)
    second_term = jnp.mean(grad_scaled * scaled, axis=-1, keepdims=True)
    grad_in = inverse * (grad_scaled - first_term - scaled * second_term)
    return (grad_in, jnp.sum(grad_out * scaled, axis=0), jnp.sum(grad_out, axis=0))


def rotary_tables(span_table, block_rows, width):
    row_count = span_table.shape[0] * block_rows
    row_ids = jnp.arange(row_count)
    block_ids = row_ids // block_rows
    span_rows = jnp.repeat(span_table, block_rows)
    position = (row_ids % block_rows + block_rows * (block_ids % 2) * (span_rows == 2)).astype(
        jnp.float32
    )
    columns = jnp.arange(width) % HD
    half_dim = HD // 2
    freq_index = (columns % half_dim).astype(jnp.float32)
    frequency = ROPE_BASE ** (-2.0 * freq_index / HD)
    angles = position[:, None] * frequency[None, :]
    signs = jnp.where(columns < half_dim, -1.0, 1.0).astype(jnp.float32)
    return (jnp.cos(angles), jnp.sin(angles) * signs)


def swap_halves(values):
    row_count = values.shape[0]
    width = values.shape[1]
    parts = values.reshape(row_count, width // HD, 2, HD // 2)
    return jnp.flip(parts, axis=2).reshape(row_count, width)


def rotate(values, cosine, sine_signed):
    return values * cosine + swap_halves(values) * sine_signed


def rotate_back(grads_in, cosine, sine_signed):
    return grads_in * cosine + swap_halves(grads_in * sine_signed)


def pair_mask(block_index, span_table, valid_table, block_rows):
    pair_first = block_index // 2 * 2
    offsets = jnp.arange(2 * block_rows)
    key_block = pair_first + offsets // block_rows
    within = offsets % block_rows
    first_len = lax.dynamic_index_in_dim(valid_table, pair_first, keepdims=False)
    second_len = lax.dynamic_index_in_dim(valid_table, pair_first + 1, keepdims=False)
    own_span = lax.dynamic_index_in_dim(span_table, block_index, keepdims=False)
    length_bound = jnp.where(offsets < block_rows, first_len, second_len)
    return (within < length_bound) & ((own_span == 2) | (key_block == block_index))


def on_device_any_mesh(
    tokens,
    window_span,
    valid_len,
    norm1_gain,
    norm1_shift,
    w_query,
    w_key,
    w_value,
    w_out,
    norm2_gain,
    norm2_shift,
    w_gate,
    w_up,
    w_down,
    cotangent,
):
    local_rows = tokens.shape[0]
    group_rows = local_rows * lax.axis_size("narrow")
    block_count = window_span.shape[0]
    block_rows = group_rows // block_count
    local_width = w_query.shape[1]
    local_heads = local_width // HD
    local_hidden = w_gate.shape[1]
    softmax_scale = HD ** (-0.5)
    token_values = tokens.astype(jnp.float32)
    normed_one, scaled_one, inverse_one = norm_forward(token_values, norm1_gain, norm1_shift)
    normed_one = normed_one.astype(jnp.bfloat16)
    gathered_one = lax.all_gather(normed_one, "narrow", axis=0, tiled=True)
    joined_qkv = jnp.concatenate([w_query, w_key, w_value], axis=1)
    projected = jnp.dot(gathered_one, joined_qkv, preferred_element_type=jnp.float32)
    cosine, sine_signed = rotary_tables(window_span, block_rows, local_width)
    query_rows = (rotate(projected[:, :local_width], cosine, sine_signed) * softmax_scale).astype(
        jnp.bfloat16
    )
    key_rows = rotate(projected[:, local_width : 2 * local_width], cosine, sine_signed).astype(
        jnp.bfloat16
    )
    value_rows = projected[:, 2 * local_width :].astype(jnp.bfloat16)

    def block_slices(block_index):
        query_block = lax.dynamic_slice_in_dim(query_rows, block_index * block_rows, block_rows, 0)
        pair_start = block_index // 2 * 2 * block_rows
        return (
            query_block.reshape(block_rows, local_heads, HD),
            key_rows.reshape(2 * block_rows, local_heads, HD),
            value_rows.reshape(2 * block_rows, local_heads, HD),
            pair_start,
        )

    def masked_scores(block_index, query_block, key_pair):
        scores = jnp.einsum(
            "qhd,khd->hqk", query_block, key_pair, preferred_element_type=jnp.float32
        )
        key_mask = pair_mask(block_index, window_span, valid_len, block_rows)
        return jnp.where(key_mask[None, None, :], scores, MASKED)

    def attend_forward(block_index):
        query_block, key_pair, value_pair, pair_start = block_slices(block_index)
        scores = masked_scores(block_index, query_block, key_pair)
        highest = jnp.max(scores, axis=-1, keepdims=True)
        weights = jnp.exp(scores - highest)
        weight_total = jnp.sum(weights, axis=-1, keepdims=True)
        attention_probs = (weights / weight_total).astype(jnp.bfloat16)
        mixed_block = jnp.einsum(
            "hqk,khd->qhd", attention_probs, value_pair, preferred_element_type=jnp.float32
        )
        return (
            mixed_block.reshape(block_rows, local_width).astype(jnp.bfloat16),
            (highest + jnp.log(weight_total))[:, :, 0],
        )

    mixed_blocks, log_totals = lax.map(attend_forward, jnp.arange(block_count))
    mixed_rows = mixed_blocks.reshape(group_rows, local_width)
    resid_values = token_values + lax.psum_scatter(
        jnp.dot(mixed_rows, w_out, preferred_element_type=jnp.float32),
        "narrow",
        scatter_dimension=0,
        tiled=True,
    )
    normed_two, scaled_two, inverse_two = norm_forward(resid_values, norm2_gain, norm2_shift)
    normed_two = normed_two.astype(jnp.bfloat16)
    gathered_two = lax.all_gather(normed_two, "narrow", axis=0, tiled=True)
    joined_gate_up = jnp.concatenate([w_gate, w_up], axis=1)
    gate_up = jnp.dot(gathered_two, joined_gate_up, preferred_element_type=jnp.float32)
    gate_values = gate_up[:, :local_hidden]
    up_values = gate_up[:, local_hidden:]
    sigmoid_gate = jax.nn.sigmoid(gate_values)
    hidden_rows = (gate_values * sigmoid_gate * up_values).astype(jnp.bfloat16)
    out_values = resid_values + lax.psum_scatter(
        jnp.dot(hidden_rows, w_down, preferred_element_type=jnp.float32).astype(jnp.bfloat16),
        "narrow",
        scatter_dimension=0,
        tiled=True,
    ).astype(jnp.float32)
    shard_rows = lax.all_gather(cotangent, "narrow", axis=0, tiled=True)
    grad_hidden = times_transpose(shard_rows, w_down)
    grad_down_w, grad_hidden = (transpose_times(hidden_rows, shard_rows), grad_hidden)
    silu_grad = sigmoid_gate * (1.0 + gate_values * (1.0 - sigmoid_gate))
    grad_gate_up = jnp.concatenate(
        [grad_hidden * up_values * silu_grad, grad_hidden * gate_values * sigmoid_gate], axis=1
    ).astype(jnp.bfloat16)
    grad_normed_two = lax.psum_scatter(
        times_transpose(grad_gate_up, joined_gate_up), "narrow", scatter_dimension=0, tiled=True
    )
    grad_gate_up_w = transpose_times(gathered_two, grad_gate_up)
    grad_in_two, gain_two_grad, shift_two_grad = norm_backward(
        grad_normed_two, scaled_two, inverse_two, norm2_gain
    )
    grad_resid = cotangent.astype(jnp.float32) + grad_in_two
    shard_rows = lax.all_gather(grad_resid.astype(jnp.bfloat16), "narrow", axis=0, tiled=True)
    grad_mixed_sum = times_transpose(shard_rows, w_out)
    grad_out_w, grad_mixed_sum = (transpose_times(mixed_rows, shard_rows), grad_mixed_sum)
    grad_mixed = grad_mixed_sum.astype(jnp.bfloat16)

    def attend_backward(block_index, running):
        grad_query, grad_key, grad_value = running
        query_block, key_pair, value_pair, pair_start = block_slices(block_index)
        grad_rows = lax.dynamic_slice_in_dim(
            grad_mixed, block_index * block_rows, block_rows, 0
        ).reshape(block_rows, local_heads, HD)
        scores = masked_scores(block_index, query_block, key_pair)
        log_total = lax.dynamic_index_in_dim(log_totals, block_index, keepdims=False)
        attention_probs = jnp.exp(scores - log_total[:, :, None])
        grad_probs = jnp.einsum(
            "qhd,khd->hqk", grad_rows, value_pair, preferred_element_type=jnp.float32
        )
        centre = jnp.sum(attention_probs * grad_probs, axis=-1, keepdims=True)
        grad_scores = (attention_probs * (grad_probs - centre)).astype(jnp.bfloat16)
        block_query = jnp.einsum(
            "hqk,khd->qhd", grad_scores, key_pair, preferred_element_type=jnp.float32
        ).reshape(block_rows, local_width)
        pair_key = jnp.einsum(
            "hqk,qhd->khd", grad_scores, query_block, preferred_element_type=jnp.float32
        ).reshape(2 * block_rows, local_width)
        pair_value = jnp.einsum(
            "hqk,qhd->khd",
            attention_probs.astype(jnp.bfloat16),
            grad_rows,
            preferred_element_type=jnp.float32,
        ).reshape(2 * block_rows, local_width)
        grad_query = lax.dynamic_update_slice_in_dim(
            grad_query, block_query, block_index * block_rows, 0
        )
        grad_key = grad_key + pair_key
        grad_value = grad_value + pair_value
        return (grad_query, grad_key, grad_value)

    zero_rows = jnp.zeros((group_rows, local_width), jnp.float32)
    grad_query, grad_key, grad_value = lax.fori_loop(
        0, block_count, attend_backward, (zero_rows, zero_rows, zero_rows)
    )
    grad_query_raw = rotate_back(grad_query * softmax_scale, cosine, sine_signed)
    grad_key_raw = rotate_back(grad_key, cosine, sine_signed)
    grad_qkv = jnp.concatenate([grad_query_raw, grad_key_raw, grad_value], axis=1).astype(
        jnp.bfloat16
    )
    grad_normed_one = lax.psum_scatter(
        times_transpose(grad_qkv, joined_qkv).astype(jnp.bfloat16),
        "narrow",
        scatter_dimension=0,
        tiled=True,
    ).astype(jnp.float32)
    grad_qkv_w = transpose_times(gathered_one, grad_qkv)
    grad_in_one, gain_one_grad, shift_one_grad = norm_backward(
        grad_normed_one, scaled_one, inverse_one, norm1_gain
    )
    token_grad = grad_resid + grad_in_one
    qkv_summed, out_summed, gate_up_summed, down_summed = (
        lax.psum(grad_qkv_w.astype(jnp.bfloat16), "wide").astype(jnp.float32),
        lax.psum(grad_out_w.astype(jnp.bfloat16), "wide").astype(jnp.float32),
        lax.psum(grad_gate_up_w.astype(jnp.bfloat16), "wide").astype(jnp.float32),
        lax.psum(grad_down_w.astype(jnp.bfloat16), "wide").astype(jnp.float32),
    )
    norm_summed = lax.psum(
        (gain_one_grad, shift_one_grad, gain_two_grad, shift_two_grad), ("wide", "narrow")
    )
    return (
        out_values,
        token_grad,
        norm_summed[0],
        norm_summed[1],
        qkv_summed[:, :local_width],
        qkv_summed[:, local_width : 2 * local_width],
        qkv_summed[:, 2 * local_width :],
        out_summed,
        norm_summed[2],
        norm_summed[3],
        gate_up_summed[:, :local_hidden],
        gate_up_summed[:, local_hidden:],
        down_summed,
    )


PLANES = 4


def wide_index(x, y, z):
    return z * 4 + y * 2 + x


def chip_positions():
    return [(x, y, z) for z in range(PLANES) for y in range(2) for x in range(2)]


def flip_pairs(axis):
    if axis == "x":
        return [(wide_index(x, y, z), wide_index(1 - x, y, z)) for x, y, z in chip_positions()]
    return [(wide_index(x, y, z), wide_index(x, 1 - y, z)) for x, y, z in chip_positions()]


def middle_flip_pairs(axis):
    return [
        pair for pair, (_, _, z) in zip(flip_pairs(axis), chip_positions()) if z in (1, 2)
    ]


def plane_pairs(moves):
    return [
        (wide_index(x, y, src), wide_index(x, y, dst))
        for src, dst in moves
        for y in range(2)
        for x in range(2)
    ]


INWARD = ((0, 1), (3, 2))
ACROSS = ((1, 2), (2, 1))
OUTWARD = ((1, 0), (2, 3))


def send(values, pairs):
    return lax.ppermute(values, "wide", pairs)


def partner(values):
    return lax.ppermute(values, "narrow", [(0, 1), (1, 0)])


def add_low(left, right):
    return (left.astype(jnp.float32) + right.astype(jnp.float32)).astype(jnp.bfloat16)


def ordered(own, other, own_first):
    first = jnp.where(own_first, own, other)
    second = jnp.where(own_first, other, own)
    return jnp.concatenate([first, second], axis=0)


def summed_over_wide(product, rows, outer):
    position = lax.axis_index("wide")
    inner = "y" if outer == "x" else "x"
    outer_bit = position % 2 if outer == "x" else position // 2 % 2
    plane = position // 4
    half = rows // 2
    away = product((1 - outer_bit) * half, half).astype(jnp.bfloat16)
    received = send(away, flip_pairs(outer))
    pair_sum = (product(outer_bit * half, half) + received.astype(jnp.float32)).astype(jnp.bfloat16)
    column_sum = add_low(pair_sum, send(pair_sum, plane_pairs(INWARD)))
    quarter = half // 2
    upper = plane >= 2
    first, second = column_sum[:quarter], column_sum[quarter:]
    kept = jnp.where(upper, second, first)
    given = jnp.where(upper, first, second)
    line_sum = add_low(kept, send(given, plane_pairs(ACROSS)))
    total = add_low(line_sum, send(line_sum, middle_flip_pairs(inner)))
    full = ordered(total, send(total, plane_pairs(ACROSS)), jnp.logical_not(upper))
    outward = send(full, plane_pairs(OUTWARD))
    is_middle = (plane == 1) | (plane == 2)
    full = jnp.where(is_middle, full, outward)
    return ordered(full, send(full, flip_pairs(outer)), outer_bit == 0)


def gradient_sum(left, right):
    rows = left.shape[1]

    def half_sum(base, outer):
        def product(start, size):
            columns = lax.dynamic_slice_in_dim(left, base + start, size, 1)
            return transpose_times(columns, right)

        return summed_over_wide(product, rows // 2, outer)

    return jnp.concatenate([half_sum(0, "x"), half_sum(rows // 2, "y")], axis=0).astype(
        jnp.float32
    )


def vector_sum(values):
    values = values + partner(values)
    values = values + send(values, flip_pairs("x"))
    values = values + send(values, flip_pairs("y"))
    values = values + send(values, plane_pairs(INWARD))
    values = values + send(values, plane_pairs(ACROSS))
    plane = lax.axis_index("wide") // 4
    outward = send(values, plane_pairs(OUTWARD))
    return jnp.where((plane == 1) | (plane == 2), values, outward)


def rows_of(own, other):
    return jnp.concatenate([own, other], axis=0)


def rotary_own_first(position, width):
    columns = jnp.arange(width) % HD
    half_dim = HD // 2
    freq_index = (columns % half_dim).astype(jnp.float32)
    frequency = ROPE_BASE ** (-2.0 * freq_index / HD)
    angles = position[:, None] * frequency[None, :]
    signs = jnp.where(columns < half_dim, -1.0, 1.0).astype(jnp.float32)
    return (jnp.cos(angles), jnp.sin(angles) * signs)


def on_device(
    tokens,
    window_span,
    valid_len,
    norm1_gain,
    norm1_shift,
    w_query,
    w_key,
    w_value,
    w_out,
    norm2_gain,
    norm2_shift,
    w_gate,
    w_up,
    w_down,
    cotangent,
):
    block_rows = tokens.shape[0]
    local_width = w_query.shape[1]
    local_heads = local_width // HD
    local_hidden = w_gate.shape[1]
    softmax_scale = HD ** (-0.5)
    own_block = lax.axis_index("narrow")
    joined = window_span[0] == 2
    block_ids = jnp.stack([own_block, 1 - own_block])
    lengths = valid_len[block_ids]
    position = (
        jnp.arange(block_rows)[None, :]
        + block_rows * (block_ids[:, None] * joined.astype(jnp.int32))
    ).reshape(-1).astype(jnp.float32)

    token_values = tokens.astype(jnp.float32)
    normed_one, scaled_one, inverse_one = norm_forward(token_values, norm1_gain, norm1_shift)
    normed_one = normed_one.astype(jnp.bfloat16)
    gathered_one = rows_of(normed_one, partner(normed_one))
    cot_rows = rows_of(cotangent, partner(cotangent))
    joined_qkv = jnp.concatenate([w_query, w_key, w_value], axis=1)
    projected = jnp.dot(gathered_one, joined_qkv, preferred_element_type=jnp.float32)
    cosine, sine_signed = rotary_own_first(position, local_width)
    query_rows = (rotate(projected[:, :local_width], cosine, sine_signed) * softmax_scale).astype(
        jnp.bfloat16
    )
    key_rows = rotate(projected[:, local_width : 2 * local_width], cosine, sine_signed).astype(
        jnp.bfloat16
    )
    value_rows = projected[:, 2 * local_width :].astype(jnp.bfloat16)
    query_heads = query_rows.reshape(2, block_rows, local_heads, HD)
    key_heads = key_rows.reshape(2 * block_rows, local_heads, HD)
    value_heads = value_rows.reshape(2 * block_rows, local_heads, HD)
    offsets = jnp.arange(2 * block_rows)
    within = offsets % block_rows < jnp.repeat(lengths, block_rows)

    def masked_scores(index):
        scores = jnp.einsum(
            "qhd,khd->hqk", query_heads[index], key_heads, preferred_element_type=jnp.float32
        )
        key_mask = within & (joined | (offsets // block_rows == index))
        return jnp.where(key_mask[None, None, :], scores, MASKED)

    def attend_forward(index):
        scores = masked_scores(index)
        highest = jnp.max(scores, axis=-1, keepdims=True)
        weights = jnp.exp(scores - highest)
        weight_total = jnp.sum(weights, axis=-1, keepdims=True)
        attention_probs = (weights / weight_total).astype(jnp.bfloat16)
        mixed_block = jnp.einsum(
            "hqk,khd->qhd", attention_probs, value_heads, preferred_element_type=jnp.float32
        )
        return (
            mixed_block.reshape(block_rows, local_width).astype(jnp.bfloat16),
            (highest + jnp.log(weight_total))[:, :, 0],
        )

    mixed_own, log_own = attend_forward(0)
    mixed_other, log_other = attend_forward(1)
    mixed_rows = rows_of(mixed_own, mixed_other)
    other_share = jnp.dot(mixed_other, w_out, preferred_element_type=jnp.float32)
    resid_values = (
        token_values
        + jnp.dot(mixed_own, w_out, preferred_element_type=jnp.float32)
        + partner(other_share)
    )
    normed_two, scaled_two, inverse_two = norm_forward(resid_values, norm2_gain, norm2_shift)
    normed_two = normed_two.astype(jnp.bfloat16)
    gathered_two = rows_of(normed_two, partner(normed_two))
    gate_values = jnp.dot(gathered_two, w_gate, preferred_element_type=jnp.float32)
    up_values = jnp.dot(gathered_two, w_up, preferred_element_type=jnp.float32)
    sigmoid_gate = jax.nn.sigmoid(gate_values)
    hidden_rows = (gate_values * sigmoid_gate * up_values).astype(jnp.bfloat16)
    down_summed = gradient_sum(hidden_rows, cot_rows)

    out_other = jnp.dot(
        hidden_rows[block_rows:], w_down, preferred_element_type=jnp.float32
    ).astype(jnp.bfloat16)
    out_values = (
        resid_values
        + jnp.dot(hidden_rows[:block_rows], w_down, preferred_element_type=jnp.float32)
        + partner(out_other).astype(jnp.float32)
    )
    grad_hidden = times_transpose(cot_rows, w_down)
    silu_grad = sigmoid_gate * (1.0 + gate_values * (1.0 - sigmoid_gate))
    grad_gate = (grad_hidden * up_values * silu_grad).astype(jnp.bfloat16)
    grad_up = (grad_hidden * gate_values * sigmoid_gate).astype(jnp.bfloat16)
    gate_summed = gradient_sum(gathered_two, grad_gate)
    up_summed = gradient_sum(gathered_two, grad_up)

    def grad_two_share(rows):
        return times_transpose(grad_gate[rows], w_gate) + times_transpose(grad_up[rows], w_up)

    grad_two_other = grad_two_share(slice(block_rows, None))
    grad_normed_two = grad_two_share(slice(0, block_rows)) + partner(grad_two_other)
    grad_in_two, gain_two_grad, shift_two_grad = norm_backward(
        grad_normed_two, scaled_two, inverse_two, norm2_gain
    )
    grad_resid = cotangent.astype(jnp.float32) + grad_in_two
    grad_attention = grad_resid.astype(jnp.bfloat16)
    grad_rows = rows_of(grad_attention, partner(grad_attention))
    grad_mixed = times_transpose(grad_rows, w_out).astype(jnp.bfloat16)
    out_summed = gradient_sum(mixed_rows, grad_rows)
    grad_mixed_heads = grad_mixed.reshape(2, block_rows, local_heads, HD)

    def attend_backward(index, log_total):
        grad_block = grad_mixed_heads[index]
        scores = masked_scores(index)
        attention_probs = jnp.exp(scores - log_total[:, :, None])
        grad_probs = jnp.einsum(
            "qhd,khd->hqk", grad_block, value_heads, preferred_element_type=jnp.float32
        )
        centre = jnp.sum(attention_probs * grad_probs, axis=-1, keepdims=True)
        grad_scores = (attention_probs * (grad_probs - centre)).astype(jnp.bfloat16)
        block_query = jnp.einsum(
            "hqk,khd->qhd", grad_scores, key_heads, preferred_element_type=jnp.float32
        ).reshape(block_rows, local_width)
        pair_key = jnp.einsum(
            "hqk,qhd->khd", grad_scores, query_heads[index], preferred_element_type=jnp.float32
        ).reshape(2 * block_rows, local_width)
        pair_value = jnp.einsum(
            "hqk,qhd->khd",
            attention_probs.astype(jnp.bfloat16),
            grad_block,
            preferred_element_type=jnp.float32,
        ).reshape(2 * block_rows, local_width)
        return block_query, pair_key, pair_value

    query_own, key_own, value_own = attend_backward(0, log_own)
    query_other, key_other, value_other = attend_backward(1, log_other)
    grad_query = rows_of(query_own, query_other)
    grad_query_raw = rotate_back(grad_query * softmax_scale, cosine, sine_signed)
    grad_key_raw = rotate_back(key_own + key_other, cosine, sine_signed)
    grad_qkv = jnp.concatenate(
        [grad_query_raw, grad_key_raw, value_own + value_other], axis=1
    ).astype(jnp.bfloat16)
    qkv_summed = gradient_sum(gathered_one, grad_qkv)
    grad_one_other = times_transpose(grad_qkv[block_rows:], joined_qkv).astype(jnp.bfloat16)
    grad_normed_one = times_transpose(grad_qkv[:block_rows], joined_qkv) + partner(
        grad_one_other
    ).astype(jnp.float32)
    grad_in_one, gain_one_grad, shift_one_grad = norm_backward(
        grad_normed_one, scaled_one, inverse_one, norm1_gain
    )
    token_grad = grad_resid + grad_in_one
    norm_summed = vector_sum(
        jnp.stack([gain_one_grad, shift_one_grad, gain_two_grad, shift_two_grad])
    )
    return (
        out_values,
        token_grad,
        norm_summed[0],
        norm_summed[1],
        qkv_summed[:, :local_width],
        qkv_summed[:, local_width : 2 * local_width],
        qkv_summed[:, 2 * local_width :],
        out_summed,
        norm_summed[2],
        norm_summed[3],
        gate_summed,
        up_summed,
        down_summed,
    )


def solution(mesh):
    fits = mesh.shape["wide"] == PLANES * 4 and mesh.shape["narrow"] == 2
    in_specs = (
        P(("wide", "narrow"), None),
        P("wide"),
        P("wide"),
        P(),
        P(),
        P(None, "narrow"),
        P(None, "narrow"),
        P(None, "narrow"),
        P("narrow", None),
        P(),
        P(),
        P(None, "narrow"),
        P(None, "narrow"),
        P("narrow", None),
        P(("wide", "narrow"), None),
    )
    out_specs = (
        P(("wide", "narrow"), None),
        P(("wide", "narrow"), None),
        P(),
        P(),
        P(None, "narrow"),
        P(None, "narrow"),
        P(None, "narrow"),
        P("narrow", None),
        P(),
        P(),
        P(None, "narrow"),
        P(None, "narrow"),
        P("narrow", None),
    )
    return jax.shard_map(
        on_device if fits else on_device_any_mesh, mesh=mesh, in_specs=in_specs, out_specs=out_specs, check_vma=False
    )
```

```python
import functools

import jax
import jax.numpy as jnp
from jax import lax
from jax.experimental import pallas as pl
from jax.experimental.pallas import tpu as pltpu
from jax.sharding import PartitionSpec as P

MESH = pl.DeviceIdType.MESH

HD = 64


EPSILON = 1e-05
MASKED = -1e30
ROPE_BASE = 10000.0


def times_transpose(left, right):
    return lax.dot_general(
        left, right, (((1,), (1,)), ((), ())), preferred_element_type=jnp.float32
    )


def transpose_times(left, right):
    return lax.dot_general(
        left, right, (((0,), (0,)), ((), ())), preferred_element_type=jnp.float32
    )


def norm_forward(values, norm_gain, norm_shift):
    average = jnp.mean(values, axis=-1, keepdims=True)
    centred = values - average
    inverse = lax.rsqrt(jnp.mean(centred * centred, axis=-1, keepdims=True) + EPSILON)
    scaled = centred * inverse
    return (scaled * norm_gain + norm_shift, scaled, inverse)


def norm_backward(grad_out, scaled, inverse, norm_gain):
    grad_scaled = grad_out * norm_gain
    first_term = jnp.mean(grad_scaled, axis=-1, keepdims=True)
    second_term = jnp.mean(grad_scaled * scaled, axis=-1, keepdims=True)
    grad_in = inverse * (grad_scaled - first_term - scaled * second_term)
    return (grad_in, jnp.sum(grad_out * scaled, axis=0), jnp.sum(grad_out, axis=0))


def rotary_tables(span_table, block_rows, width):
    row_count = span_table.shape[0] * block_rows
    row_ids = jnp.arange(row_count)
    block_ids = row_ids // block_rows
    span_rows = jnp.repeat(span_table, block_rows)
    position = (row_ids % block_rows + block_rows * (block_ids % 2) * (span_rows == 2)).astype(
        jnp.float32
    )
    columns = jnp.arange(width) % HD
    half_dim = HD // 2
    freq_index = (columns % half_dim).astype(jnp.float32)
    frequency = ROPE_BASE ** (-2.0 * freq_index / HD)
    angles = position[:, None] * frequency[None, :]
    signs = jnp.where(columns < half_dim, -1.0, 1.0).astype(jnp.float32)
    return (jnp.cos(angles), jnp.sin(angles) * signs)


def swap_halves(values):
    row_count = values.shape[0]
    width = values.shape[1]
    parts = values.reshape(row_count, width // HD, 2, HD // 2)
    return jnp.flip(parts, axis=2).reshape(row_count, width)


def rotate(values, cosine, sine_signed):
    return values * cosine + swap_halves(values) * sine_signed


def rotate_back(grads_in, cosine, sine_signed):
    return grads_in * cosine + swap_halves(grads_in * sine_signed)


def pair_mask(block_index, span_table, valid_table, block_rows):
    pair_first = block_index // 2 * 2
    offsets = jnp.arange(2 * block_rows)
    key_block = pair_first + offsets // block_rows
    within = offsets % block_rows
    first_len = lax.dynamic_index_in_dim(valid_table, pair_first, keepdims=False)
    second_len = lax.dynamic_index_in_dim(valid_table, pair_first + 1, keepdims=False)
    own_span = lax.dynamic_index_in_dim(span_table, block_index, keepdims=False)
    length_bound = jnp.where(offsets < block_rows, first_len, second_len)
    return (within < length_bound) & ((own_span == 2) | (key_block == block_index))


def on_device_any_mesh(
    tokens,
    window_span,
    valid_len,
    norm1_gain,
    norm1_shift,
    w_query,
    w_key,
    w_value,
    w_out,
    norm2_gain,
    norm2_shift,
    w_gate,
    w_up,
    w_down,
    cotangent,
):
    local_rows = tokens.shape[0]
    group_rows = local_rows * lax.axis_size("narrow")
    block_count = window_span.shape[0]
    block_rows = group_rows // block_count
    local_width = w_query.shape[1]
    local_heads = local_width // HD
    local_hidden = w_gate.shape[1]
    softmax_scale = HD ** (-0.5)
    token_values = tokens.astype(jnp.float32)
    normed_one, scaled_one, inverse_one = norm_forward(token_values, norm1_gain, norm1_shift)
    normed_one = normed_one.astype(jnp.bfloat16)
    gathered_one = lax.all_gather(normed_one, "narrow", axis=0, tiled=True)
    joined_qkv = jnp.concatenate([w_query, w_key, w_value], axis=1)
    projected = jnp.dot(gathered_one, joined_qkv, preferred_element_type=jnp.float32)
    cosine, sine_signed = rotary_tables(window_span, block_rows, local_width)
    query_rows = (rotate(projected[:, :local_width], cosine, sine_signed) * softmax_scale).astype(
        jnp.bfloat16
    )
    key_rows = rotate(projected[:, local_width : 2 * local_width], cosine, sine_signed).astype(
        jnp.bfloat16
    )
    value_rows = projected[:, 2 * local_width :].astype(jnp.bfloat16)

    def block_slices(block_index):
        query_block = lax.dynamic_slice_in_dim(query_rows, block_index * block_rows, block_rows, 0)
        pair_start = block_index // 2 * 2 * block_rows
        return (
            query_block.reshape(block_rows, local_heads, HD),
            key_rows.reshape(2 * block_rows, local_heads, HD),
            value_rows.reshape(2 * block_rows, local_heads, HD),
            pair_start,
        )

    def masked_scores(block_index, query_block, key_pair):
        scores = jnp.einsum(
            "qhd,khd->hqk", query_block, key_pair, preferred_element_type=jnp.float32
        )
        key_mask = pair_mask(block_index, window_span, valid_len, block_rows)
        return jnp.where(key_mask[None, None, :], scores, MASKED)

    def attend_forward(block_index):
        query_block, key_pair, value_pair, pair_start = block_slices(block_index)
        scores = masked_scores(block_index, query_block, key_pair)
        highest = jnp.max(scores, axis=-1, keepdims=True)
        weights = jnp.exp(scores - highest)
        weight_total = jnp.sum(weights, axis=-1, keepdims=True)
        attention_probs = (weights / weight_total).astype(jnp.bfloat16)
        mixed_block = jnp.einsum(
            "hqk,khd->qhd", attention_probs, value_pair, preferred_element_type=jnp.float32
        )
        return (
            mixed_block.reshape(block_rows, local_width).astype(jnp.bfloat16),
            (highest + jnp.log(weight_total))[:, :, 0],
        )

    mixed_blocks, log_totals = lax.map(attend_forward, jnp.arange(block_count))
    mixed_rows = mixed_blocks.reshape(group_rows, local_width)
    resid_values = token_values + lax.psum_scatter(
        jnp.dot(mixed_rows, w_out, preferred_element_type=jnp.float32),
        "narrow",
        scatter_dimension=0,
        tiled=True,
    )
    normed_two, scaled_two, inverse_two = norm_forward(resid_values, norm2_gain, norm2_shift)
    normed_two = normed_two.astype(jnp.bfloat16)
    gathered_two = lax.all_gather(normed_two, "narrow", axis=0, tiled=True)
    joined_gate_up = jnp.concatenate([w_gate, w_up], axis=1)
    gate_up = jnp.dot(gathered_two, joined_gate_up, preferred_element_type=jnp.float32)
    gate_values = gate_up[:, :local_hidden]
    up_values = gate_up[:, local_hidden:]
    sigmoid_gate = jax.nn.sigmoid(gate_values)
    hidden_rows = (gate_values * sigmoid_gate * up_values).astype(jnp.bfloat16)
    out_values = resid_values + lax.psum_scatter(
        jnp.dot(hidden_rows, w_down, preferred_element_type=jnp.float32).astype(jnp.bfloat16),
        "narrow",
        scatter_dimension=0,
        tiled=True,
    ).astype(jnp.float32)
    shard_rows = lax.all_gather(cotangent, "narrow", axis=0, tiled=True)
    grad_hidden = times_transpose(shard_rows, w_down)
    grad_down_w, grad_hidden = (transpose_times(hidden_rows, shard_rows), grad_hidden)
    silu_grad = sigmoid_gate * (1.0 + gate_values * (1.0 - sigmoid_gate))
    grad_gate_up = jnp.concatenate(
        [grad_hidden * up_values * silu_grad, grad_hidden * gate_values * sigmoid_gate], axis=1
    ).astype(jnp.bfloat16)
    grad_normed_two = lax.psum_scatter(
        times_transpose(grad_gate_up, joined_gate_up), "narrow", scatter_dimension=0, tiled=True
    )
    grad_gate_up_w = transpose_times(gathered_two, grad_gate_up)
    grad_in_two, gain_two_grad, shift_two_grad = norm_backward(
        grad_normed_two, scaled_two, inverse_two, norm2_gain
    )
    grad_resid = cotangent.astype(jnp.float32) + grad_in_two
    shard_rows = lax.all_gather(grad_resid.astype(jnp.bfloat16), "narrow", axis=0, tiled=True)
    grad_mixed_sum = times_transpose(shard_rows, w_out)
    grad_out_w, grad_mixed_sum = (transpose_times(mixed_rows, shard_rows), grad_mixed_sum)
    grad_mixed = grad_mixed_sum.astype(jnp.bfloat16)

    def attend_backward(block_index, running):
        grad_query, grad_key, grad_value = running
        query_block, key_pair, value_pair, pair_start = block_slices(block_index)
        grad_rows = lax.dynamic_slice_in_dim(
            grad_mixed, block_index * block_rows, block_rows, 0
        ).reshape(block_rows, local_heads, HD)
        scores = masked_scores(block_index, query_block, key_pair)
        log_total = lax.dynamic_index_in_dim(log_totals, block_index, keepdims=False)
        attention_probs = jnp.exp(scores - log_total[:, :, None])
        grad_probs = jnp.einsum(
            "qhd,khd->hqk", grad_rows, value_pair, preferred_element_type=jnp.float32
        )
        centre = jnp.sum(attention_probs * grad_probs, axis=-1, keepdims=True)
        grad_scores = (attention_probs * (grad_probs - centre)).astype(jnp.bfloat16)
        block_query = jnp.einsum(
            "hqk,khd->qhd", grad_scores, key_pair, preferred_element_type=jnp.float32
        ).reshape(block_rows, local_width)
        pair_key = jnp.einsum(
            "hqk,qhd->khd", grad_scores, query_block, preferred_element_type=jnp.float32
        ).reshape(2 * block_rows, local_width)
        pair_value = jnp.einsum(
            "hqk,qhd->khd",
            attention_probs.astype(jnp.bfloat16),
            grad_rows,
            preferred_element_type=jnp.float32,
        ).reshape(2 * block_rows, local_width)
        grad_query = lax.dynamic_update_slice_in_dim(
            grad_query, block_query, block_index * block_rows, 0
        )
        grad_key = grad_key + pair_key
        grad_value = grad_value + pair_value
        return (grad_query, grad_key, grad_value)

    zero_rows = jnp.zeros((group_rows, local_width), jnp.float32)
    grad_query, grad_key, grad_value = lax.fori_loop(
        0, block_count, attend_backward, (zero_rows, zero_rows, zero_rows)
    )
    grad_query_raw = rotate_back(grad_query * softmax_scale, cosine, sine_signed)
    grad_key_raw = rotate_back(grad_key, cosine, sine_signed)
    grad_qkv = jnp.concatenate([grad_query_raw, grad_key_raw, grad_value], axis=1).astype(
        jnp.bfloat16
    )
    grad_normed_one = lax.psum_scatter(
        times_transpose(grad_qkv, joined_qkv).astype(jnp.bfloat16),
        "narrow",
        scatter_dimension=0,
        tiled=True,
    ).astype(jnp.float32)
    grad_qkv_w = transpose_times(gathered_one, grad_qkv)
    grad_in_one, gain_one_grad, shift_one_grad = norm_backward(
        grad_normed_one, scaled_one, inverse_one, norm1_gain
    )
    token_grad = grad_resid + grad_in_one
    qkv_summed, out_summed, gate_up_summed, down_summed = (
        lax.psum(grad_qkv_w.astype(jnp.bfloat16), "wide").astype(jnp.float32),
        lax.psum(grad_out_w.astype(jnp.bfloat16), "wide").astype(jnp.float32),
        lax.psum(grad_gate_up_w.astype(jnp.bfloat16), "wide").astype(jnp.float32),
        lax.psum(grad_down_w.astype(jnp.bfloat16), "wide").astype(jnp.float32),
    )
    norm_summed = lax.psum(
        (gain_one_grad, shift_one_grad, gain_two_grad, shift_two_grad), ("wide", "narrow")
    )
    return (
        out_values,
        token_grad,
        norm_summed[0],
        norm_summed[1],
        qkv_summed[:, :local_width],
        qkv_summed[:, local_width : 2 * local_width],
        qkv_summed[:, 2 * local_width :],
        out_summed,
        norm_summed[2],
        norm_summed[3],
        gate_up_summed[:, :local_hidden],
        gate_up_summed[:, local_hidden:],
        down_summed,
    )


PLANES = 4


class Job:
    def __init__(self, rows, cols, chunk_rows):
        self.rows, self.cols, self.chunk_rows = rows, cols, chunk_rows
        self.count = rows // (2 * chunk_rows)


def scratch_for(job):
    half, quarter = job.chunk_rows // 2, job.chunk_rows // 4

    def slots(rows):
        return pltpu.VMEM((job.count, 2, rows, job.cols), jnp.bfloat16)

    return [
        pltpu.VMEM((job.rows, job.cols), jnp.bfloat16),
        slots(half),
        slots(half),
        slots(quarter),
        slots(quarter),
        slots(quarter),
        slots(half),
        pltpu.SemaphoreType.DMA((job.count, 2, 9)),
        pltpu.SemaphoreType.DMA((job.count, 2, 9)),
        pltpu.SemaphoreType.DMA((job.count,)),
        pltpu.SemaphoreType.DMA((job.count, 2, 3)),
    ]


OUTER, INWARD, ACROSS, CROSS, BACK, OUT_A, OUT_B, GATHER_A, GATHER_B = range(9)


class Links:
    def __init__(self):
        position = lax.axis_index("wide")
        self.x = lax.rem(position, 2)
        self.y = lax.rem(position // 2, 2)
        self.z = position // 4
        self.middle = jnp.logical_and(self.z >= 1, self.z <= 2)
        self.edge = jnp.logical_or(self.z == 0, self.z == PLANES - 1)
        self.upper = self.z // 2
        self.across = self.at(self.x, self.y, 3 - self.z)
        step = 1 - 2 * self.upper
        self.inward = self.at(self.x, self.y, lax.rem(self.z + step + PLANES, PLANES))
        self.outward = self.at(self.x, self.y, lax.rem(self.z - step + PLANES, PLANES))
        self.flips = [self.at(1 - self.x, self.y, self.z), self.at(self.x, 1 - self.y, self.z)]
        self.bits = [self.x, self.y]

    def at(self, x, y, z):
        return z * 4 + y * 2 + x

    def greet(self):
        barrier = pltpu.get_barrier_semaphore()

        def signal(target):
            pl.semaphore_signal(barrier, inc=1, device_id={"wide": target}, device_id_type=MESH)

        for target in self.flips:
            signal(target)

        @pl.when(self.edge)
        def _():
            signal(self.inward)
            pl.semaphore_wait(barrier, 3)

        @pl.when(self.middle)
        def _():
            signal(self.across)
            signal(self.outward)
            pl.semaphore_wait(barrier, 4)


def add_rows(held, start, other, rows):
    held[pl.ds(start, rows), :] = (
        held[pl.ds(start, rows), :].astype(jnp.float32) + other[...].astype(jnp.float32)
    ).astype(jnp.bfloat16)


class Chunk:
    STEPS = 8

    def __init__(self, links, job, refs, output, index, colour):
        self.links, self.colour, self.index, self.output = links, colour, index, output
        self.held = refs[0]
        self.pair_in, self.column_in, self.across_in, self.cross_in, self.back_in, self.gather_in = [
            ref.at[index, colour] for ref in refs[1:7]
        ]
        self.sent, self.got, self.loaded, self.stored = refs[7:11]
        self.half, self.quarter = job.chunk_rows // 2, job.chunk_rows // 4
        self.base = (2 * index + colour) * job.chunk_rows
        bit = links.bits[colour]
        self.keep = pl.multiple_of(self.base + bit * self.half, self.quarter)
        self.away = pl.multiple_of(self.base + (1 - bit) * self.half, self.quarter)
        self.near = pl.multiple_of(links.upper * self.quarter, self.quarter)
        self.far = pl.multiple_of((1 - links.upper) * self.quarter, self.quarter)
        self.kept = pl.multiple_of(self.keep + self.near, self.quarter)
        self.given = pl.multiple_of(self.keep + self.far, self.quarter)
        self.outer_peer = links.flips[colour]
        self.inner_peer = links.flips[1 - colour]

    def rows(self, start, size):
        return self.held.at[pl.ds(start, size), :]

    def part(self, ref, start):
        return ref.at[pl.ds(start, self.quarter), :]

    def copy(self, step, source, target, peer):
        return pltpu.make_async_remote_copy(
            src_ref=source,
            dst_ref=target,
            send_sem=self.sent.at[self.index, self.colour, step],
            recv_sem=self.got.at[self.index, self.colour, step],
            device_id={"wide": peer},
            device_id_type=MESH,
        )

    def outer(self):
        return self.copy(OUTER, self.rows(self.away, self.half), self.pair_in, self.outer_peer)

    def inward(self):
        return self.copy(INWARD, self.rows(self.keep, self.half), self.column_in, self.links.inward)

    def across(self):
        return self.copy(ACROSS, self.rows(self.given, self.quarter), self.across_in, self.links.across)

    def cross(self):
        return self.copy(CROSS, self.rows(self.kept, self.quarter), self.cross_in, self.inner_peer)

    def back(self):
        return self.copy(BACK, self.rows(self.kept, self.quarter), self.back_in, self.links.across)

    def out_a(self):
        target = self.part(self.column_in, self.near)
        return self.copy(OUT_A, self.rows(self.kept, self.quarter), target, self.links.outward)

    def out_b(self):
        return self.copy(OUT_B, self.back_in, self.part(self.column_in, self.far), self.links.outward)

    def gather_a(self, source):
        return self.copy(GATHER_A, source, self.part(self.gather_in, self.near), self.outer_peer)

    def gather_b(self, source):
        return self.copy(GATHER_B, source, self.part(self.gather_in, self.far), self.outer_peer)

    def store(self, place, source, start, size):
        target = self.output.at[pl.ds(start, size), :]
        return pltpu.make_async_copy(source, target, self.stored.at[self.index, self.colour, place])

    def totals(self, near, far):
        return self.store(0, near, self.kept, self.quarter), self.store(1, far, self.given, self.quarter)

    def partner_total(self):
        return self.store(2, self.gather_in, self.away, self.half)

    def step(self, number):
        links = self.links
        near_total = self.rows(self.kept, self.quarter)
        edge_near, edge_far = self.part(self.column_in, self.near), self.part(self.column_in, self.far)
        if number == 0:
            self.outer().start()
        if number == 1:
            self.outer().wait_recv()
            add_rows(self.held, self.keep, self.pair_in, self.half)

            @pl.when(links.edge)
            def _():
                self.inward().start()

        if number == 2:

            @pl.when(links.middle)
            def _():
                self.inward().wait_recv()
                add_rows(self.held, self.keep, self.column_in, self.half)
                self.across().start()

        if number == 3:

            @pl.when(links.middle)
            def _():
                self.across().wait_recv()
                add_rows(self.held, self.kept, self.across_in, self.quarter)
                self.cross().start()

        if number == 4:

            @pl.when(links.middle)
            def _():
                self.cross().wait()
                add_rows(self.held, self.kept, self.cross_in, self.quarter)
                self.back().start()
                self.out_a().start()
                self.gather_a(near_total).start()

        if number == 5:

            @pl.when(links.middle)
            def _():
                self.back().wait_recv()
                self.out_b().start()
                self.gather_b(self.back_in).start()
                for store in self.totals(near_total, self.back_in):
                    store.start()

            @pl.when(links.edge)
            def _():
                self.out_a().wait_recv()
                self.gather_a(edge_near).start()

        if number == 6:

            @pl.when(links.edge)
            def _():
                self.out_b().wait_recv()
                self.gather_b(edge_far).start()
                for store in self.totals(edge_near, edge_far):
                    store.start()

        if number == 7:
            self.gather_a(near_total).wait_recv()
            self.gather_b(self.back_in).wait_recv()
            self.partner_total().start()

    def close(self):
        near_total = self.rows(self.kept, self.quarter)
        self.outer().wait_send()
        self.gather_a(near_total).wait_send()
        self.gather_b(self.back_in).wait_send()

        @pl.when(self.links.middle)
        def _():
            self.across().wait_send()
            self.back().wait_send()
            self.out_a().wait_send()
            self.out_b().wait_send()

        @pl.when(self.links.edge)
        def _():
            self.inward().wait_send()

        for store in self.totals(near_total, self.back_in):
            store.wait()
        self.partner_total().wait()


def sum_kernel(jobs, *refs):
    count = len(jobs)
    inputs, outputs, scratch = refs[:count], refs[count : 2 * count], refs[2 * count :]
    per_job = len(scratch) // count
    links = Links()
    items = []
    for number, job in enumerate(jobs):
        own = scratch[number * per_job : (number + 1) * per_job]
        for index in range(job.count):
            pair = [Chunk(links, job, own, outputs[number], index, colour) for colour in range(2)]
            span = pl.ds(2 * index * job.chunk_rows, 2 * job.chunk_rows)
            load = pltpu.make_async_copy(inputs[number].at[span, :], own[0].at[span, :], own[9].at[index])
            load.start()
            items.append((pair, load))
    links.greet()
    for tick in range(len(items) + Chunk.STEPS - 1):
        for place, (pair, load) in enumerate(items):
            step = tick - place
            if 0 <= step < Chunk.STEPS:
                if step == 0:
                    load.wait()
                for chunk in pair:
                    chunk.step(step)
    for pair, _ in items:
        for chunk in pair:
            chunk.close()


def summed_over_wide(gradients, chunk_rows, collective_id):
    jobs = [Job(g.shape[0], g.shape[1], r) for g, r in zip(gradients, chunk_rows)]
    scratch = []
    for job in jobs:
        scratch += scratch_for(job)
    sent = sum(2 * g.size * 5 // 4 for g in gradients)
    return pl.pallas_call(
        functools.partial(sum_kernel, jobs),
        out_shape=[jax.ShapeDtypeStruct(g.shape, jnp.bfloat16) for g in gradients],
        in_specs=[pl.BlockSpec(memory_space=pl.ANY)] * len(jobs),
        out_specs=[pl.BlockSpec(memory_space=pl.ANY)] * len(jobs),
        scratch_shapes=scratch,
        compiler_params=pltpu.CompilerParams(
            collective_id=collective_id, has_side_effects=True, vmem_limit_bytes=60 * 1024 * 1024
        ),
        cost_estimate=pl.CostEstimate(flops=0, bytes_accessed=2 * sent, transcendentals=0),
    )(*gradients)


def wide_index(x, y, z):
    return z * 4 + y * 2 + x


def chip_positions():
    return [(x, y, z) for z in range(PLANES) for y in range(2) for x in range(2)]


def flip_pairs(axis):
    if axis == "x":
        return [(wide_index(x, y, z), wide_index(1 - x, y, z)) for x, y, z in chip_positions()]
    return [(wide_index(x, y, z), wide_index(x, 1 - y, z)) for x, y, z in chip_positions()]


def middle_flip_pairs(axis):
    return [
        pair for pair, (_, _, z) in zip(flip_pairs(axis), chip_positions()) if z in (1, 2)
    ]


def plane_pairs(moves):
    return [
        (wide_index(x, y, src), wide_index(x, y, dst))
        for src, dst in moves
        for y in range(2)
        for x in range(2)
    ]


INWARD_MOVES = ((0, 1), (3, 2))
ACROSS_MOVES = ((1, 2), (2, 1))
OUTWARD_MOVES = ((1, 0), (2, 3))


def send(values, pairs):
    return lax.ppermute(values, "wide", pairs)


def partner(values):
    return lax.ppermute(values, "narrow", [(0, 1), (1, 0)])


def vector_sum(values):
    values = values + partner(values)
    values = values + send(values, flip_pairs("x"))
    values = values + send(values, flip_pairs("y"))
    values = values + send(values, plane_pairs(INWARD_MOVES))
    values = values + send(values, plane_pairs(ACROSS_MOVES))
    plane = lax.axis_index("wide") // 4
    outward = send(values, plane_pairs(OUTWARD_MOVES))
    return jnp.where((plane == 1) | (plane == 2), values, outward)


def rows_of(own, other):
    return jnp.concatenate([own, other], axis=0)


def rotary_own_first(position, width):
    columns = jnp.arange(width) % HD
    half_dim = HD // 2
    freq_index = (columns % half_dim).astype(jnp.float32)
    frequency = ROPE_BASE ** (-2.0 * freq_index / HD)
    angles = position[:, None] * frequency[None, :]
    signs = jnp.where(columns < half_dim, -1.0, 1.0).astype(jnp.float32)
    return (jnp.cos(angles), jnp.sin(angles) * signs)


def on_device(
    tokens,
    window_span,
    valid_len,
    norm1_gain,
    norm1_shift,
    w_query,
    w_key,
    w_value,
    w_out,
    norm2_gain,
    norm2_shift,
    w_gate,
    w_up,
    w_down,
    cotangent,
):
    block_rows = tokens.shape[0]
    local_width = w_query.shape[1]
    local_heads = local_width // HD
    local_hidden = w_gate.shape[1]
    softmax_scale = HD ** (-0.5)
    own_block = lax.axis_index("narrow")
    joined = window_span[0] == 2
    block_ids = jnp.stack([own_block, 1 - own_block])
    lengths = valid_len[block_ids]
    position = (
        jnp.arange(block_rows)[None, :]
        + block_rows * (block_ids[:, None] * joined.astype(jnp.int32))
    ).reshape(-1).astype(jnp.float32)

    token_values = tokens.astype(jnp.float32)
    normed_one, scaled_one, inverse_one = norm_forward(token_values, norm1_gain, norm1_shift)
    normed_one = normed_one.astype(jnp.bfloat16)
    gathered_one = rows_of(normed_one, partner(normed_one))
    cot_rows = rows_of(cotangent, partner(cotangent))
    joined_qkv = jnp.concatenate([w_query, w_key, w_value], axis=1)
    projected = jnp.dot(gathered_one, joined_qkv, preferred_element_type=jnp.float32)
    cosine, sine_signed = rotary_own_first(position, local_width)
    query_rows = (rotate(projected[:, :local_width], cosine, sine_signed) * softmax_scale).astype(
        jnp.bfloat16
    )
    key_rows = rotate(projected[:, local_width : 2 * local_width], cosine, sine_signed).astype(
        jnp.bfloat16
    )
    value_rows = projected[:, 2 * local_width :].astype(jnp.bfloat16)
    query_heads = query_rows.reshape(2, block_rows, local_heads, HD)
    key_heads = key_rows.reshape(2 * block_rows, local_heads, HD)
    value_heads = value_rows.reshape(2 * block_rows, local_heads, HD)
    offsets = jnp.arange(2 * block_rows)
    within = offsets % block_rows < jnp.repeat(lengths, block_rows)

    def masked_scores(index):
        scores = jnp.einsum(
            "qhd,khd->hqk", query_heads[index], key_heads, preferred_element_type=jnp.float32
        )
        key_mask = within & (joined | (offsets // block_rows == index))
        return jnp.where(key_mask[None, None, :], scores, MASKED)

    def attend_forward(index):
        scores = masked_scores(index)
        highest = jnp.max(scores, axis=-1, keepdims=True)
        weights = jnp.exp(scores - highest)
        weight_total = jnp.sum(weights, axis=-1, keepdims=True)
        attention_probs = (weights / weight_total).astype(jnp.bfloat16)
        mixed_block = jnp.einsum(
            "hqk,khd->qhd", attention_probs, value_heads, preferred_element_type=jnp.float32
        )
        return (
            mixed_block.reshape(block_rows, local_width).astype(jnp.bfloat16),
            (highest + jnp.log(weight_total))[:, :, 0],
        )

    mixed_own, log_own = attend_forward(0)
    mixed_other, log_other = attend_forward(1)
    mixed_rows = rows_of(mixed_own, mixed_other)
    other_share = jnp.dot(mixed_other, w_out, preferred_element_type=jnp.float32)
    resid_values = (
        token_values
        + jnp.dot(mixed_own, w_out, preferred_element_type=jnp.float32)
        + partner(other_share)
    )
    normed_two, scaled_two, inverse_two = norm_forward(resid_values, norm2_gain, norm2_shift)
    normed_two = normed_two.astype(jnp.bfloat16)
    gathered_two = rows_of(normed_two, partner(normed_two))
    gate_values = jnp.dot(gathered_two, w_gate, preferred_element_type=jnp.float32)
    up_values = jnp.dot(gathered_two, w_up, preferred_element_type=jnp.float32)
    sigmoid_gate = jax.nn.sigmoid(gate_values)
    hidden_rows = (gate_values * sigmoid_gate * up_values).astype(jnp.bfloat16)
    down_summed = transpose_times(hidden_rows, cot_rows).astype(jnp.bfloat16)

    out_other = jnp.dot(
        hidden_rows[block_rows:], w_down, preferred_element_type=jnp.float32
    ).astype(jnp.bfloat16)
    out_values = (
        resid_values
        + jnp.dot(hidden_rows[:block_rows], w_down, preferred_element_type=jnp.float32)
        + partner(out_other).astype(jnp.float32)
    )
    grad_hidden = times_transpose(cot_rows, w_down)
    silu_grad = sigmoid_gate * (1.0 + gate_values * (1.0 - sigmoid_gate))
    grad_gate = (grad_hidden * up_values * silu_grad).astype(jnp.bfloat16)
    grad_up = (grad_hidden * gate_values * sigmoid_gate).astype(jnp.bfloat16)
    gate_summed = transpose_times(gathered_two, grad_gate).astype(jnp.bfloat16)
    up_summed = transpose_times(gathered_two, grad_up).astype(jnp.bfloat16)

    def grad_two_share(rows):
        return times_transpose(grad_gate[rows], w_gate) + times_transpose(grad_up[rows], w_up)

    grad_two_other = grad_two_share(slice(block_rows, None))
    grad_normed_two = grad_two_share(slice(0, block_rows)) + partner(grad_two_other)
    grad_in_two, gain_two_grad, shift_two_grad = norm_backward(
        grad_normed_two, scaled_two, inverse_two, norm2_gain
    )
    grad_resid = cotangent.astype(jnp.float32) + grad_in_two
    grad_attention = grad_resid.astype(jnp.bfloat16)
    grad_rows = rows_of(grad_attention, partner(grad_attention))
    grad_mixed = times_transpose(grad_rows, w_out).astype(jnp.bfloat16)
    out_summed = transpose_times(mixed_rows, grad_rows).astype(jnp.bfloat16)
    grad_mixed_heads = grad_mixed.reshape(2, block_rows, local_heads, HD)

    def attend_backward(index, log_total):
        grad_block = grad_mixed_heads[index]
        scores = masked_scores(index)
        attention_probs = jnp.exp(scores - log_total[:, :, None])
        grad_probs = jnp.einsum(
            "qhd,khd->hqk", grad_block, value_heads, preferred_element_type=jnp.float32
        )
        centre = jnp.sum(attention_probs * grad_probs, axis=-1, keepdims=True)
        grad_scores = (attention_probs * (grad_probs - centre)).astype(jnp.bfloat16)
        block_query = jnp.einsum(
            "hqk,khd->qhd", grad_scores, key_heads, preferred_element_type=jnp.float32
        ).reshape(block_rows, local_width)
        pair_key = jnp.einsum(
            "hqk,qhd->khd", grad_scores, query_heads[index], preferred_element_type=jnp.float32
        ).reshape(2 * block_rows, local_width)
        pair_value = jnp.einsum(
            "hqk,qhd->khd",
            attention_probs.astype(jnp.bfloat16),
            grad_block,
            preferred_element_type=jnp.float32,
        ).reshape(2 * block_rows, local_width)
        return block_query, pair_key, pair_value

    query_own, key_own, value_own = attend_backward(0, log_own)
    query_other, key_other, value_other = attend_backward(1, log_other)
    grad_query = rows_of(query_own, query_other)
    grad_query_raw = rotate_back(grad_query * softmax_scale, cosine, sine_signed)
    grad_key_raw = rotate_back(key_own + key_other, cosine, sine_signed)
    grad_qkv = jnp.concatenate(
        [grad_query_raw, grad_key_raw, value_own + value_other], axis=1
    ).astype(jnp.bfloat16)
    qkv_summed = transpose_times(gathered_one, grad_qkv).astype(jnp.bfloat16)
    grad_one_other = times_transpose(grad_qkv[block_rows:], joined_qkv).astype(jnp.bfloat16)
    grad_normed_one = times_transpose(grad_qkv[:block_rows], joined_qkv) + partner(
        grad_one_other
    ).astype(jnp.float32)
    grad_in_one, gain_one_grad, shift_one_grad = norm_backward(
        grad_normed_one, scaled_one, inverse_one, norm1_gain
    )
    token_grad = grad_resid + grad_in_one
    norm_summed = vector_sum(
        jnp.stack([gain_one_grad, shift_one_grad, gain_two_grad, shift_two_grad])
    )
    width = local_width
    down_summed, gate_summed, up_summed, out_summed, query_summed, key_summed, value_summed = [
        total.astype(jnp.float32)
        for total in summed_over_wide(
            [
                down_summed,
                gate_summed,
                up_summed,
                out_summed,
                qkv_summed[:, :width],
                qkv_summed[:, width : 2 * width],
                qkv_summed[:, 2 * width :],
            ],
            [128, 64, 64, 128, 128, 128, 128],
            1,
        )
    ]
    return (
        out_values,
        token_grad,
        norm_summed[0],
        norm_summed[1],
        query_summed,
        key_summed,
        value_summed,
        out_summed,
        norm_summed[2],
        norm_summed[3],
        gate_summed,
        up_summed,
        down_summed,
    )


def solution(mesh):
    fits = mesh.shape["wide"] == PLANES * 4 and mesh.shape["narrow"] == 2
    in_specs = (
        P(("wide", "narrow"), None),
        P("wide"),
        P("wide"),
        P(),
        P(),
        P(None, "narrow"),
        P(None, "narrow"),
        P(None, "narrow"),
        P("narrow", None),
        P(),
        P(),
        P(None, "narrow"),
        P(None, "narrow"),
        P("narrow", None),
        P(("wide", "narrow"), None),
    )
    out_specs = (
        P(("wide", "narrow"), None),
        P(("wide", "narrow"), None),
        P(),
        P(),
        P(None, "narrow"),
        P(None, "narrow"),
        P(None, "narrow"),
        P("narrow", None),
        P(),
        P(),
        P(None, "narrow"),
        P(None, "narrow"),
        P("narrow", None),
    )
    return jax.shard_map(
        on_device if fits else on_device_any_mesh, mesh=mesh, in_specs=in_specs, out_specs=out_specs, check_vma=False
    )
```

```python
import functools

import jax
import jax.numpy as jnp
from jax import lax
from jax.experimental import pallas as pl
from jax.experimental.pallas import tpu as pltpu
from jax.sharding import PartitionSpec as P

MESH = pl.DeviceIdType.MESH

HD = 64


EPSILON = 1e-05
MASKED = -1e30
ROPE_BASE = 10000.0


def times_transpose(left, right):
    return lax.dot_general(
        left, right, (((1,), (1,)), ((), ())), preferred_element_type=jnp.float32
    )


def transpose_times(left, right):
    return lax.dot_general(
        left, right, (((0,), (0,)), ((), ())), preferred_element_type=jnp.float32
    )


def norm_forward(values, norm_gain, norm_shift):
    average = jnp.mean(values, axis=-1, keepdims=True)
    centred = values - average
    inverse = lax.rsqrt(jnp.mean(centred * centred, axis=-1, keepdims=True) + EPSILON)
    scaled = centred * inverse
    return (scaled * norm_gain + norm_shift, scaled, inverse)


def norm_backward(grad_out, scaled, inverse, norm_gain):
    grad_scaled = grad_out * norm_gain
    first_term = jnp.mean(grad_scaled, axis=-1, keepdims=True)
    second_term = jnp.mean(grad_scaled * scaled, axis=-1, keepdims=True)
    grad_in = inverse * (grad_scaled - first_term - scaled * second_term)
    return (grad_in, jnp.sum(grad_out * scaled, axis=0), jnp.sum(grad_out, axis=0))


def rotary_tables(span_table, block_rows, width):
    row_count = span_table.shape[0] * block_rows
    row_ids = jnp.arange(row_count)
    block_ids = row_ids // block_rows
    span_rows = jnp.repeat(span_table, block_rows)
    position = (row_ids % block_rows + block_rows * (block_ids % 2) * (span_rows == 2)).astype(
        jnp.float32
    )
    columns = jnp.arange(width) % HD
    half_dim = HD // 2
    freq_index = (columns % half_dim).astype(jnp.float32)
    frequency = ROPE_BASE ** (-2.0 * freq_index / HD)
    angles = position[:, None] * frequency[None, :]
    signs = jnp.where(columns < half_dim, -1.0, 1.0).astype(jnp.float32)
    return (jnp.cos(angles), jnp.sin(angles) * signs)


def swap_halves(values):
    row_count = values.shape[0]
    width = values.shape[1]
    parts = values.reshape(row_count, width // HD, 2, HD // 2)
    return jnp.flip(parts, axis=2).reshape(row_count, width)


def rotate(values, cosine, sine_signed):
    return values * cosine + swap_halves(values) * sine_signed


def rotate_back(grads_in, cosine, sine_signed):
    return grads_in * cosine + swap_halves(grads_in * sine_signed)


def pair_mask(block_index, span_table, valid_table, block_rows):
    pair_first = block_index // 2 * 2
    offsets = jnp.arange(2 * block_rows)
    key_block = pair_first + offsets // block_rows
    within = offsets % block_rows
    first_len = lax.dynamic_index_in_dim(valid_table, pair_first, keepdims=False)
    second_len = lax.dynamic_index_in_dim(valid_table, pair_first + 1, keepdims=False)
    own_span = lax.dynamic_index_in_dim(span_table, block_index, keepdims=False)
    length_bound = jnp.where(offsets < block_rows, first_len, second_len)
    return (within < length_bound) & ((own_span == 2) | (key_block == block_index))


def on_device_any_mesh(
    tokens,
    window_span,
    valid_len,
    norm1_gain,
    norm1_shift,
    w_query,
    w_key,
    w_value,
    w_out,
    norm2_gain,
    norm2_shift,
    w_gate,
    w_up,
    w_down,
    cotangent,
):
    local_rows = tokens.shape[0]
    group_rows = local_rows * lax.axis_size("narrow")
    block_count = window_span.shape[0]
    block_rows = group_rows // block_count
    local_width = w_query.shape[1]
    local_heads = local_width // HD
    local_hidden = w_gate.shape[1]
    softmax_scale = HD ** (-0.5)
    token_values = tokens.astype(jnp.float32)
    normed_one, scaled_one, inverse_one = norm_forward(token_values, norm1_gain, norm1_shift)
    normed_one = normed_one.astype(jnp.bfloat16)
    gathered_one = lax.all_gather(normed_one, "narrow", axis=0, tiled=True)
    joined_qkv = jnp.concatenate([w_query, w_key, w_value], axis=1)
    projected = jnp.dot(gathered_one, joined_qkv, preferred_element_type=jnp.float32)
    cosine, sine_signed = rotary_tables(window_span, block_rows, local_width)
    query_rows = (rotate(projected[:, :local_width], cosine, sine_signed) * softmax_scale).astype(
        jnp.bfloat16
    )
    key_rows = rotate(projected[:, local_width : 2 * local_width], cosine, sine_signed).astype(
        jnp.bfloat16
    )
    value_rows = projected[:, 2 * local_width :].astype(jnp.bfloat16)

    def block_slices(block_index):
        query_block = lax.dynamic_slice_in_dim(query_rows, block_index * block_rows, block_rows, 0)
        pair_start = block_index // 2 * 2 * block_rows
        return (
            query_block.reshape(block_rows, local_heads, HD),
            key_rows.reshape(2 * block_rows, local_heads, HD),
            value_rows.reshape(2 * block_rows, local_heads, HD),
            pair_start,
        )

    def masked_scores(block_index, query_block, key_pair):
        scores = jnp.einsum(
            "qhd,khd->hqk", query_block, key_pair, preferred_element_type=jnp.float32
        )
        key_mask = pair_mask(block_index, window_span, valid_len, block_rows)
        return jnp.where(key_mask[None, None, :], scores, MASKED)

    def attend_forward(block_index):
        query_block, key_pair, value_pair, pair_start = block_slices(block_index)
        scores = masked_scores(block_index, query_block, key_pair)
        highest = jnp.max(scores, axis=-1, keepdims=True)
        weights = jnp.exp(scores - highest)
        weight_total = jnp.sum(weights, axis=-1, keepdims=True)
        attention_probs = (weights / weight_total).astype(jnp.bfloat16)
        mixed_block = jnp.einsum(
            "hqk,khd->qhd", attention_probs, value_pair, preferred_element_type=jnp.float32
        )
        return (
            mixed_block.reshape(block_rows, local_width).astype(jnp.bfloat16),
            (highest + jnp.log(weight_total))[:, :, 0],
        )

    mixed_blocks, log_totals = lax.map(attend_forward, jnp.arange(block_count))
    mixed_rows = mixed_blocks.reshape(group_rows, local_width)
    resid_values = token_values + lax.psum_scatter(
        jnp.dot(mixed_rows, w_out, preferred_element_type=jnp.float32),
        "narrow",
        scatter_dimension=0,
        tiled=True,
    )
    normed_two, scaled_two, inverse_two = norm_forward(resid_values, norm2_gain, norm2_shift)
    normed_two = normed_two.astype(jnp.bfloat16)
    gathered_two = lax.all_gather(normed_two, "narrow", axis=0, tiled=True)
    joined_gate_up = jnp.concatenate([w_gate, w_up], axis=1)
    gate_up = jnp.dot(gathered_two, joined_gate_up, preferred_element_type=jnp.float32)
    gate_values = gate_up[:, :local_hidden]
    up_values = gate_up[:, local_hidden:]
    sigmoid_gate = jax.nn.sigmoid(gate_values)
    hidden_rows = (gate_values * sigmoid_gate * up_values).astype(jnp.bfloat16)
    out_values = resid_values + lax.psum_scatter(
        jnp.dot(hidden_rows, w_down, preferred_element_type=jnp.float32).astype(jnp.bfloat16),
        "narrow",
        scatter_dimension=0,
        tiled=True,
    ).astype(jnp.float32)
    shard_rows = lax.all_gather(cotangent, "narrow", axis=0, tiled=True)
    grad_hidden = times_transpose(shard_rows, w_down)
    grad_down_w, grad_hidden = (transpose_times(hidden_rows, shard_rows), grad_hidden)
    silu_grad = sigmoid_gate * (1.0 + gate_values * (1.0 - sigmoid_gate))
    grad_gate_up = jnp.concatenate(
        [grad_hidden * up_values * silu_grad, grad_hidden * gate_values * sigmoid_gate], axis=1
    ).astype(jnp.bfloat16)
    grad_normed_two = lax.psum_scatter(
        times_transpose(grad_gate_up, joined_gate_up), "narrow", scatter_dimension=0, tiled=True
    )
    grad_gate_up_w = transpose_times(gathered_two, grad_gate_up)
    grad_in_two, gain_two_grad, shift_two_grad = norm_backward(
        grad_normed_two, scaled_two, inverse_two, norm2_gain
    )
    grad_resid = cotangent.astype(jnp.float32) + grad_in_two
    shard_rows = lax.all_gather(grad_resid.astype(jnp.bfloat16), "narrow", axis=0, tiled=True)
    grad_mixed_sum = times_transpose(shard_rows, w_out)
    grad_out_w, grad_mixed_sum = (transpose_times(mixed_rows, shard_rows), grad_mixed_sum)
    grad_mixed = grad_mixed_sum.astype(jnp.bfloat16)

    def attend_backward(block_index, running):
        grad_query, grad_key, grad_value = running
        query_block, key_pair, value_pair, pair_start = block_slices(block_index)
        grad_rows = lax.dynamic_slice_in_dim(
            grad_mixed, block_index * block_rows, block_rows, 0
        ).reshape(block_rows, local_heads, HD)
        scores = masked_scores(block_index, query_block, key_pair)
        log_total = lax.dynamic_index_in_dim(log_totals, block_index, keepdims=False)
        attention_probs = jnp.exp(scores - log_total[:, :, None])
        grad_probs = jnp.einsum(
            "qhd,khd->hqk", grad_rows, value_pair, preferred_element_type=jnp.float32
        )
        centre = jnp.sum(attention_probs * grad_probs, axis=-1, keepdims=True)
        grad_scores = (attention_probs * (grad_probs - centre)).astype(jnp.bfloat16)
        block_query = jnp.einsum(
            "hqk,khd->qhd", grad_scores, key_pair, preferred_element_type=jnp.float32
        ).reshape(block_rows, local_width)
        pair_key = jnp.einsum(
            "hqk,qhd->khd", grad_scores, query_block, preferred_element_type=jnp.float32
        ).reshape(2 * block_rows, local_width)
        pair_value = jnp.einsum(
            "hqk,qhd->khd",
            attention_probs.astype(jnp.bfloat16),
            grad_rows,
            preferred_element_type=jnp.float32,
        ).reshape(2 * block_rows, local_width)
        grad_query = lax.dynamic_update_slice_in_dim(
            grad_query, block_query, block_index * block_rows, 0
        )
        grad_key = grad_key + pair_key
        grad_value = grad_value + pair_value
        return (grad_query, grad_key, grad_value)

    zero_rows = jnp.zeros((group_rows, local_width), jnp.float32)
    grad_query, grad_key, grad_value = lax.fori_loop(
        0, block_count, attend_backward, (zero_rows, zero_rows, zero_rows)
    )
    grad_query_raw = rotate_back(grad_query * softmax_scale, cosine, sine_signed)
    grad_key_raw = rotate_back(grad_key, cosine, sine_signed)
    grad_qkv = jnp.concatenate([grad_query_raw, grad_key_raw, grad_value], axis=1).astype(
        jnp.bfloat16
    )
    grad_normed_one = lax.psum_scatter(
        times_transpose(grad_qkv, joined_qkv).astype(jnp.bfloat16),
        "narrow",
        scatter_dimension=0,
        tiled=True,
    ).astype(jnp.float32)
    grad_qkv_w = transpose_times(gathered_one, grad_qkv)
    grad_in_one, gain_one_grad, shift_one_grad = norm_backward(
        grad_normed_one, scaled_one, inverse_one, norm1_gain
    )
    token_grad = grad_resid + grad_in_one
    qkv_summed, out_summed, gate_up_summed, down_summed = (
        lax.psum(grad_qkv_w.astype(jnp.bfloat16), "wide").astype(jnp.float32),
        lax.psum(grad_out_w.astype(jnp.bfloat16), "wide").astype(jnp.float32),
        lax.psum(grad_gate_up_w.astype(jnp.bfloat16), "wide").astype(jnp.float32),
        lax.psum(grad_down_w.astype(jnp.bfloat16), "wide").astype(jnp.float32),
    )
    norm_summed = lax.psum(
        (gain_one_grad, shift_one_grad, gain_two_grad, shift_two_grad), ("wide", "narrow")
    )
    return (
        out_values,
        token_grad,
        norm_summed[0],
        norm_summed[1],
        qkv_summed[:, :local_width],
        qkv_summed[:, local_width : 2 * local_width],
        qkv_summed[:, 2 * local_width :],
        out_summed,
        norm_summed[2],
        norm_summed[3],
        gate_up_summed[:, :local_hidden],
        gate_up_summed[:, local_hidden:],
        down_summed,
    )


PLANES = 4


class Job:
    def __init__(self, rows, cols, chunk_rows):
        self.rows, self.cols, self.chunk_rows = rows, cols, chunk_rows
        self.count = rows // (2 * chunk_rows)


def scratch_for(job):
    half, quarter = job.chunk_rows // 2, job.chunk_rows // 4

    def slots(rows):
        return pltpu.VMEM((job.count, 2, rows, job.cols), jnp.bfloat16)

    return [
        pltpu.VMEM((job.rows, job.cols), jnp.bfloat16),
        slots(half),
        slots(half),
        slots(quarter),
        slots(quarter),
        slots(quarter),
        slots(half),
        pltpu.SemaphoreType.DMA((job.count, 2, 9)),
        pltpu.SemaphoreType.DMA((job.count, 2, 9)),
        pltpu.SemaphoreType.DMA((job.count,)),
        pltpu.SemaphoreType.DMA((job.count, 2, 3)),
    ]


OUTER, INWARD, ACROSS, CROSS, BACK, OUT_A, OUT_B, GATHER_A, GATHER_B = range(9)


class Links:
    def __init__(self):
        position = lax.axis_index("wide")
        self.x = lax.rem(position, 2)
        self.y = lax.rem(position // 2, 2)
        self.z = position // 4
        self.middle = jnp.logical_and(self.z >= 1, self.z <= 2)
        self.edge = jnp.logical_or(self.z == 0, self.z == PLANES - 1)
        self.upper = self.z // 2
        self.across = self.at(self.x, self.y, 3 - self.z)
        step = 1 - 2 * self.upper
        self.inward = self.at(self.x, self.y, lax.rem(self.z + step + PLANES, PLANES))
        self.outward = self.at(self.x, self.y, lax.rem(self.z - step + PLANES, PLANES))
        self.flips = [self.at(1 - self.x, self.y, self.z), self.at(self.x, 1 - self.y, self.z)]
        self.bits = [self.x, self.y]

    def at(self, x, y, z):
        return z * 4 + y * 2 + x

    def greet(self):
        barrier = pltpu.get_barrier_semaphore()

        def signal(target):
            pl.semaphore_signal(barrier, inc=1, device_id={"wide": target}, device_id_type=MESH)

        for target in self.flips:
            signal(target)

        @pl.when(self.edge)
        def _():
            signal(self.inward)
            pl.semaphore_wait(barrier, 3)

        @pl.when(self.middle)
        def _():
            signal(self.across)
            signal(self.outward)
            pl.semaphore_wait(barrier, 4)


def add_rows(held, start, other, rows):
    held[pl.ds(start, rows), :] = (
        held[pl.ds(start, rows), :].astype(jnp.float32) + other[...].astype(jnp.float32)
    ).astype(jnp.bfloat16)


class Chunk:
    STEPS = 8

    def __init__(self, links, job, refs, output, index, colour):
        self.links, self.colour, self.index, self.output = links, colour, index, output
        self.held = refs[0]
        self.pair_in, self.column_in, self.across_in, self.cross_in, self.back_in, self.gather_in = [
            ref.at[index, colour] for ref in refs[1:7]
        ]
        self.sent, self.got, self.loaded, self.stored = refs[7:11]
        self.half, self.quarter = job.chunk_rows // 2, job.chunk_rows // 4
        self.base = (2 * index + colour) * job.chunk_rows
        bit = links.bits[colour]
        self.keep = pl.multiple_of(self.base + bit * self.half, self.quarter)
        self.away = pl.multiple_of(self.base + (1 - bit) * self.half, self.quarter)
        self.near = pl.multiple_of(links.upper * self.quarter, self.quarter)
        self.far = pl.multiple_of((1 - links.upper) * self.quarter, self.quarter)
        self.kept = pl.multiple_of(self.keep + self.near, self.quarter)
        self.given = pl.multiple_of(self.keep + self.far, self.quarter)
        self.outer_peer = links.flips[colour]
        self.inner_peer = links.flips[1 - colour]

    def rows(self, start, size):
        return self.held.at[pl.ds(start, size), :]

    def part(self, ref, start):
        return ref.at[pl.ds(start, self.quarter), :]

    def copy(self, step, source, target, peer):
        return pltpu.make_async_remote_copy(
            src_ref=source,
            dst_ref=target,
            send_sem=self.sent.at[self.index, self.colour, step],
            recv_sem=self.got.at[self.index, self.colour, step],
            device_id={"wide": peer},
            device_id_type=MESH,
        )

    def outer(self):
        return self.copy(OUTER, self.rows(self.away, self.half), self.pair_in, self.outer_peer)

    def inward(self):
        return self.copy(INWARD, self.rows(self.keep, self.half), self.column_in, self.links.inward)

    def across(self):
        return self.copy(ACROSS, self.rows(self.given, self.quarter), self.across_in, self.links.across)

    def cross(self):
        return self.copy(CROSS, self.rows(self.kept, self.quarter), self.cross_in, self.inner_peer)

    def back(self):
        return self.copy(BACK, self.rows(self.kept, self.quarter), self.back_in, self.links.across)

    def out_a(self):
        target = self.part(self.column_in, self.near)
        return self.copy(OUT_A, self.rows(self.kept, self.quarter), target, self.links.outward)

    def out_b(self):
        return self.copy(OUT_B, self.back_in, self.part(self.column_in, self.far), self.links.outward)

    def gather_a(self, source):
        return self.copy(GATHER_A, source, self.part(self.gather_in, self.near), self.outer_peer)

    def gather_b(self, source):
        return self.copy(GATHER_B, source, self.part(self.gather_in, self.far), self.outer_peer)

    def store(self, place, source, start, size):
        target = self.output.at[pl.ds(start, size), :]
        return pltpu.make_async_copy(source, target, self.stored.at[self.index, self.colour, place])

    def totals(self, near, far):
        return self.store(0, near, self.kept, self.quarter), self.store(1, far, self.given, self.quarter)

    def partner_total(self):
        return self.store(2, self.gather_in, self.away, self.half)

    def step(self, number):
        links = self.links
        near_total = self.rows(self.kept, self.quarter)
        edge_near, edge_far = self.part(self.column_in, self.near), self.part(self.column_in, self.far)
        if number == 0:
            self.outer().start()
        if number == 1:
            self.outer().wait_recv()
            add_rows(self.held, self.keep, self.pair_in, self.half)

            @pl.when(links.edge)
            def _():
                self.inward().start()

        if number == 2:

            @pl.when(links.middle)
            def _():
                self.inward().wait_recv()
                add_rows(self.held, self.keep, self.column_in, self.half)
                self.across().start()

        if number == 3:

            @pl.when(links.middle)
            def _():
                self.across().wait_recv()
                add_rows(self.held, self.kept, self.across_in, self.quarter)
                self.cross().start()

        if number == 4:

            @pl.when(links.middle)
            def _():
                self.cross().wait()
                add_rows(self.held, self.kept, self.cross_in, self.quarter)
                self.back().start()
                self.out_a().start()
                self.gather_a(near_total).start()

        if number == 5:

            @pl.when(links.middle)
            def _():
                self.back().wait_recv()
                self.out_b().start()
                self.gather_b(self.back_in).start()
                for store in self.totals(near_total, self.back_in):
                    store.start()

            @pl.when(links.edge)
            def _():
                self.out_a().wait_recv()
                self.gather_a(edge_near).start()

        if number == 6:

            @pl.when(links.edge)
            def _():
                self.out_b().wait_recv()
                self.gather_b(edge_far).start()
                for store in self.totals(edge_near, edge_far):
                    store.start()

        if number == 7:
            self.gather_a(near_total).wait_recv()
            self.gather_b(self.back_in).wait_recv()
            self.partner_total().start()

    def close(self):
        near_total = self.rows(self.kept, self.quarter)
        self.outer().wait_send()
        self.gather_a(near_total).wait_send()
        self.gather_b(self.back_in).wait_send()

        @pl.when(self.links.middle)
        def _():
            self.across().wait_send()
            self.back().wait_send()
            self.out_a().wait_send()
            self.out_b().wait_send()

        @pl.when(self.links.edge)
        def _():
            self.inward().wait_send()

        for store in self.totals(near_total, self.back_in):
            store.wait()
        self.partner_total().wait()


def sum_kernel(jobs, *refs):
    count = len(jobs)
    inputs, outputs, scratch = refs[:count], refs[count : 2 * count], refs[2 * count :]
    per_job = len(scratch) // count
    links = Links()
    items = []
    for number, job in enumerate(jobs):
        own = scratch[number * per_job : (number + 1) * per_job]
        for index in range(job.count):
            pair = [Chunk(links, job, own, outputs[number], index, colour) for colour in range(2)]
            span = pl.ds(2 * index * job.chunk_rows, 2 * job.chunk_rows)
            load = pltpu.make_async_copy(inputs[number].at[span, :], own[0].at[span, :], own[9].at[index])
            load.start()
            items.append((pair, load))
    links.greet()
    for tick in range(len(items) + Chunk.STEPS - 1):
        for place, (pair, load) in enumerate(items):
            step = tick - place
            if 0 <= step < Chunk.STEPS:
                if step == 0:
                    load.wait()
                for chunk in pair:
                    chunk.step(step)
    for pair, _ in items:
        for chunk in pair:
            chunk.close()


def summed_over_wide(gradients, chunk_rows, collective_id):
    jobs = [Job(g.shape[0], g.shape[1], r) for g, r in zip(gradients, chunk_rows)]
    scratch = []
    for job in jobs:
        scratch += scratch_for(job)
    sent = sum(2 * g.size * 5 // 4 for g in gradients)
    return pl.pallas_call(
        functools.partial(sum_kernel, jobs),
        out_shape=[jax.ShapeDtypeStruct(g.shape, jnp.bfloat16) for g in gradients],
        in_specs=[pl.BlockSpec(memory_space=pl.ANY)] * len(jobs),
        out_specs=[pl.BlockSpec(memory_space=pl.ANY)] * len(jobs),
        scratch_shapes=scratch,
        compiler_params=pltpu.CompilerParams(
            collective_id=collective_id, has_side_effects=True, vmem_limit_bytes=60 * 1024 * 1024
        ),
        cost_estimate=pl.CostEstimate(flops=0, bytes_accessed=2 * sent, transcendentals=0),
    )(*gradients)


LANES = 128
QUERY_TILE = 512
BACK_TILE = 256


def nt_dot(left, right):
    return lax.dot_general(
        left, right, (((1,), (1,)), ((), ())), preferred_element_type=jnp.float32
    )


def nn_dot(left, right):
    return jnp.dot(left, right, preferred_element_type=jnp.float32)


def swap_lanes(values):
    lane = lax.broadcasted_iota(jnp.int32, values.shape, 1)
    half_dim = HD // 2
    ahead = pltpu.roll(values, LANES - half_dim, axis=1)
    behind = pltpu.roll(values, half_dim, axis=1)
    return jnp.where(lane % HD < half_dim, ahead, behind)


def head_lanes(rows, head):
    return lax.broadcasted_iota(jnp.int32, (rows, LANES), 1) // HD == head


def masked_keys(keys, mask, head):
    lane = lax.broadcasted_iota(jnp.int32, keys.shape, 1)
    spare = (1 - head) * HD
    keys = jnp.where(lane // HD == head, keys, jnp.zeros_like(keys))
    for block in range(2):
        keys = jnp.where(lane == spare + block, mask[:, block : block + 1], keys)
    return keys


def head_queries(queries, head, block):
    lane = lax.broadcasted_iota(jnp.int32, queries.shape, 1)
    spare = (1 - head) * HD
    queries = jnp.where(lane // HD == head, queries, jnp.zeros_like(queries))
    return jnp.where(lane == spare + block, jnp.ones_like(queries), queries)


def attend_kernel(
    query_raw, key_raw, value_raw, cosine, sine, mask, query_out, key_out, value_out, mixed_out, log_out, mixed_t
):
    rows = query_raw.shape[0]
    block_rows = rows // 2
    cos, sin = cosine[...], sine[...]
    queries = query_raw[...]
    query_out[...] = ((queries * cos + swap_lanes(queries) * sin) * HD ** (-0.5)).astype(jnp.bfloat16)
    keys = key_raw[...]
    key_out[...] = (keys * cos + swap_lanes(keys) * sin).astype(jnp.bfloat16)
    value_out[...] = value_raw[...].astype(jnp.bfloat16)
    values_t = value_out[...].T
    mask_low = mask[...].astype(jnp.bfloat16)
    keys_of = [masked_keys(key_out[...], mask_low, head) for head in range(2)]

    def tile(index, carry):
        span = pl.ds(pl.multiple_of(index * QUERY_TILE, QUERY_TILE), QUERY_TILE)
        block = index * QUERY_TILE // block_rows
        for head in range(2):
            scores = nt_dot(keys_of[head], head_queries(query_out[span, :], head, block))
            highest = jnp.max(scores, axis=0, keepdims=True)
            weights = jnp.exp(scores - highest)
            total = jnp.sum(weights, axis=0, keepdims=True)
            mixed = nn_dot(values_t[head * HD : (head + 1) * HD], weights.astype(jnp.bfloat16)) / total
            mixed_t[pl.ds(head * HD, HD), span] = mixed
            log_out[0, pl.ds(head, 1), span] = highest + jnp.log(total)
        return carry

    lax.fori_loop(0, rows // QUERY_TILE, tile, 0, unroll=True)
    mixed_out[...] = mixed_t[...].T.astype(jnp.bfloat16)


def attend(query_raw, key_raw, value_raw, cosine, sine, mask):
    rows, width = query_raw.shape
    pairs = width // LANES
    wide_block = pl.BlockSpec((rows, LANES), lambda pair: (0, pair))
    table = pl.BlockSpec((rows, LANES), lambda pair: (0, 0))
    low = jax.ShapeDtypeStruct((rows, width), jnp.bfloat16)
    return pl.pallas_call(
        attend_kernel,
        grid=(pairs,),
        in_specs=[wide_block] * 3 + [table, table, pl.BlockSpec((rows, 2), lambda pair: (0, 0))],
        out_specs=[wide_block] * 4 + [pl.BlockSpec((1, 2, rows), lambda pair: (pair, 0, 0))],
        out_shape=[low] * 4 + [jax.ShapeDtypeStruct((pairs, 2, rows), jnp.float32)],
        scratch_shapes=[pltpu.VMEM((LANES, rows), jnp.float32)],
        compiler_params=pltpu.CompilerParams(vmem_limit_bytes=32 * 1024 * 1024),
        cost_estimate=pl.CostEstimate(
            flops=4 * rows * rows * width, bytes_accessed=20 * rows * width, transcendentals=rows * rows * width // HD
        ),
    )(query_raw, key_raw, value_raw, cosine, sine, mask)


def attend_back_pair(
    query_rows, key_rows, value_rows, mixed_rows, grad_mixed, logs, cos, sin, mask, outs, grad_query_t, grad_key, grad_value, grad_t
):
    rows = query_rows.shape[0]
    block_rows = rows // 2
    mask_low = mask[...].astype(jnp.bfloat16)
    keys_t = key_rows[...].T
    values = value_rows[...]
    grad_t[...] = (grad_mixed[...].astype(jnp.float32) * mixed_rows[...].astype(jnp.float32)).T
    grad_key[...] = jnp.zeros_like(grad_key)
    grad_value[...] = jnp.zeros_like(grad_value)
    keys_of = [masked_keys(key_rows[...], mask_low, head) for head in range(2)]

    def tile(index, carry):
        span = pl.ds(pl.multiple_of(index * BACK_TILE, BACK_TILE), BACK_TILE)
        block = index * BACK_TILE // block_rows
        for head in range(2):
            inside = head_lanes(BACK_TILE, head)
            queries = query_rows[span, :]
            grads = grad_mixed[span, :]
            grads = jnp.where(inside, grads, jnp.zeros_like(grads))
            centre = jnp.sum(grad_t[pl.ds(head * HD, HD), span], axis=0, keepdims=True)
            scores = nt_dot(keys_of[head], head_queries(queries, head, block))
            probs = jnp.exp(scores - logs[0, pl.ds(head, 1), span])
            grad_probs = nt_dot(values, grads)
            grad_scores = (probs * (grad_probs - centre)).astype(jnp.bfloat16)
            grad_value[...] += nn_dot(probs.astype(jnp.bfloat16), grads)
            grad_key[...] += nn_dot(grad_scores, jnp.where(inside, queries, jnp.zeros_like(queries)))
            grad_query_t[pl.ds(head * HD, HD), span] = nn_dot(keys_t[head * HD : (head + 1) * HD], grad_scores)
        return carry

    lax.fori_loop(0, rows // BACK_TILE, tile, 0, unroll=True)
    grad_query = grad_query_t[...].T * HD ** (-0.5)
    outs[0][...] = (grad_query * cos[...] + swap_lanes(grad_query * sin[...])).astype(jnp.bfloat16)
    grad_keys = grad_key[...]
    outs[1][...] = (grad_keys * cos[...] + swap_lanes(grad_keys * sin[...])).astype(jnp.bfloat16)
    outs[2][...] = grad_value[...].astype(jnp.bfloat16)


def attend_back_kernel(
    query_rows, key_rows, value_rows, mixed_rows, grad_mixed, logs, cos, sin, mask, grad_q, grad_k, grad_v, *scratch
):
    attend_back_pair(
        query_rows, key_rows, value_rows, mixed_rows, grad_mixed, logs, cos, sin, mask, (grad_q, grad_k, grad_v), *scratch
    )


def attend_back(query_rows, key_rows, value_rows, mixed_rows, grad_mixed, logs, cosine, sine, mask):
    rows, width = query_rows.shape
    pairs = width // LANES
    wide_block = pl.BlockSpec((rows, LANES), lambda pair: (0, pair))
    table = pl.BlockSpec((rows, LANES), lambda pair: (0, 0))
    low = jax.ShapeDtypeStruct((rows, width), jnp.bfloat16)
    return pl.pallas_call(
        attend_back_kernel,
        grid=(pairs,),
        in_specs=[wide_block] * 5
        + [pl.BlockSpec((1, 2, rows), lambda pair: (pair, 0, 0)), table, table, pl.BlockSpec((rows, 2), lambda pair: (0, 0))],
        out_specs=[wide_block] * 3,
        out_shape=[low] * 3,
        scratch_shapes=[
            pltpu.VMEM((LANES, rows), jnp.float32),
            pltpu.VMEM((rows, LANES), jnp.float32),
            pltpu.VMEM((rows, LANES), jnp.float32),
            pltpu.VMEM((LANES, rows), jnp.float32),
        ],
        compiler_params=pltpu.CompilerParams(vmem_limit_bytes=32 * 1024 * 1024),
        cost_estimate=pl.CostEstimate(
            flops=10 * rows * rows * width, bytes_accessed=16 * rows * width, transcendentals=rows * rows * width // HD
        ),
    )(query_rows, key_rows, value_rows, mixed_rows, grad_mixed, logs, cosine, sine, mask)


def wide_index(x, y, z):
    return z * 4 + y * 2 + x


def chip_positions():
    return [(x, y, z) for z in range(PLANES) for y in range(2) for x in range(2)]


def flip_pairs(axis):
    if axis == "x":
        return [(wide_index(x, y, z), wide_index(1 - x, y, z)) for x, y, z in chip_positions()]
    return [(wide_index(x, y, z), wide_index(x, 1 - y, z)) for x, y, z in chip_positions()]


def plane_pairs(moves):
    return [
        (wide_index(x, y, src), wide_index(x, y, dst))
        for src, dst in moves
        for y in range(2)
        for x in range(2)
    ]


def send(values, pairs):
    return lax.ppermute(values, "wide", pairs)


def vector_sum(values):
    values = values + partner(values)
    values = values + send(values, flip_pairs("x"))
    values = values + send(values, flip_pairs("y"))
    values = values + send(values, plane_pairs(((0, 1), (3, 2))))
    values = values + send(values, plane_pairs(((1, 2), (2, 1))))
    plane = lax.axis_index("wide") // 4
    outward = send(values, plane_pairs(((1, 0), (2, 3))))
    return jnp.where((plane == 1) | (plane == 2), values, outward)


def partner(values):
    return lax.ppermute(values, "narrow", [(0, 1), (1, 0)])


def rows_of(own, other):
    return jnp.concatenate([own, other], axis=0)


def rotary_pair_tables(position):
    lane = jnp.arange(LANES) % HD
    half_dim = HD // 2
    frequency = ROPE_BASE ** (-2.0 * (lane % half_dim).astype(jnp.float32) / HD)
    angles = position[:, None] * frequency[None, :]
    signs = jnp.where(lane < half_dim, -1.0, 1.0).astype(jnp.float32)
    return (jnp.cos(angles), jnp.sin(angles) * signs)


def on_device(
    tokens,
    window_span,
    valid_len,
    norm1_gain,
    norm1_shift,
    w_query,
    w_key,
    w_value,
    w_out,
    norm2_gain,
    norm2_shift,
    w_gate,
    w_up,
    w_down,
    cotangent,
):
    block_rows = tokens.shape[0]
    own_block = lax.axis_index("narrow")
    joined = window_span[0] == 2
    block_ids = jnp.stack([own_block, 1 - own_block])
    lengths = valid_len[block_ids]
    offsets = jnp.arange(2 * block_rows)
    row_block = offsets // block_rows
    position = offsets % block_rows + block_rows * jnp.repeat(block_ids, block_rows) * joined.astype(jnp.int32)
    cosine, sine = rotary_pair_tables(position.astype(jnp.float32))
    within = offsets % block_rows < jnp.repeat(lengths, block_rows)
    seen = within[:, None] & (joined | (row_block[:, None] == jnp.arange(2)[None, :]))
    mask = jnp.where(seen, 0.0, MASKED).astype(jnp.float32)

    token_values = tokens.astype(jnp.float32)
    normed_one, scaled_one, inverse_one = norm_forward(token_values, norm1_gain, norm1_shift)
    normed_one = normed_one.astype(jnp.bfloat16)
    gathered_one = rows_of(normed_one, partner(normed_one))
    cot_rows = rows_of(cotangent, partner(cotangent))
    projected = [
        jnp.dot(gathered_one, weight, preferred_element_type=jnp.float32)
        for weight in (w_query, w_key, w_value)
    ]
    query_rows, key_rows, value_rows, mixed_rows, logs = attend(*projected, cosine, sine, mask)
    other_share = jnp.dot(mixed_rows[block_rows:], w_out, preferred_element_type=jnp.float32)
    resid_values = (
        token_values
        + jnp.dot(mixed_rows[:block_rows], w_out, preferred_element_type=jnp.float32)
        + partner(other_share)
    )
    normed_two, scaled_two, inverse_two = norm_forward(resid_values, norm2_gain, norm2_shift)
    normed_two = normed_two.astype(jnp.bfloat16)
    gathered_two = rows_of(normed_two, partner(normed_two))
    gate_values = jnp.dot(gathered_two, w_gate, preferred_element_type=jnp.float32)
    up_values = jnp.dot(gathered_two, w_up, preferred_element_type=jnp.float32)
    sigmoid_gate = jax.nn.sigmoid(gate_values)
    hidden_rows = (gate_values * sigmoid_gate * up_values).astype(jnp.bfloat16)
    down_grad = transpose_times(hidden_rows, cot_rows).astype(jnp.bfloat16)

    out_other = jnp.dot(
        hidden_rows[block_rows:], w_down, preferred_element_type=jnp.float32
    ).astype(jnp.bfloat16)
    out_values = (
        resid_values
        + jnp.dot(hidden_rows[:block_rows], w_down, preferred_element_type=jnp.float32)
        + partner(out_other).astype(jnp.float32)
    )
    grad_hidden = times_transpose(cot_rows, w_down)
    silu_grad = sigmoid_gate * (1.0 + gate_values * (1.0 - sigmoid_gate))
    grad_gate = (grad_hidden * up_values * silu_grad).astype(jnp.bfloat16)
    grad_up = (grad_hidden * gate_values * sigmoid_gate).astype(jnp.bfloat16)
    gate_grad = transpose_times(gathered_two, grad_gate).astype(jnp.bfloat16)
    up_grad = transpose_times(gathered_two, grad_up).astype(jnp.bfloat16)

    def grad_two_share(rows):
        return times_transpose(grad_gate[rows], w_gate) + times_transpose(grad_up[rows], w_up)

    grad_two_other = grad_two_share(slice(block_rows, None))
    grad_normed_two = grad_two_share(slice(0, block_rows)) + partner(grad_two_other)
    grad_in_two, gain_two_grad, shift_two_grad = norm_backward(
        grad_normed_two, scaled_two, inverse_two, norm2_gain
    )
    grad_resid = cotangent.astype(jnp.float32) + grad_in_two
    grad_attention = grad_resid.astype(jnp.bfloat16)
    grad_rows = rows_of(grad_attention, partner(grad_attention))
    grad_mixed = times_transpose(grad_rows, w_out).astype(jnp.bfloat16)
    out_grad = transpose_times(mixed_rows, grad_rows).astype(jnp.bfloat16)
    grad_projected = attend_back(
        query_rows, key_rows, value_rows, mixed_rows, grad_mixed, logs, cosine, sine, mask
    )
    qkv_grads = [transpose_times(gathered_one, g).astype(jnp.bfloat16) for g in grad_projected]

    def grad_one_share(rows):
        return sum(
            times_transpose(g[rows], weight)
            for g, weight in zip(grad_projected, (w_query, w_key, w_value))
        )

    grad_one_other = grad_one_share(slice(block_rows, None)).astype(jnp.bfloat16)
    grad_normed_one = grad_one_share(slice(0, block_rows)) + partner(grad_one_other).astype(
        jnp.float32
    )
    grad_in_one, gain_one_grad, shift_one_grad = norm_backward(
        grad_normed_one, scaled_one, inverse_one, norm1_gain
    )
    token_grad = grad_resid + grad_in_one
    norm_summed = vector_sum(
        jnp.stack([gain_one_grad, shift_one_grad, gain_two_grad, shift_two_grad])
    )
    down_summed, gate_summed, up_summed, out_summed, query_summed, key_summed, value_summed = [
        total.astype(jnp.float32)
        for total in summed_over_wide(
            [down_grad, gate_grad, up_grad, out_grad] + qkv_grads,
            [128, 64, 64, 128, 128, 128, 128],
            1,
        )
    ]
    return (
        out_values,
        token_grad,
        norm_summed[0],
        norm_summed[1],
        query_summed,
        key_summed,
        value_summed,
        out_summed,
        norm_summed[2],
        norm_summed[3],
        gate_summed,
        up_summed,
        down_summed,
    )


def solution(mesh):
    fits = mesh.shape["wide"] == PLANES * 4 and mesh.shape["narrow"] == 2
    in_specs = (
        P(("wide", "narrow"), None),
        P("wide"),
        P("wide"),
        P(),
        P(),
        P(None, "narrow"),
        P(None, "narrow"),
        P(None, "narrow"),
        P("narrow", None),
        P(),
        P(),
        P(None, "narrow"),
        P(None, "narrow"),
        P("narrow", None),
        P(("wide", "narrow"), None),
    )
    out_specs = (
        P(("wide", "narrow"), None),
        P(("wide", "narrow"), None),
        P(),
        P(),
        P(None, "narrow"),
        P(None, "narrow"),
        P(None, "narrow"),
        P("narrow", None),
        P(),
        P(),
        P(None, "narrow"),
        P(None, "narrow"),
        P("narrow", None),
    )
    return jax.shard_map(
        on_device if fits else on_device_any_mesh, mesh=mesh, in_specs=in_specs, out_specs=out_specs, check_vma=False
    )
```

```python
import functools

import jax
import jax.numpy as jnp
from jax import lax
from jax.experimental import pallas as pl
from jax.experimental.pallas import tpu as pltpu
from jax.sharding import PartitionSpec as P

MESH = pl.DeviceIdType.MESH

HD = 64


EPSILON = 1e-05
MASKED = -1e30
ROPE_BASE = 10000.0


def times_transpose(left, right):
    return lax.dot_general(
        left, right, (((1,), (1,)), ((), ())), preferred_element_type=jnp.float32
    )


def transpose_times(left, right):
    return lax.dot_general(
        left, right, (((0,), (0,)), ((), ())), preferred_element_type=jnp.float32
    )


def norm_forward(values, norm_gain, norm_shift):
    average = jnp.mean(values, axis=-1, keepdims=True)
    centred = values - average
    inverse = lax.rsqrt(jnp.mean(centred * centred, axis=-1, keepdims=True) + EPSILON)
    scaled = centred * inverse
    return (scaled * norm_gain + norm_shift, scaled, inverse)


def norm_backward(grad_out, scaled, inverse, norm_gain):
    grad_scaled = grad_out * norm_gain
    first_term = jnp.mean(grad_scaled, axis=-1, keepdims=True)
    second_term = jnp.mean(grad_scaled * scaled, axis=-1, keepdims=True)
    grad_in = inverse * (grad_scaled - first_term - scaled * second_term)
    return (grad_in, jnp.sum(grad_out * scaled, axis=0), jnp.sum(grad_out, axis=0))


def rotary_tables(span_table, block_rows, width):
    row_count = span_table.shape[0] * block_rows
    row_ids = jnp.arange(row_count)
    block_ids = row_ids // block_rows
    span_rows = jnp.repeat(span_table, block_rows)
    position = (row_ids % block_rows + block_rows * (block_ids % 2) * (span_rows == 2)).astype(
        jnp.float32
    )
    columns = jnp.arange(width) % HD
    half_dim = HD // 2
    freq_index = (columns % half_dim).astype(jnp.float32)
    frequency = ROPE_BASE ** (-2.0 * freq_index / HD)
    angles = position[:, None] * frequency[None, :]
    signs = jnp.where(columns < half_dim, -1.0, 1.0).astype(jnp.float32)
    return (jnp.cos(angles), jnp.sin(angles) * signs)


def swap_halves(values):
    row_count = values.shape[0]
    width = values.shape[1]
    parts = values.reshape(row_count, width // HD, 2, HD // 2)
    return jnp.flip(parts, axis=2).reshape(row_count, width)


def rotate(values, cosine, sine_signed):
    return values * cosine + swap_halves(values) * sine_signed


def rotate_back(grads_in, cosine, sine_signed):
    return grads_in * cosine + swap_halves(grads_in * sine_signed)


def pair_mask(block_index, span_table, valid_table, block_rows):
    pair_first = block_index // 2 * 2
    offsets = jnp.arange(2 * block_rows)
    key_block = pair_first + offsets // block_rows
    within = offsets % block_rows
    first_len = lax.dynamic_index_in_dim(valid_table, pair_first, keepdims=False)
    second_len = lax.dynamic_index_in_dim(valid_table, pair_first + 1, keepdims=False)
    own_span = lax.dynamic_index_in_dim(span_table, block_index, keepdims=False)
    length_bound = jnp.where(offsets < block_rows, first_len, second_len)
    return (within < length_bound) & ((own_span == 2) | (key_block == block_index))


def on_device_any_mesh(
    tokens,
    window_span,
    valid_len,
    norm1_gain,
    norm1_shift,
    w_query,
    w_key,
    w_value,
    w_out,
    norm2_gain,
    norm2_shift,
    w_gate,
    w_up,
    w_down,
    cotangent,
):
    local_rows = tokens.shape[0]
    group_rows = local_rows * lax.axis_size("narrow")
    block_count = window_span.shape[0]
    block_rows = group_rows // block_count
    local_width = w_query.shape[1]
    local_heads = local_width // HD
    local_hidden = w_gate.shape[1]
    softmax_scale = HD ** (-0.5)
    token_values = tokens.astype(jnp.float32)
    normed_one, scaled_one, inverse_one = norm_forward(token_values, norm1_gain, norm1_shift)
    normed_one = normed_one.astype(jnp.bfloat16)
    gathered_one = lax.all_gather(normed_one, "narrow", axis=0, tiled=True)
    joined_qkv = jnp.concatenate([w_query, w_key, w_value], axis=1)
    projected = jnp.dot(gathered_one, joined_qkv, preferred_element_type=jnp.float32)
    cosine, sine_signed = rotary_tables(window_span, block_rows, local_width)
    query_rows = (rotate(projected[:, :local_width], cosine, sine_signed) * softmax_scale).astype(
        jnp.bfloat16
    )
    key_rows = rotate(projected[:, local_width : 2 * local_width], cosine, sine_signed).astype(
        jnp.bfloat16
    )
    value_rows = projected[:, 2 * local_width :].astype(jnp.bfloat16)

    def block_slices(block_index):
        query_block = lax.dynamic_slice_in_dim(query_rows, block_index * block_rows, block_rows, 0)
        pair_start = block_index // 2 * 2 * block_rows
        return (
            query_block.reshape(block_rows, local_heads, HD),
            key_rows.reshape(2 * block_rows, local_heads, HD),
            value_rows.reshape(2 * block_rows, local_heads, HD),
            pair_start,
        )

    def masked_scores(block_index, query_block, key_pair):
        scores = jnp.einsum(
            "qhd,khd->hqk", query_block, key_pair, preferred_element_type=jnp.float32
        )
        key_mask = pair_mask(block_index, window_span, valid_len, block_rows)
        return jnp.where(key_mask[None, None, :], scores, MASKED)

    def attend_forward(block_index):
        query_block, key_pair, value_pair, pair_start = block_slices(block_index)
        scores = masked_scores(block_index, query_block, key_pair)
        highest = jnp.max(scores, axis=-1, keepdims=True)
        weights = jnp.exp(scores - highest)
        weight_total = jnp.sum(weights, axis=-1, keepdims=True)
        attention_probs = (weights / weight_total).astype(jnp.bfloat16)
        mixed_block = jnp.einsum(
            "hqk,khd->qhd", attention_probs, value_pair, preferred_element_type=jnp.float32
        )
        return (
            mixed_block.reshape(block_rows, local_width).astype(jnp.bfloat16),
            (highest + jnp.log(weight_total))[:, :, 0],
        )

    mixed_blocks, log_totals = lax.map(attend_forward, jnp.arange(block_count))
    mixed_rows = mixed_blocks.reshape(group_rows, local_width)
    resid_values = token_values + lax.psum_scatter(
        jnp.dot(mixed_rows, w_out, preferred_element_type=jnp.float32),
        "narrow",
        scatter_dimension=0,
        tiled=True,
    )
    normed_two, scaled_two, inverse_two = norm_forward(resid_values, norm2_gain, norm2_shift)
    normed_two = normed_two.astype(jnp.bfloat16)
    gathered_two = lax.all_gather(normed_two, "narrow", axis=0, tiled=True)
    joined_gate_up = jnp.concatenate([w_gate, w_up], axis=1)
    gate_up = jnp.dot(gathered_two, joined_gate_up, preferred_element_type=jnp.float32)
    gate_values = gate_up[:, :local_hidden]
    up_values = gate_up[:, local_hidden:]
    sigmoid_gate = jax.nn.sigmoid(gate_values)
    hidden_rows = (gate_values * sigmoid_gate * up_values).astype(jnp.bfloat16)
    out_values = resid_values + lax.psum_scatter(
        jnp.dot(hidden_rows, w_down, preferred_element_type=jnp.float32).astype(jnp.bfloat16),
        "narrow",
        scatter_dimension=0,
        tiled=True,
    ).astype(jnp.float32)
    shard_rows = lax.all_gather(cotangent, "narrow", axis=0, tiled=True)
    grad_hidden = times_transpose(shard_rows, w_down)
    grad_down_w, grad_hidden = (transpose_times(hidden_rows, shard_rows), grad_hidden)
    silu_grad = sigmoid_gate * (1.0 + gate_values * (1.0 - sigmoid_gate))
    grad_gate_up = jnp.concatenate(
        [grad_hidden * up_values * silu_grad, grad_hidden * gate_values * sigmoid_gate], axis=1
    ).astype(jnp.bfloat16)
    grad_normed_two = lax.psum_scatter(
        times_transpose(grad_gate_up, joined_gate_up), "narrow", scatter_dimension=0, tiled=True
    )
    grad_gate_up_w = transpose_times(gathered_two, grad_gate_up)
    grad_in_two, gain_two_grad, shift_two_grad = norm_backward(
        grad_normed_two, scaled_two, inverse_two, norm2_gain
    )
    grad_resid = cotangent.astype(jnp.float32) + grad_in_two
    shard_rows = lax.all_gather(grad_resid.astype(jnp.bfloat16), "narrow", axis=0, tiled=True)
    grad_mixed_sum = times_transpose(shard_rows, w_out)
    grad_out_w, grad_mixed_sum = (transpose_times(mixed_rows, shard_rows), grad_mixed_sum)
    grad_mixed = grad_mixed_sum.astype(jnp.bfloat16)

    def attend_backward(block_index, running):
        grad_query, grad_key, grad_value = running
        query_block, key_pair, value_pair, pair_start = block_slices(block_index)
        grad_rows = lax.dynamic_slice_in_dim(
            grad_mixed, block_index * block_rows, block_rows, 0
        ).reshape(block_rows, local_heads, HD)
        scores = masked_scores(block_index, query_block, key_pair)
        log_total = lax.dynamic_index_in_dim(log_totals, block_index, keepdims=False)
        attention_probs = jnp.exp(scores - log_total[:, :, None])
        grad_probs = jnp.einsum(
            "qhd,khd->hqk", grad_rows, value_pair, preferred_element_type=jnp.float32
        )
        centre = jnp.sum(attention_probs * grad_probs, axis=-1, keepdims=True)
        grad_scores = (attention_probs * (grad_probs - centre)).astype(jnp.bfloat16)
        block_query = jnp.einsum(
            "hqk,khd->qhd", grad_scores, key_pair, preferred_element_type=jnp.float32
        ).reshape(block_rows, local_width)
        pair_key = jnp.einsum(
            "hqk,qhd->khd", grad_scores, query_block, preferred_element_type=jnp.float32
        ).reshape(2 * block_rows, local_width)
        pair_value = jnp.einsum(
            "hqk,qhd->khd",
            attention_probs.astype(jnp.bfloat16),
            grad_rows,
            preferred_element_type=jnp.float32,
        ).reshape(2 * block_rows, local_width)
        grad_query = lax.dynamic_update_slice_in_dim(
            grad_query, block_query, block_index * block_rows, 0
        )
        grad_key = grad_key + pair_key
        grad_value = grad_value + pair_value
        return (grad_query, grad_key, grad_value)

    zero_rows = jnp.zeros((group_rows, local_width), jnp.float32)
    grad_query, grad_key, grad_value = lax.fori_loop(
        0, block_count, attend_backward, (zero_rows, zero_rows, zero_rows)
    )
    grad_query_raw = rotate_back(grad_query * softmax_scale, cosine, sine_signed)
    grad_key_raw = rotate_back(grad_key, cosine, sine_signed)
    grad_qkv = jnp.concatenate([grad_query_raw, grad_key_raw, grad_value], axis=1).astype(
        jnp.bfloat16
    )
    grad_normed_one = lax.psum_scatter(
        times_transpose(grad_qkv, joined_qkv).astype(jnp.bfloat16),
        "narrow",
        scatter_dimension=0,
        tiled=True,
    ).astype(jnp.float32)
    grad_qkv_w = transpose_times(gathered_one, grad_qkv)
    grad_in_one, gain_one_grad, shift_one_grad = norm_backward(
        grad_normed_one, scaled_one, inverse_one, norm1_gain
    )
    token_grad = grad_resid + grad_in_one
    qkv_summed, out_summed, gate_up_summed, down_summed = (
        lax.psum(grad_qkv_w.astype(jnp.bfloat16), "wide").astype(jnp.float32),
        lax.psum(grad_out_w.astype(jnp.bfloat16), "wide").astype(jnp.float32),
        lax.psum(grad_gate_up_w.astype(jnp.bfloat16), "wide").astype(jnp.float32),
        lax.psum(grad_down_w.astype(jnp.bfloat16), "wide").astype(jnp.float32),
    )
    norm_summed = lax.psum(
        (gain_one_grad, shift_one_grad, gain_two_grad, shift_two_grad), ("wide", "narrow")
    )
    return (
        out_values,
        token_grad,
        norm_summed[0],
        norm_summed[1],
        qkv_summed[:, :local_width],
        qkv_summed[:, local_width : 2 * local_width],
        qkv_summed[:, 2 * local_width :],
        out_summed,
        norm_summed[2],
        norm_summed[3],
        gate_up_summed[:, :local_hidden],
        gate_up_summed[:, local_hidden:],
        down_summed,
    )


PLANES = 4


class Job:
    def __init__(self, rows, cols, chunk_rows):
        self.rows, self.cols, self.chunk_rows = rows, cols, chunk_rows
        self.count = rows // (2 * chunk_rows)


def scratch_for(job):
    half, quarter = job.chunk_rows // 2, job.chunk_rows // 4

    def slots(rows):
        return pltpu.VMEM((job.count, 2, rows, job.cols), jnp.bfloat16)

    return [
        pltpu.VMEM((job.rows, job.cols), jnp.bfloat16),
        slots(half),
        slots(half),
        slots(quarter),
        slots(quarter),
        slots(quarter),
        slots(half),
        pltpu.SemaphoreType.DMA((job.count, 2, 9)),
        pltpu.SemaphoreType.DMA((job.count, 2, 9)),
        pltpu.SemaphoreType.DMA((job.count,)),
        pltpu.SemaphoreType.DMA((job.count, 2, 3)),
    ]


OUTER, INWARD, ACROSS, CROSS, BACK, OUT_A, OUT_B, GATHER_A, GATHER_B = range(9)


class Links:
    def __init__(self):
        position = lax.axis_index("wide")
        self.x = lax.rem(position, 2)
        self.y = lax.rem(position // 2, 2)
        self.z = position // 4
        self.middle = jnp.logical_and(self.z >= 1, self.z <= 2)
        self.edge = jnp.logical_or(self.z == 0, self.z == PLANES - 1)
        self.upper = self.z // 2
        self.across = self.at(self.x, self.y, 3 - self.z)
        step = 1 - 2 * self.upper
        self.inward = self.at(self.x, self.y, lax.rem(self.z + step + PLANES, PLANES))
        self.outward = self.at(self.x, self.y, lax.rem(self.z - step + PLANES, PLANES))
        self.flips = [self.at(1 - self.x, self.y, self.z), self.at(self.x, 1 - self.y, self.z)]
        self.bits = [self.x, self.y]

    def at(self, x, y, z):
        return z * 4 + y * 2 + x

    def greet(self):
        barrier = pltpu.get_barrier_semaphore()

        def signal(target):
            pl.semaphore_signal(barrier, inc=1, device_id={"wide": target}, device_id_type=MESH)

        pl.semaphore_signal(
            barrier, inc=1, device_id={"narrow": 1 - lax.axis_index("narrow")}, device_id_type=MESH
        )
        for target in self.flips:
            signal(target)

        @pl.when(self.edge)
        def _():
            signal(self.inward)
            pl.semaphore_wait(barrier, 4)

        @pl.when(self.middle)
        def _():
            signal(self.across)
            signal(self.outward)
            pl.semaphore_wait(barrier, 5)


ADD_ROWS = 16


def add_rows(held, start, other, rows):
    def add(index, carry):
        own = pl.ds(pl.multiple_of(start + index * ADD_ROWS, ADD_ROWS), ADD_ROWS)
        arrived = other[pl.ds(pl.multiple_of(index * ADD_ROWS, ADD_ROWS), ADD_ROWS), :]
        held[own, :] = (held[own, :].astype(jnp.float32) + arrived.astype(jnp.float32)).astype(jnp.bfloat16)
        return carry

    lax.fori_loop(0, rows // ADD_ROWS, add, 0)


class Vectors:
    STEPS = 7

    def __init__(self, links, source, output, stages, arrived, sent, got):
        self.links, self.source, self.output = links, source, output
        self.stages, self.arrived, self.sent, self.got = stages, arrived, sent, got

    def copy(self, number, source, target):
        return pltpu.make_async_remote_copy(
            src_ref=source,
            dst_ref=self.arrived.at[number],
            send_sem=self.sent.at[number],
            recv_sem=self.got.at[number],
            device_id=target,
            device_id_type=MESH,
        )

    def exchange(self, number):
        links = self.links
        targets = [
            {"narrow": 1 - lax.axis_index("narrow")},
            {"wide": links.flips[0]},
            {"wide": links.flips[1]},
            {"wide": links.inward},
            {"wide": links.across},
            {"wide": links.outward},
        ]
        source = self.source if number == 0 else self.stages.at[number]
        return self.copy(number, source, targets[number])

    def add(self, number):
        source = self.source if number == 0 else self.stages.at[number]
        self.stages[number + 1] = source[...] + self.arrived[number]

    def step(self, number):
        links = self.links
        if number in (1, 2, 3):
            self.exchange(number - 1).wait_recv()
            self.add(number - 1)
        if number < 3:
            self.exchange(number).start()
        if number == 3:

            @pl.when(links.edge)
            def _():
                self.exchange(3).start()

        if number in (4, 5):

            @pl.when(links.middle)
            def _():
                self.exchange(number - 1).wait_recv()
                self.add(number - 1)
                self.exchange(number).start()

        if number == 6:

            @pl.when(links.middle)
            def _():
                self.output[...] = self.stages[5]

            @pl.when(links.edge)
            def _():
                self.exchange(5).wait_recv()
                self.output[...] = self.arrived[5]

    def close(self):
        for number in range(3):
            self.exchange(number).wait_send()

        @pl.when(self.links.edge)
        def _():
            self.exchange(3).wait_send()

        @pl.when(self.links.middle)
        def _():
            self.exchange(4).wait_send()
            self.exchange(5).wait_send()


class Chunk:
    STEPS = 8

    def __init__(self, links, job, refs, output, index, colour):
        self.links, self.colour, self.index, self.output = links, colour, index, output
        self.held = refs[0]
        self.pair_in, self.column_in, self.across_in, self.cross_in, self.back_in, self.gather_in = [
            ref.at[index, colour] for ref in refs[1:7]
        ]
        self.sent, self.got, self.loaded, self.stored = refs[7:11]
        self.half, self.quarter = job.chunk_rows // 2, job.chunk_rows // 4
        self.base = (2 * index + colour) * job.chunk_rows
        bit = links.bits[colour]
        self.keep = pl.multiple_of(self.base + bit * self.half, self.quarter)
        self.away = pl.multiple_of(self.base + (1 - bit) * self.half, self.quarter)
        self.near = pl.multiple_of(links.upper * self.quarter, self.quarter)
        self.far = pl.multiple_of((1 - links.upper) * self.quarter, self.quarter)
        self.kept = pl.multiple_of(self.keep + self.near, self.quarter)
        self.given = pl.multiple_of(self.keep + self.far, self.quarter)
        self.outer_peer = links.flips[colour]
        self.inner_peer = links.flips[1 - colour]

    def rows(self, start, size):
        return self.held.at[pl.ds(start, size), :]

    def part(self, ref, start):
        return ref.at[pl.ds(start, self.quarter), :]

    def copy(self, step, source, target, peer):
        return pltpu.make_async_remote_copy(
            src_ref=source,
            dst_ref=target,
            send_sem=self.sent.at[self.index, self.colour, step],
            recv_sem=self.got.at[self.index, self.colour, step],
            device_id={"wide": peer},
            device_id_type=MESH,
        )

    def outer(self):
        return self.copy(OUTER, self.rows(self.away, self.half), self.pair_in, self.outer_peer)

    def inward(self):
        return self.copy(INWARD, self.rows(self.keep, self.half), self.column_in, self.links.inward)

    def across(self):
        return self.copy(ACROSS, self.rows(self.given, self.quarter), self.across_in, self.links.across)

    def cross(self):
        return self.copy(CROSS, self.rows(self.kept, self.quarter), self.cross_in, self.inner_peer)

    def back(self):
        return self.copy(BACK, self.rows(self.kept, self.quarter), self.back_in, self.links.across)

    def out_a(self):
        target = self.part(self.column_in, self.near)
        return self.copy(OUT_A, self.rows(self.kept, self.quarter), target, self.links.outward)

    def out_b(self):
        return self.copy(OUT_B, self.back_in, self.part(self.column_in, self.far), self.links.outward)

    def gather_a(self, source):
        return self.copy(GATHER_A, source, self.part(self.gather_in, self.near), self.outer_peer)

    def gather_b(self, source):
        return self.copy(GATHER_B, source, self.part(self.gather_in, self.far), self.outer_peer)

    def store(self, place, source, start, size):
        target = self.output.at[pl.ds(start, size), :]
        return pltpu.make_async_copy(source, target, self.stored.at[self.index, self.colour, place])

    def totals(self, near, far):
        return self.store(0, near, self.kept, self.quarter), self.store(1, far, self.given, self.quarter)

    def partner_total(self):
        return self.store(2, self.gather_in, self.away, self.half)

    def step(self, number):
        links = self.links
        near_total = self.rows(self.kept, self.quarter)
        edge_near, edge_far = self.part(self.column_in, self.near), self.part(self.column_in, self.far)
        if number == 0:
            self.outer().start()
        if number == 1:
            self.outer().wait_recv()
            add_rows(self.held, self.keep, self.pair_in, self.half)

            @pl.when(links.edge)
            def _():
                self.inward().start()

        if number == 2:

            @pl.when(links.middle)
            def _():
                self.inward().wait_recv()
                add_rows(self.held, self.keep, self.column_in, self.half)
                self.across().start()

        if number == 3:

            @pl.when(links.middle)
            def _():
                self.across().wait_recv()
                add_rows(self.held, self.kept, self.across_in, self.quarter)
                self.cross().start()

        if number == 4:

            @pl.when(links.middle)
            def _():
                self.cross().wait()
                add_rows(self.held, self.kept, self.cross_in, self.quarter)
                self.back().start()
                self.out_a().start()
                self.gather_a(near_total).start()

        if number == 5:

            @pl.when(links.middle)
            def _():
                self.back().wait_recv()
                self.out_b().start()
                self.gather_b(self.back_in).start()
                for store in self.totals(near_total, self.back_in):
                    store.start()

            @pl.when(links.edge)
            def _():
                self.out_a().wait_recv()
                self.gather_a(edge_near).start()

        if number == 6:

            @pl.when(links.edge)
            def _():
                self.out_b().wait_recv()
                self.gather_b(edge_far).start()
                for store in self.totals(edge_near, edge_far):
                    store.start()

        if number == 7:
            self.gather_a(near_total).wait_recv()
            self.gather_b(self.back_in).wait_recv()
            self.partner_total().start()

    def close(self):
        near_total = self.rows(self.kept, self.quarter)
        self.outer().wait_send()
        self.gather_a(near_total).wait_send()
        self.gather_b(self.back_in).wait_send()

        @pl.when(self.links.middle)
        def _():
            self.across().wait_send()
            self.back().wait_send()
            self.out_a().wait_send()
            self.out_b().wait_send()

        @pl.when(self.links.edge)
        def _():
            self.inward().wait_send()

        for store in self.totals(near_total, self.back_in):
            store.wait()
        self.partner_total().wait()


def sum_kernel(jobs, *refs):
    count = len(jobs)
    inputs, refs = refs[: count + 1], refs[count + 1 :]
    outputs, scratch = refs[: count + 1], refs[count + 1 :]
    scratch, vector_scratch = scratch[:-4], scratch[-4:]
    per_job = len(scratch) // count
    links = Links()
    vectors = Vectors(links, inputs[count], outputs[count], *vector_scratch)
    items = []
    for number, job in enumerate(jobs):
        own = scratch[number * per_job : (number + 1) * per_job]
        for index in range(job.count):
            pair = [Chunk(links, job, own, outputs[number], index, colour) for colour in range(2)]
            span = pl.ds(2 * index * job.chunk_rows, 2 * job.chunk_rows)
            load = pltpu.make_async_copy(inputs[number].at[span, :], own[0].at[span, :], own[9].at[index])
            load.start()
            items.append((pair, load))
    links.greet()
    for tick in range(len(items) + Chunk.STEPS - 1):
        if tick < Vectors.STEPS:
            vectors.step(tick)
        for place, (pair, load) in enumerate(items):
            step = tick - place
            if 0 <= step < Chunk.STEPS:
                if step == 0:
                    load.wait()
                for chunk in pair:
                    chunk.step(step)
    for pair, _ in items:
        for chunk in pair:
            chunk.close()
    vectors.close()


def summed_over_wide(gradients, chunk_rows, vectors, collective_id):
    jobs = [Job(g.shape[0], g.shape[1], r) for g, r in zip(gradients, chunk_rows)]
    scratch = []
    for job in jobs:
        scratch += scratch_for(job)
    scratch += [
        pltpu.VMEM((6, *vectors.shape), jnp.float32),
        pltpu.VMEM((6, *vectors.shape), jnp.float32),
        pltpu.SemaphoreType.DMA((6,)),
        pltpu.SemaphoreType.DMA((6,)),
    ]
    sent = sum(2 * g.size * 5 // 4 for g in gradients)
    return pl.pallas_call(
        functools.partial(sum_kernel, jobs),
        out_shape=[jax.ShapeDtypeStruct(g.shape, jnp.bfloat16) for g in gradients]
        + [jax.ShapeDtypeStruct(vectors.shape, jnp.float32)],
        in_specs=[pl.BlockSpec(memory_space=pl.ANY)] * len(jobs) + [pl.BlockSpec(memory_space=pltpu.VMEM)],
        out_specs=[pl.BlockSpec(memory_space=pl.ANY)] * len(jobs) + [pl.BlockSpec(memory_space=pltpu.VMEM)],
        scratch_shapes=scratch,
        compiler_params=pltpu.CompilerParams(
            collective_id=collective_id, has_side_effects=True, vmem_limit_bytes=60 * 1024 * 1024
        ),
        cost_estimate=pl.CostEstimate(flops=0, bytes_accessed=2 * sent, transcendentals=0),
    )(*gradients, vectors)


LANES = 128
QUERY_TILE = 512
BACK_TILE = 256


def nt_dot(left, right):
    return lax.dot_general(
        left, right, (((1,), (1,)), ((), ())), preferred_element_type=jnp.float32
    )


def nn_dot(left, right):
    return jnp.dot(left, right, preferred_element_type=jnp.float32)


def swap_lanes(values):
    lane = lax.broadcasted_iota(jnp.int32, values.shape, 1)
    half_dim = HD // 2
    ahead = pltpu.roll(values, LANES - half_dim, axis=1)
    behind = pltpu.roll(values, half_dim, axis=1)
    return jnp.where(lane % HD < half_dim, ahead, behind)


def head_lanes(rows, head):
    return lax.broadcasted_iota(jnp.int32, (rows, LANES), 1) // HD == head


def masked_keys(keys, mask, head):
    lane = lax.broadcasted_iota(jnp.int32, keys.shape, 1)
    spare = (1 - head) * HD
    keys = jnp.where(lane // HD == head, keys, jnp.zeros_like(keys))
    for block in range(2):
        keys = jnp.where(lane == spare + block, mask[:, block : block + 1], keys)
    return keys


def head_queries(queries, head, block):
    lane = lax.broadcasted_iota(jnp.int32, queries.shape, 1)
    spare = (1 - head) * HD
    queries = jnp.where(lane // HD == head, queries, jnp.zeros_like(queries))
    return jnp.where(lane == spare + block, jnp.ones_like(queries), queries)


def attend_kernel(
    query_raw, key_raw, value_raw, cosine, sine, mask, query_out, key_out, value_out, mixed_out, log_out, mixed_t
):
    rows = query_raw.shape[0]
    block_rows = rows // 2
    cos, sin = cosine[...], sine[...]
    queries = query_raw[...]
    query_out[...] = ((queries * cos + swap_lanes(queries) * sin) * HD ** (-0.5)).astype(jnp.bfloat16)
    keys = key_raw[...]
    key_out[...] = (keys * cos + swap_lanes(keys) * sin).astype(jnp.bfloat16)
    value_out[...] = value_raw[...].astype(jnp.bfloat16)
    values_t = value_out[...].T
    mask_low = mask[...].astype(jnp.bfloat16)
    keys_of = [masked_keys(key_out[...], mask_low, head) for head in range(2)]

    def tile(index, carry):
        span = pl.ds(pl.multiple_of(index * QUERY_TILE, QUERY_TILE), QUERY_TILE)
        block = index * QUERY_TILE // block_rows
        for head in range(2):
            scores = nt_dot(keys_of[head], head_queries(query_out[span, :], head, block))
            highest = jnp.max(scores, axis=0, keepdims=True)
            weights = jnp.exp(scores - highest)
            total = jnp.sum(weights, axis=0, keepdims=True)
            mixed = nn_dot(values_t[head * HD : (head + 1) * HD], weights.astype(jnp.bfloat16)) / total
            mixed_t[pl.ds(head * HD, HD), span] = mixed
            log_out[0, pl.ds(head, 1), span] = highest + jnp.log(total)
        return carry

    lax.fori_loop(0, rows // QUERY_TILE, tile, 0, unroll=True)
    mixed_out[...] = mixed_t[...].T.astype(jnp.bfloat16)


def attend(query_raw, key_raw, value_raw, cosine, sine, mask):
    rows, width = query_raw.shape
    pairs = width // LANES
    wide_block = pl.BlockSpec((rows, LANES), lambda pair: (0, pair))
    table = pl.BlockSpec((rows, LANES), lambda pair: (0, 0))
    low = jax.ShapeDtypeStruct((rows, width), jnp.bfloat16)
    return pl.pallas_call(
        attend_kernel,
        grid=(pairs,),
        in_specs=[wide_block] * 3 + [table, table, pl.BlockSpec((rows, 2), lambda pair: (0, 0))],
        out_specs=[wide_block] * 4 + [pl.BlockSpec((1, 2, rows), lambda pair: (pair, 0, 0))],
        out_shape=[low] * 4 + [jax.ShapeDtypeStruct((pairs, 2, rows), jnp.float32)],
        scratch_shapes=[pltpu.VMEM((LANES, rows), jnp.float32)],
        compiler_params=pltpu.CompilerParams(vmem_limit_bytes=32 * 1024 * 1024),
        cost_estimate=pl.CostEstimate(
            flops=4 * rows * rows * width, bytes_accessed=20 * rows * width, transcendentals=rows * rows * width // HD
        ),
    )(query_raw, key_raw, value_raw, cosine, sine, mask)


def attend_back_pair(
    query_rows, key_rows, value_rows, mixed_rows, grad_mixed, logs, cos, sin, mask, outs, grad_query_t, grad_key, grad_value, grad_t
):
    rows = query_rows.shape[0]
    block_rows = rows // 2
    mask_low = mask[...].astype(jnp.bfloat16)
    keys_t = key_rows[...].T
    values = value_rows[...]
    grad_t[...] = (grad_mixed[...].astype(jnp.float32) * mixed_rows[...].astype(jnp.float32)).T
    grad_key[...] = jnp.zeros_like(grad_key)
    grad_value[...] = jnp.zeros_like(grad_value)
    keys_of = [masked_keys(key_rows[...], mask_low, head) for head in range(2)]

    def tile(index, carry):
        span = pl.ds(pl.multiple_of(index * BACK_TILE, BACK_TILE), BACK_TILE)
        block = index * BACK_TILE // block_rows
        for head in range(2):
            inside = head_lanes(BACK_TILE, head)
            queries = query_rows[span, :]
            grads = grad_mixed[span, :]
            grads = jnp.where(inside, grads, jnp.zeros_like(grads))
            centre = jnp.sum(grad_t[pl.ds(head * HD, HD), span], axis=0, keepdims=True)
            scores = nt_dot(keys_of[head], head_queries(queries, head, block))
            probs = jnp.exp(scores - logs[0, pl.ds(head, 1), span])
            grad_probs = nt_dot(values, grads)
            grad_scores = (probs * (grad_probs - centre)).astype(jnp.bfloat16)
            grad_value[...] += nn_dot(probs.astype(jnp.bfloat16), grads)
            grad_key[...] += nn_dot(grad_scores, jnp.where(inside, queries, jnp.zeros_like(queries)))
            grad_query_t[pl.ds(head * HD, HD), span] = nn_dot(keys_t[head * HD : (head + 1) * HD], grad_scores)
        return carry

    lax.fori_loop(0, rows // BACK_TILE, tile, 0, unroll=True)
    grad_query = grad_query_t[...].T * HD ** (-0.5)
    outs[0][...] = (grad_query * cos[...] + swap_lanes(grad_query * sin[...])).astype(jnp.bfloat16)
    grad_keys = grad_key[...]
    outs[1][...] = (grad_keys * cos[...] + swap_lanes(grad_keys * sin[...])).astype(jnp.bfloat16)
    outs[2][...] = grad_value[...].astype(jnp.bfloat16)


def attend_back_kernel(
    query_rows, key_rows, value_rows, mixed_rows, grad_mixed, logs, cos, sin, mask, grad_q, grad_k, grad_v, *scratch
):
    attend_back_pair(
        query_rows, key_rows, value_rows, mixed_rows, grad_mixed, logs, cos, sin, mask, (grad_q, grad_k, grad_v), *scratch
    )


def attend_back(query_rows, key_rows, value_rows, mixed_rows, grad_mixed, logs, cosine, sine, mask):
    rows, width = query_rows.shape
    pairs = width // LANES
    wide_block = pl.BlockSpec((rows, LANES), lambda pair: (0, pair))
    table = pl.BlockSpec((rows, LANES), lambda pair: (0, 0))
    low = jax.ShapeDtypeStruct((rows, width), jnp.bfloat16)
    return pl.pallas_call(
        attend_back_kernel,
        grid=(pairs,),
        in_specs=[wide_block] * 5
        + [pl.BlockSpec((1, 2, rows), lambda pair: (pair, 0, 0)), table, table, pl.BlockSpec((rows, 2), lambda pair: (0, 0))],
        out_specs=[wide_block] * 3,
        out_shape=[low] * 3,
        scratch_shapes=[
            pltpu.VMEM((LANES, rows), jnp.float32),
            pltpu.VMEM((rows, LANES), jnp.float32),
            pltpu.VMEM((rows, LANES), jnp.float32),
            pltpu.VMEM((LANES, rows), jnp.float32),
        ],
        compiler_params=pltpu.CompilerParams(vmem_limit_bytes=32 * 1024 * 1024),
        cost_estimate=pl.CostEstimate(
            flops=10 * rows * rows * width, bytes_accessed=16 * rows * width, transcendentals=rows * rows * width // HD
        ),
    )(query_rows, key_rows, value_rows, mixed_rows, grad_mixed, logs, cosine, sine, mask)


NAMES = ("down", "gate", "up", "out", "query", "key", "value")
CHUNK = {"down": 128, "gate": 64, "up": 64, "out": 128, "query": 128, "key": 128, "value": 128}
SLOW = ("down", "gate")


def partner(values):
    return lax.ppermute(values, "narrow", [(0, 1), (1, 0)])


def rows_of(own, other):
    return jnp.concatenate([own, other], axis=0)


def rotary_pair_tables(position):
    lane = jnp.arange(LANES) % HD
    half_dim = HD // 2
    frequency = ROPE_BASE ** (-2.0 * (lane % half_dim).astype(jnp.float32) / HD)
    angles = position[:, None] * frequency[None, :]
    signs = jnp.where(lane < half_dim, -1.0, 1.0).astype(jnp.float32)
    return (jnp.cos(angles), jnp.sin(angles) * signs)


def on_device(
    tokens,
    window_span,
    valid_len,
    norm1_gain,
    norm1_shift,
    w_query,
    w_key,
    w_value,
    w_out,
    norm2_gain,
    norm2_shift,
    w_gate,
    w_up,
    w_down,
    cotangent,
):
    block_rows = tokens.shape[0]
    own_block = lax.axis_index("narrow")
    joined = window_span[0] == 2
    block_ids = jnp.stack([own_block, 1 - own_block])
    lengths = valid_len[block_ids]
    offsets = jnp.arange(2 * block_rows)
    row_block = offsets // block_rows
    position = offsets % block_rows + block_rows * jnp.repeat(block_ids, block_rows) * joined.astype(jnp.int32)
    cosine, sine = rotary_pair_tables(position.astype(jnp.float32))
    within = offsets % block_rows < jnp.repeat(lengths, block_rows)
    seen = within[:, None] & (joined | (row_block[:, None] == jnp.arange(2)[None, :]))
    mask = jnp.where(seen, 0.0, MASKED).astype(jnp.float32)

    token_values = tokens.astype(jnp.float32)
    normed_one, scaled_one, inverse_one = norm_forward(token_values, norm1_gain, norm1_shift)
    normed_one = normed_one.astype(jnp.bfloat16)
    gathered_one = rows_of(normed_one, partner(normed_one))
    cot_rows = rows_of(cotangent, partner(cotangent))
    projected = [
        jnp.dot(gathered_one, weight, preferred_element_type=jnp.float32)
        for weight in (w_query, w_key, w_value)
    ]
    query_rows, key_rows, value_rows, mixed_rows, logs = attend(*projected, cosine, sine, mask)
    other_share = jnp.dot(mixed_rows[block_rows:], w_out, preferred_element_type=jnp.float32)
    resid_values = (
        token_values
        + jnp.dot(mixed_rows[:block_rows], w_out, preferred_element_type=jnp.float32)
        + partner(other_share)
    )
    normed_two, scaled_two, inverse_two = norm_forward(resid_values, norm2_gain, norm2_shift)
    normed_two = normed_two.astype(jnp.bfloat16)
    gathered_two = rows_of(normed_two, partner(normed_two))
    gate_values = jnp.dot(gathered_two, w_gate, preferred_element_type=jnp.float32)
    up_values = jnp.dot(gathered_two, w_up, preferred_element_type=jnp.float32)
    sigmoid_gate = jax.nn.sigmoid(gate_values)
    hidden_rows = (gate_values * sigmoid_gate * up_values).astype(jnp.bfloat16)
    down_grad = transpose_times(hidden_rows, cot_rows).astype(jnp.bfloat16)

    out_other = jnp.dot(
        hidden_rows[block_rows:], w_down, preferred_element_type=jnp.float32
    ).astype(jnp.bfloat16)
    out_values = (
        resid_values
        + jnp.dot(hidden_rows[:block_rows], w_down, preferred_element_type=jnp.float32)
        + partner(out_other).astype(jnp.float32)
    )
    grad_hidden = times_transpose(cot_rows, w_down)
    silu_grad = sigmoid_gate * (1.0 + gate_values * (1.0 - sigmoid_gate))
    grad_gate = (grad_hidden * up_values * silu_grad).astype(jnp.bfloat16)
    grad_up = (grad_hidden * gate_values * sigmoid_gate).astype(jnp.bfloat16)
    gate_grad = transpose_times(gathered_two, grad_gate).astype(jnp.bfloat16)
    up_grad = transpose_times(gathered_two, grad_up).astype(jnp.bfloat16)

    def grad_two_share(rows):
        return times_transpose(grad_gate[rows], w_gate) + times_transpose(grad_up[rows], w_up)

    grad_two_other = grad_two_share(slice(block_rows, None))
    grad_normed_two = grad_two_share(slice(0, block_rows)) + partner(grad_two_other)
    grad_in_two, gain_two_grad, shift_two_grad = norm_backward(
        grad_normed_two, scaled_two, inverse_two, norm2_gain
    )
    grad_resid = cotangent.astype(jnp.float32) + grad_in_two
    grad_attention = grad_resid.astype(jnp.bfloat16)
    grad_rows = rows_of(grad_attention, partner(grad_attention))
    grad_mixed = times_transpose(grad_rows, w_out).astype(jnp.bfloat16)
    out_grad = transpose_times(mixed_rows, grad_rows).astype(jnp.bfloat16)
    grad_projected = attend_back(
        query_rows, key_rows, value_rows, mixed_rows, grad_mixed, logs, cosine, sine, mask
    )
    qkv_grads = [transpose_times(gathered_one, g).astype(jnp.bfloat16) for g in grad_projected]

    def grad_one_share(rows):
        return sum(
            times_transpose(g[rows], weight)
            for g, weight in zip(grad_projected, (w_query, w_key, w_value))
        )

    grad_one_other = grad_one_share(slice(block_rows, None)).astype(jnp.bfloat16)
    grad_normed_one = grad_one_share(slice(0, block_rows)) + partner(grad_one_other).astype(
        jnp.float32
    )
    grad_in_one, gain_one_grad, shift_one_grad = norm_backward(
        grad_normed_one, scaled_one, inverse_one, norm1_gain
    )
    token_grad = grad_resid + grad_in_one
    norm_grads = jnp.stack([gain_one_grad, shift_one_grad, gain_two_grad, shift_two_grad])
    gradients = dict(zip(NAMES, [down_grad, gate_grad, up_grad, out_grad] + qkv_grads))
    fast = [name for name in NAMES if name not in SLOW]
    *fast_sums, norm_summed = summed_over_wide(
        [gradients[n] for n in fast], [CHUNK[n] for n in fast], jnp.pad(norm_grads, ((0, 4), (0, 0))), 1
    )
    sums = dict(zip(fast, fast_sums))
    for name in SLOW:
        sums[name] = lax.psum(gradients[name], "wide")
    down_summed, gate_summed, up_summed, out_summed, query_summed, key_summed, value_summed = [
        sums[name].astype(jnp.float32) for name in NAMES
    ]
    return (
        out_values,
        token_grad,
        norm_summed[0],
        norm_summed[1],
        query_summed,
        key_summed,
        value_summed,
        out_summed,
        norm_summed[2],
        norm_summed[3],
        gate_summed,
        up_summed,
        down_summed,
    )


def solution(mesh):
    fits = mesh.shape["wide"] == PLANES * 4 and mesh.shape["narrow"] == 2
    in_specs = (
        P(("wide", "narrow"), None),
        P("wide"),
        P("wide"),
        P(),
        P(),
        P(None, "narrow"),
        P(None, "narrow"),
        P(None, "narrow"),
        P("narrow", None),
        P(),
        P(),
        P(None, "narrow"),
        P(None, "narrow"),
        P("narrow", None),
        P(("wide", "narrow"), None),
    )
    out_specs = (
        P(("wide", "narrow"), None),
        P(("wide", "narrow"), None),
        P(),
        P(),
        P(None, "narrow"),
        P(None, "narrow"),
        P(None, "narrow"),
        P("narrow", None),
        P(),
        P(),
        P(None, "narrow"),
        P(None, "narrow"),
        P("narrow", None),
    )
    return jax.shard_map(
        on_device if fits else on_device_any_mesh, mesh=mesh, in_specs=in_specs, out_specs=out_specs, check_vma=False
    )
```

```python
import functools

import jax
import jax.numpy as jnp
from jax import lax
from jax.experimental import pallas as pl
from jax.experimental.pallas import tpu as pltpu
from jax.sharding import PartitionSpec as P

MESH = pl.DeviceIdType.MESH

HD = 64


EPSILON = 1e-05
MASKED = -1e30
ROPE_BASE = 10000.0


def times_transpose(left, right):
    return lax.dot_general(
        left, right, (((1,), (1,)), ((), ())), preferred_element_type=jnp.float32
    )


def transpose_times(left, right):
    return lax.dot_general(
        left, right, (((0,), (0,)), ((), ())), preferred_element_type=jnp.float32
    )


def norm_forward(values, norm_gain, norm_shift):
    average = jnp.mean(values, axis=-1, keepdims=True)
    centred = values - average
    inverse = lax.rsqrt(jnp.mean(centred * centred, axis=-1, keepdims=True) + EPSILON)
    scaled = centred * inverse
    return (scaled * norm_gain + norm_shift, scaled, inverse)


def norm_backward(grad_out, scaled, inverse, norm_gain):
    grad_scaled = grad_out * norm_gain
    first_term = jnp.mean(grad_scaled, axis=-1, keepdims=True)
    second_term = jnp.mean(grad_scaled * scaled, axis=-1, keepdims=True)
    grad_in = inverse * (grad_scaled - first_term - scaled * second_term)
    return (grad_in, jnp.sum(grad_out * scaled, axis=0), jnp.sum(grad_out, axis=0))


def rotary_tables(span_table, block_rows, width):
    row_count = span_table.shape[0] * block_rows
    row_ids = jnp.arange(row_count)
    block_ids = row_ids // block_rows
    span_rows = jnp.repeat(span_table, block_rows)
    position = (row_ids % block_rows + block_rows * (block_ids % 2) * (span_rows == 2)).astype(
        jnp.float32
    )
    columns = jnp.arange(width) % HD
    half_dim = HD // 2
    freq_index = (columns % half_dim).astype(jnp.float32)
    frequency = ROPE_BASE ** (-2.0 * freq_index / HD)
    angles = position[:, None] * frequency[None, :]
    signs = jnp.where(columns < half_dim, -1.0, 1.0).astype(jnp.float32)
    return (jnp.cos(angles), jnp.sin(angles) * signs)


def swap_halves(values):
    row_count = values.shape[0]
    width = values.shape[1]
    parts = values.reshape(row_count, width // HD, 2, HD // 2)
    return jnp.flip(parts, axis=2).reshape(row_count, width)


def rotate(values, cosine, sine_signed):
    return values * cosine + swap_halves(values) * sine_signed


def rotate_back(grads_in, cosine, sine_signed):
    return grads_in * cosine + swap_halves(grads_in * sine_signed)


def pair_mask(block_index, span_table, valid_table, block_rows):
    pair_first = block_index // 2 * 2
    offsets = jnp.arange(2 * block_rows)
    key_block = pair_first + offsets // block_rows
    within = offsets % block_rows
    first_len = lax.dynamic_index_in_dim(valid_table, pair_first, keepdims=False)
    second_len = lax.dynamic_index_in_dim(valid_table, pair_first + 1, keepdims=False)
    own_span = lax.dynamic_index_in_dim(span_table, block_index, keepdims=False)
    length_bound = jnp.where(offsets < block_rows, first_len, second_len)
    return (within < length_bound) & ((own_span == 2) | (key_block == block_index))


def on_device_any_mesh(
    tokens,
    window_span,
    valid_len,
    norm1_gain,
    norm1_shift,
    w_query,
    w_key,
    w_value,
    w_out,
    norm2_gain,
    norm2_shift,
    w_gate,
    w_up,
    w_down,
    cotangent,
):
    local_rows = tokens.shape[0]
    group_rows = local_rows * lax.axis_size("narrow")
    block_count = window_span.shape[0]
    block_rows = group_rows // block_count
    local_width = w_query.shape[1]
    local_heads = local_width // HD
    local_hidden = w_gate.shape[1]
    softmax_scale = HD ** (-0.5)
    token_values = tokens.astype(jnp.float32)
    normed_one, scaled_one, inverse_one = norm_forward(token_values, norm1_gain, norm1_shift)
    normed_one = normed_one.astype(jnp.bfloat16)
    gathered_one = lax.all_gather(normed_one, "narrow", axis=0, tiled=True)
    joined_qkv = jnp.concatenate([w_query, w_key, w_value], axis=1)
    projected = jnp.dot(gathered_one, joined_qkv, preferred_element_type=jnp.float32)
    cosine, sine_signed = rotary_tables(window_span, block_rows, local_width)
    query_rows = (rotate(projected[:, :local_width], cosine, sine_signed) * softmax_scale).astype(
        jnp.bfloat16
    )
    key_rows = rotate(projected[:, local_width : 2 * local_width], cosine, sine_signed).astype(
        jnp.bfloat16
    )
    value_rows = projected[:, 2 * local_width :].astype(jnp.bfloat16)

    def block_slices(block_index):
        query_block = lax.dynamic_slice_in_dim(query_rows, block_index * block_rows, block_rows, 0)
        pair_start = block_index // 2 * 2 * block_rows
        return (
            query_block.reshape(block_rows, local_heads, HD),
            key_rows.reshape(2 * block_rows, local_heads, HD),
            value_rows.reshape(2 * block_rows, local_heads, HD),
            pair_start,
        )

    def masked_scores(block_index, query_block, key_pair):
        scores = jnp.einsum(
            "qhd,khd->hqk", query_block, key_pair, preferred_element_type=jnp.float32
        )
        key_mask = pair_mask(block_index, window_span, valid_len, block_rows)
        return jnp.where(key_mask[None, None, :], scores, MASKED)

    def attend_forward(block_index):
        query_block, key_pair, value_pair, pair_start = block_slices(block_index)
        scores = masked_scores(block_index, query_block, key_pair)
        highest = jnp.max(scores, axis=-1, keepdims=True)
        weights = jnp.exp(scores - highest)
        weight_total = jnp.sum(weights, axis=-1, keepdims=True)
        attention_probs = (weights / weight_total).astype(jnp.bfloat16)
        mixed_block = jnp.einsum(
            "hqk,khd->qhd", attention_probs, value_pair, preferred_element_type=jnp.float32
        )
        return (
            mixed_block.reshape(block_rows, local_width).astype(jnp.bfloat16),
            (highest + jnp.log(weight_total))[:, :, 0],
        )

    mixed_blocks, log_totals = lax.map(attend_forward, jnp.arange(block_count))
    mixed_rows = mixed_blocks.reshape(group_rows, local_width)
    resid_values = token_values + lax.psum_scatter(
        jnp.dot(mixed_rows, w_out, preferred_element_type=jnp.float32),
        "narrow",
        scatter_dimension=0,
        tiled=True,
    )
    normed_two, scaled_two, inverse_two = norm_forward(resid_values, norm2_gain, norm2_shift)
    normed_two = normed_two.astype(jnp.bfloat16)
    gathered_two = lax.all_gather(normed_two, "narrow", axis=0, tiled=True)
    joined_gate_up = jnp.concatenate([w_gate, w_up], axis=1)
    gate_up = jnp.dot(gathered_two, joined_gate_up, preferred_element_type=jnp.float32)
    gate_values = gate_up[:, :local_hidden]
    up_values = gate_up[:, local_hidden:]
    sigmoid_gate = jax.nn.sigmoid(gate_values)
    hidden_rows = (gate_values * sigmoid_gate * up_values).astype(jnp.bfloat16)
    out_values = resid_values + lax.psum_scatter(
        jnp.dot(hidden_rows, w_down, preferred_element_type=jnp.float32).astype(jnp.bfloat16),
        "narrow",
        scatter_dimension=0,
        tiled=True,
    ).astype(jnp.float32)
    shard_rows = lax.all_gather(cotangent, "narrow", axis=0, tiled=True)
    grad_hidden = times_transpose(shard_rows, w_down)
    grad_down_w, grad_hidden = (transpose_times(hidden_rows, shard_rows), grad_hidden)
    silu_grad = sigmoid_gate * (1.0 + gate_values * (1.0 - sigmoid_gate))
    grad_gate_up = jnp.concatenate(
        [grad_hidden * up_values * silu_grad, grad_hidden * gate_values * sigmoid_gate], axis=1
    ).astype(jnp.bfloat16)
    grad_normed_two = lax.psum_scatter(
        times_transpose(grad_gate_up, joined_gate_up), "narrow", scatter_dimension=0, tiled=True
    )
    grad_gate_up_w = transpose_times(gathered_two, grad_gate_up)
    grad_in_two, gain_two_grad, shift_two_grad = norm_backward(
        grad_normed_two, scaled_two, inverse_two, norm2_gain
    )
    grad_resid = cotangent.astype(jnp.float32) + grad_in_two
    shard_rows = lax.all_gather(grad_resid.astype(jnp.bfloat16), "narrow", axis=0, tiled=True)
    grad_mixed_sum = times_transpose(shard_rows, w_out)
    grad_out_w, grad_mixed_sum = (transpose_times(mixed_rows, shard_rows), grad_mixed_sum)
    grad_mixed = grad_mixed_sum.astype(jnp.bfloat16)

    def attend_backward(block_index, running):
        grad_query, grad_key, grad_value = running
        query_block, key_pair, value_pair, pair_start = block_slices(block_index)
        grad_rows = lax.dynamic_slice_in_dim(
            grad_mixed, block_index * block_rows, block_rows, 0
        ).reshape(block_rows, local_heads, HD)
        scores = masked_scores(block_index, query_block, key_pair)
        log_total = lax.dynamic_index_in_dim(log_totals, block_index, keepdims=False)
        attention_probs = jnp.exp(scores - log_total[:, :, None])
        grad_probs = jnp.einsum(
            "qhd,khd->hqk", grad_rows, value_pair, preferred_element_type=jnp.float32
        )
        centre = jnp.sum(attention_probs * grad_probs, axis=-1, keepdims=True)
        grad_scores = (attention_probs * (grad_probs - centre)).astype(jnp.bfloat16)
        block_query = jnp.einsum(
            "hqk,khd->qhd", grad_scores, key_pair, preferred_element_type=jnp.float32
        ).reshape(block_rows, local_width)
        pair_key = jnp.einsum(
            "hqk,qhd->khd", grad_scores, query_block, preferred_element_type=jnp.float32
        ).reshape(2 * block_rows, local_width)
        pair_value = jnp.einsum(
            "hqk,qhd->khd",
            attention_probs.astype(jnp.bfloat16),
            grad_rows,
            preferred_element_type=jnp.float32,
        ).reshape(2 * block_rows, local_width)
        grad_query = lax.dynamic_update_slice_in_dim(
            grad_query, block_query, block_index * block_rows, 0
        )
        grad_key = grad_key + pair_key
        grad_value = grad_value + pair_value
        return (grad_query, grad_key, grad_value)

    zero_rows = jnp.zeros((group_rows, local_width), jnp.float32)
    grad_query, grad_key, grad_value = lax.fori_loop(
        0, block_count, attend_backward, (zero_rows, zero_rows, zero_rows)
    )
    grad_query_raw = rotate_back(grad_query * softmax_scale, cosine, sine_signed)
    grad_key_raw = rotate_back(grad_key, cosine, sine_signed)
    grad_qkv = jnp.concatenate([grad_query_raw, grad_key_raw, grad_value], axis=1).astype(
        jnp.bfloat16
    )
    grad_normed_one = lax.psum_scatter(
        times_transpose(grad_qkv, joined_qkv).astype(jnp.bfloat16),
        "narrow",
        scatter_dimension=0,
        tiled=True,
    ).astype(jnp.float32)
    grad_qkv_w = transpose_times(gathered_one, grad_qkv)
    grad_in_one, gain_one_grad, shift_one_grad = norm_backward(
        grad_normed_one, scaled_one, inverse_one, norm1_gain
    )
    token_grad = grad_resid + grad_in_one
    qkv_summed, out_summed, gate_up_summed, down_summed = (
        lax.psum(grad_qkv_w.astype(jnp.bfloat16), "wide").astype(jnp.float32),
        lax.psum(grad_out_w.astype(jnp.bfloat16), "wide").astype(jnp.float32),
        lax.psum(grad_gate_up_w.astype(jnp.bfloat16), "wide").astype(jnp.float32),
        lax.psum(grad_down_w.astype(jnp.bfloat16), "wide").astype(jnp.float32),
    )
    norm_summed = lax.psum(
        (gain_one_grad, shift_one_grad, gain_two_grad, shift_two_grad), ("wide", "narrow")
    )
    return (
        out_values,
        token_grad,
        norm_summed[0],
        norm_summed[1],
        qkv_summed[:, :local_width],
        qkv_summed[:, local_width : 2 * local_width],
        qkv_summed[:, 2 * local_width :],
        out_summed,
        norm_summed[2],
        norm_summed[3],
        gate_up_summed[:, :local_hidden],
        gate_up_summed[:, local_hidden:],
        down_summed,
    )


PLANES = 4


class Job:
    def __init__(self, rows, cols, chunk_rows):
        self.rows, self.cols, self.chunk_rows = rows, cols, chunk_rows
        self.count = rows // (2 * chunk_rows)


def scratch_for(job):
    half, quarter = job.chunk_rows // 2, job.chunk_rows // 4

    def slots(rows):
        return pltpu.VMEM((job.count, 2, rows, job.cols), jnp.bfloat16)

    return [
        pltpu.VMEM((job.rows, job.cols), jnp.bfloat16),
        slots(half),
        slots(half),
        slots(quarter),
        slots(quarter),
        slots(quarter),
        slots(half),
        pltpu.SemaphoreType.DMA((job.count, 2, 9)),
        pltpu.SemaphoreType.DMA((job.count, 2, 9)),
        pltpu.SemaphoreType.DMA((job.count,)),
        pltpu.SemaphoreType.DMA((job.count, 2, 3)),
    ]


OUTER, INWARD, ACROSS, CROSS, BACK, OUT_A, OUT_B, GATHER_A, GATHER_B = range(9)


class Links:
    def __init__(self):
        position = lax.axis_index("wide")
        self.x = lax.rem(position, 2)
        self.y = lax.rem(position // 2, 2)
        self.z = position // 4
        self.middle = jnp.logical_and(self.z >= 1, self.z <= 2)
        self.edge = jnp.logical_or(self.z == 0, self.z == PLANES - 1)
        self.upper = self.z // 2
        self.across = self.at(self.x, self.y, 3 - self.z)
        step = 1 - 2 * self.upper
        self.inward = self.at(self.x, self.y, lax.rem(self.z + step + PLANES, PLANES))
        self.outward = self.at(self.x, self.y, lax.rem(self.z - step + PLANES, PLANES))
        self.flips = [self.at(1 - self.x, self.y, self.z), self.at(self.x, 1 - self.y, self.z)]
        self.bits = [self.x, self.y]

    def at(self, x, y, z):
        return z * 4 + y * 2 + x

    def greet(self):
        barrier = pltpu.get_barrier_semaphore()

        def signal(target):
            pl.semaphore_signal(barrier, inc=1, device_id={"wide": target}, device_id_type=MESH)

        pl.semaphore_signal(
            barrier, inc=1, device_id={"narrow": 1 - lax.axis_index("narrow")}, device_id_type=MESH
        )
        for target in self.flips:
            signal(target)

        @pl.when(self.edge)
        def _():
            signal(self.inward)
            pl.semaphore_wait(barrier, 4)

        @pl.when(self.middle)
        def _():
            signal(self.across)
            signal(self.outward)
            pl.semaphore_wait(barrier, 5)


ADD_ROWS = 16


def add_rows(held, start, other, rows):
    def add(index, carry):
        own = pl.ds(pl.multiple_of(start + index * ADD_ROWS, ADD_ROWS), ADD_ROWS)
        arrived = other[pl.ds(pl.multiple_of(index * ADD_ROWS, ADD_ROWS), ADD_ROWS), :]
        held[own, :] = (held[own, :].astype(jnp.float32) + arrived.astype(jnp.float32)).astype(jnp.bfloat16)
        return carry

    lax.fori_loop(0, rows // ADD_ROWS, add, 0)


class Vectors:
    STEPS = 7

    def __init__(self, links, source, output, stages, arrived, sent, got):
        self.links, self.source, self.output = links, source, output
        self.stages, self.arrived, self.sent, self.got = stages, arrived, sent, got

    def copy(self, number, source, target):
        return pltpu.make_async_remote_copy(
            src_ref=source,
            dst_ref=self.arrived.at[number],
            send_sem=self.sent.at[number],
            recv_sem=self.got.at[number],
            device_id=target,
            device_id_type=MESH,
        )

    def exchange(self, number):
        links = self.links
        targets = [
            {"narrow": 1 - lax.axis_index("narrow")},
            {"wide": links.flips[0]},
            {"wide": links.flips[1]},
            {"wide": links.inward},
            {"wide": links.across},
            {"wide": links.outward},
        ]
        source = self.source if number == 0 else self.stages.at[number]
        return self.copy(number, source, targets[number])

    def add(self, number):
        source = self.source if number == 0 else self.stages.at[number]
        self.stages[number + 1] = source[...] + self.arrived[number]

    def step(self, number):
        links = self.links
        if number in (1, 2, 3):
            self.exchange(number - 1).wait_recv()
            self.add(number - 1)
        if number < 3:
            self.exchange(number).start()
        if number == 3:

            @pl.when(links.edge)
            def _():
                self.exchange(3).start()

        if number in (4, 5):

            @pl.when(links.middle)
            def _():
                self.exchange(number - 1).wait_recv()
                self.add(number - 1)
                self.exchange(number).start()

        if number == 6:

            @pl.when(links.middle)
            def _():
                self.output[...] = self.stages[5]

            @pl.when(links.edge)
            def _():
                self.exchange(5).wait_recv()
                self.output[...] = self.arrived[5]

    def close(self):
        for number in range(3):
            self.exchange(number).wait_send()

        @pl.when(self.links.edge)
        def _():
            self.exchange(3).wait_send()

        @pl.when(self.links.middle)
        def _():
            self.exchange(4).wait_send()
            self.exchange(5).wait_send()


class Chunk:
    STEPS = 8

    def __init__(self, links, job, refs, output, index, colour):
        self.links, self.colour, self.index, self.output = links, colour, index, output
        self.held = refs[0]
        self.pair_in, self.column_in, self.across_in, self.cross_in, self.back_in, self.gather_in = [
            ref.at[index, colour] for ref in refs[1:7]
        ]
        self.sent, self.got, self.loaded, self.stored = refs[7:11]
        self.half, self.quarter = job.chunk_rows // 2, job.chunk_rows // 4
        self.base = (2 * index + colour) * job.chunk_rows
        bit = links.bits[colour]
        self.keep = pl.multiple_of(self.base + bit * self.half, self.quarter)
        self.away = pl.multiple_of(self.base + (1 - bit) * self.half, self.quarter)
        self.near = pl.multiple_of(links.upper * self.quarter, self.quarter)
        self.far = pl.multiple_of((1 - links.upper) * self.quarter, self.quarter)
        self.kept = pl.multiple_of(self.keep + self.near, self.quarter)
        self.given = pl.multiple_of(self.keep + self.far, self.quarter)
        self.outer_peer = links.flips[colour]
        self.inner_peer = links.flips[1 - colour]

    def rows(self, start, size):
        return self.held.at[pl.ds(start, size), :]

    def part(self, ref, start):
        return ref.at[pl.ds(start, self.quarter), :]

    def copy(self, step, source, target, peer):
        return pltpu.make_async_remote_copy(
            src_ref=source,
            dst_ref=target,
            send_sem=self.sent.at[self.index, self.colour, step],
            recv_sem=self.got.at[self.index, self.colour, step],
            device_id={"wide": peer},
            device_id_type=MESH,
        )

    def outer(self):
        return self.copy(OUTER, self.rows(self.away, self.half), self.pair_in, self.outer_peer)

    def inward(self):
        return self.copy(INWARD, self.rows(self.keep, self.half), self.column_in, self.links.inward)

    def across(self):
        return self.copy(ACROSS, self.rows(self.given, self.quarter), self.across_in, self.links.across)

    def cross(self):
        return self.copy(CROSS, self.rows(self.kept, self.quarter), self.cross_in, self.inner_peer)

    def back(self):
        return self.copy(BACK, self.rows(self.kept, self.quarter), self.back_in, self.links.across)

    def out_a(self):
        target = self.part(self.column_in, self.near)
        return self.copy(OUT_A, self.rows(self.kept, self.quarter), target, self.links.outward)

    def out_b(self):
        return self.copy(OUT_B, self.back_in, self.part(self.column_in, self.far), self.links.outward)

    def gather_a(self, source):
        return self.copy(GATHER_A, source, self.part(self.gather_in, self.near), self.outer_peer)

    def gather_b(self, source):
        return self.copy(GATHER_B, source, self.part(self.gather_in, self.far), self.outer_peer)

    def store(self, place, source, start, size):
        target = self.output.at[pl.ds(start, size), :]
        return pltpu.make_async_copy(source, target, self.stored.at[self.index, self.colour, place])

    def totals(self, near, far):
        return self.store(0, near, self.kept, self.quarter), self.store(1, far, self.given, self.quarter)

    def partner_total(self):
        return self.store(2, self.gather_in, self.away, self.half)

    def step(self, number):
        links = self.links
        near_total = self.rows(self.kept, self.quarter)
        edge_near, edge_far = self.part(self.column_in, self.near), self.part(self.column_in, self.far)
        if number == 0:
            self.outer().start()
        if number == 1:
            self.outer().wait_recv()
            add_rows(self.held, self.keep, self.pair_in, self.half)

            @pl.when(links.edge)
            def _():
                self.inward().start()

        if number == 2:

            @pl.when(links.middle)
            def _():
                self.inward().wait_recv()
                add_rows(self.held, self.keep, self.column_in, self.half)
                self.across().start()

        if number == 3:

            @pl.when(links.middle)
            def _():
                self.across().wait_recv()
                add_rows(self.held, self.kept, self.across_in, self.quarter)
                self.cross().start()

        if number == 4:

            @pl.when(links.middle)
            def _():
                self.cross().wait()
                add_rows(self.held, self.kept, self.cross_in, self.quarter)
                self.back().start()
                self.out_a().start()
                self.gather_a(near_total).start()

        if number == 5:

            @pl.when(links.middle)
            def _():
                self.back().wait_recv()
                self.out_b().start()
                self.gather_b(self.back_in).start()
                for store in self.totals(near_total, self.back_in):
                    store.start()

            @pl.when(links.edge)
            def _():
                self.out_a().wait_recv()
                self.gather_a(edge_near).start()

        if number == 6:

            @pl.when(links.edge)
            def _():
                self.out_b().wait_recv()
                self.gather_b(edge_far).start()
                for store in self.totals(edge_near, edge_far):
                    store.start()

        if number == 7:
            self.gather_a(near_total).wait_recv()
            self.gather_b(self.back_in).wait_recv()
            self.partner_total().start()

    def close(self):
        near_total = self.rows(self.kept, self.quarter)
        self.outer().wait_send()
        self.gather_a(near_total).wait_send()
        self.gather_b(self.back_in).wait_send()

        @pl.when(self.links.middle)
        def _():
            self.across().wait_send()
            self.back().wait_send()
            self.out_a().wait_send()
            self.out_b().wait_send()

        @pl.when(self.links.edge)
        def _():
            self.inward().wait_send()

        for store in self.totals(near_total, self.back_in):
            store.wait()
        self.partner_total().wait()


def sum_kernel(jobs, *refs):
    count = len(jobs)
    inputs, refs = refs[: count + 1], refs[count + 1 :]
    outputs, scratch = refs[: count + 1], refs[count + 1 :]
    scratch, vector_scratch = scratch[:-4], scratch[-4:]
    per_job = len(scratch) // count
    links = Links()
    vectors = Vectors(links, inputs[count], outputs[count], *vector_scratch)
    items = []
    for number, job in enumerate(jobs):
        own = scratch[number * per_job : (number + 1) * per_job]
        for index in range(job.count):
            pair = [Chunk(links, job, own, outputs[number], index, colour) for colour in range(2)]
            span = pl.ds(2 * index * job.chunk_rows, 2 * job.chunk_rows)
            load = pltpu.make_async_copy(inputs[number].at[span, :], own[0].at[span, :], own[9].at[index])
            load.start()
            items.append((pair, load))
    links.greet()
    for tick in range(len(items) + Chunk.STEPS - 1):
        if tick < Vectors.STEPS:
            vectors.step(tick)
        for place, (pair, load) in enumerate(items):
            step = tick - place
            if 0 <= step < Chunk.STEPS:
                if step == 0:
                    load.wait()
                for chunk in pair:
                    chunk.step(step)
    for pair, _ in items:
        for chunk in pair:
            chunk.close()
    vectors.close()


def summed_over_wide(gradients, chunk_rows, vectors, collective_id):
    jobs = [Job(g.shape[0], g.shape[1], r) for g, r in zip(gradients, chunk_rows)]
    scratch = []
    for job in jobs:
        scratch += scratch_for(job)
    scratch += [
        pltpu.VMEM((6, *vectors.shape), jnp.float32),
        pltpu.VMEM((6, *vectors.shape), jnp.float32),
        pltpu.SemaphoreType.DMA((6,)),
        pltpu.SemaphoreType.DMA((6,)),
    ]
    sent = sum(2 * g.size * 5 // 4 for g in gradients)
    return pl.pallas_call(
        functools.partial(sum_kernel, jobs),
        out_shape=[jax.ShapeDtypeStruct(g.shape, jnp.bfloat16) for g in gradients]
        + [jax.ShapeDtypeStruct(vectors.shape, jnp.float32)],
        in_specs=[pl.BlockSpec(memory_space=pl.ANY)] * len(jobs) + [pl.BlockSpec(memory_space=pltpu.VMEM)],
        out_specs=[pl.BlockSpec(memory_space=pl.ANY)] * len(jobs) + [pl.BlockSpec(memory_space=pltpu.VMEM)],
        scratch_shapes=scratch,
        compiler_params=pltpu.CompilerParams(
            collective_id=collective_id, has_side_effects=True, vmem_limit_bytes=60 * 1024 * 1024
        ),
        cost_estimate=pl.CostEstimate(flops=0, bytes_accessed=2 * sent, transcendentals=0),
    )(*gradients, vectors)


LANES = 128
QUERY_TILE = 512
BACK_TILE = 256


def nt_dot(left, right):
    return lax.dot_general(
        left, right, (((1,), (1,)), ((), ())), preferred_element_type=jnp.float32
    )


def nn_dot(left, right):
    return jnp.dot(left, right, preferred_element_type=jnp.float32)


def swap_lanes(values):
    lane = lax.broadcasted_iota(jnp.int32, values.shape, 1)
    half_dim = HD // 2
    ahead = pltpu.roll(values, LANES - half_dim, axis=1)
    behind = pltpu.roll(values, half_dim, axis=1)
    return jnp.where(lane % HD < half_dim, ahead, behind)


def head_lanes(rows, head):
    return lax.broadcasted_iota(jnp.int32, (rows, LANES), 1) // HD == head


def masked_keys(keys, mask, head):
    lane = lax.broadcasted_iota(jnp.int32, keys.shape, 1)
    spare = (1 - head) * HD
    keys = jnp.where(lane // HD == head, keys, jnp.zeros_like(keys))
    for block in range(2):
        keys = jnp.where(lane == spare + block, mask[:, block : block + 1], keys)
    return keys


def head_queries(queries, head, block):
    lane = lax.broadcasted_iota(jnp.int32, queries.shape, 1)
    spare = (1 - head) * HD
    queries = jnp.where(lane // HD == head, queries, jnp.zeros_like(queries))
    return jnp.where(lane == spare + block, jnp.ones_like(queries), queries)


def attend_kernel(
    query_raw, key_raw, value_raw, cosine, sine, mask, query_out, key_out, value_out, mixed_out, log_out, mixed_t
):
    rows = query_raw.shape[0]
    block_rows = rows // 2
    cos, sin = cosine[...], sine[...]
    queries = query_raw[...]
    query_out[...] = ((queries * cos + swap_lanes(queries) * sin) * HD ** (-0.5)).astype(jnp.bfloat16)
    keys = key_raw[...]
    key_out[...] = (keys * cos + swap_lanes(keys) * sin).astype(jnp.bfloat16)
    value_out[...] = value_raw[...].astype(jnp.bfloat16)
    values_t = value_out[...].T
    mask_low = mask[...].astype(jnp.bfloat16)
    keys_of = [masked_keys(key_out[...], mask_low, head) for head in range(2)]

    def tile(index, carry):
        span = pl.ds(pl.multiple_of(index * QUERY_TILE, QUERY_TILE), QUERY_TILE)
        block = index * QUERY_TILE // block_rows
        for head in range(2):
            scores = nt_dot(keys_of[head], head_queries(query_out[span, :], head, block))
            highest = jnp.max(scores, axis=0, keepdims=True)
            weights = jnp.exp(scores - highest)
            total = jnp.sum(weights, axis=0, keepdims=True)
            mixed = nn_dot(values_t[head * HD : (head + 1) * HD], weights.astype(jnp.bfloat16)) / total
            mixed_t[pl.ds(head * HD, HD), span] = mixed
            log_out[0, pl.ds(head, 1), span] = highest + jnp.log(total)
        return carry

    lax.fori_loop(0, rows // QUERY_TILE, tile, 0, unroll=True)
    mixed_out[...] = mixed_t[...].T.astype(jnp.bfloat16)


def attend(query_raw, key_raw, value_raw, cosine, sine, mask):
    rows, width = query_raw.shape
    pairs = width // LANES
    wide_block = pl.BlockSpec((rows, LANES), lambda pair: (0, pair))
    table = pl.BlockSpec((rows, LANES), lambda pair: (0, 0))
    low = jax.ShapeDtypeStruct((rows, width), jnp.bfloat16)
    return pl.pallas_call(
        attend_kernel,
        grid=(pairs,),
        in_specs=[wide_block] * 3 + [table, table, pl.BlockSpec((rows, 2), lambda pair: (0, 0))],
        out_specs=[wide_block] * 4 + [pl.BlockSpec((1, 2, rows), lambda pair: (pair, 0, 0))],
        out_shape=[low] * 4 + [jax.ShapeDtypeStruct((pairs, 2, rows), jnp.float32)],
        scratch_shapes=[pltpu.VMEM((LANES, rows), jnp.float32)],
        compiler_params=pltpu.CompilerParams(vmem_limit_bytes=32 * 1024 * 1024),
        cost_estimate=pl.CostEstimate(
            flops=4 * rows * rows * width, bytes_accessed=20 * rows * width, transcendentals=rows * rows * width // HD
        ),
    )(query_raw, key_raw, value_raw, cosine, sine, mask)


def attend_back_pair(
    query_rows, key_rows, value_rows, mixed_rows, grad_mixed, logs, cos, sin, mask, outs, grad_query_t, grad_key, grad_value, grad_t
):
    rows = query_rows.shape[0]
    block_rows = rows // 2
    mask_low = mask[...].astype(jnp.bfloat16)
    keys_t = key_rows[...].T
    values = value_rows[...]
    grad_t[...] = (grad_mixed[...].astype(jnp.float32) * mixed_rows[...].astype(jnp.float32)).T
    grad_key[...] = jnp.zeros_like(grad_key)
    grad_value[...] = jnp.zeros_like(grad_value)
    keys_of = [masked_keys(key_rows[...], mask_low, head) for head in range(2)]

    def tile(index, carry):
        span = pl.ds(pl.multiple_of(index * BACK_TILE, BACK_TILE), BACK_TILE)
        block = index * BACK_TILE // block_rows
        for head in range(2):
            inside = head_lanes(BACK_TILE, head)
            queries = query_rows[span, :]
            grads = grad_mixed[span, :]
            grads = jnp.where(inside, grads, jnp.zeros_like(grads))
            centre = jnp.sum(grad_t[pl.ds(head * HD, HD), span], axis=0, keepdims=True)
            scores = nt_dot(keys_of[head], head_queries(queries, head, block))
            probs = jnp.exp(scores - logs[0, pl.ds(head, 1), span])
            grad_probs = nt_dot(values, grads)
            grad_scores = (probs * (grad_probs - centre)).astype(jnp.bfloat16)
            grad_value[...] += nn_dot(probs.astype(jnp.bfloat16), grads)
            grad_key[...] += nn_dot(grad_scores, jnp.where(inside, queries, jnp.zeros_like(queries)))
            grad_query_t[pl.ds(head * HD, HD), span] = nn_dot(keys_t[head * HD : (head + 1) * HD], grad_scores)
        return carry

    lax.fori_loop(0, rows // BACK_TILE, tile, 0, unroll=True)
    grad_query = grad_query_t[...].T * HD ** (-0.5)
    outs[0][...] = (grad_query * cos[...] + swap_lanes(grad_query * sin[...])).astype(jnp.bfloat16)
    grad_keys = grad_key[...]
    outs[1][...] = (grad_keys * cos[...] + swap_lanes(grad_keys * sin[...])).astype(jnp.bfloat16)
    outs[2][...] = grad_value[...].astype(jnp.bfloat16)


def attend_back_kernel(
    query_rows, key_rows, value_rows, mixed_rows, grad_mixed, logs, cos, sin, mask, grad_q, grad_k, grad_v, *scratch
):
    attend_back_pair(
        query_rows, key_rows, value_rows, mixed_rows, grad_mixed, logs, cos, sin, mask, (grad_q, grad_k, grad_v), *scratch
    )


def attend_back(query_rows, key_rows, value_rows, mixed_rows, grad_mixed, logs, cosine, sine, mask):
    rows, width = query_rows.shape
    pairs = width // LANES
    wide_block = pl.BlockSpec((rows, LANES), lambda pair: (0, pair))
    table = pl.BlockSpec((rows, LANES), lambda pair: (0, 0))
    low = jax.ShapeDtypeStruct((rows, width), jnp.bfloat16)
    return pl.pallas_call(
        attend_back_kernel,
        grid=(pairs,),
        in_specs=[wide_block] * 5
        + [pl.BlockSpec((1, 2, rows), lambda pair: (pair, 0, 0)), table, table, pl.BlockSpec((rows, 2), lambda pair: (0, 0))],
        out_specs=[wide_block] * 3,
        out_shape=[low] * 3,
        scratch_shapes=[
            pltpu.VMEM((LANES, rows), jnp.float32),
            pltpu.VMEM((rows, LANES), jnp.float32),
            pltpu.VMEM((rows, LANES), jnp.float32),
            pltpu.VMEM((LANES, rows), jnp.float32),
        ],
        compiler_params=pltpu.CompilerParams(vmem_limit_bytes=32 * 1024 * 1024),
        cost_estimate=pl.CostEstimate(
            flops=10 * rows * rows * width, bytes_accessed=16 * rows * width, transcendentals=rows * rows * width // HD
        ),
    )(query_rows, key_rows, value_rows, mixed_rows, grad_mixed, logs, cosine, sine, mask)


NAMES = ("down", "gate", "up", "out", "query", "key", "value")
CHUNK = {"down": 128, "gate": 64, "up": 64, "out": 128, "query": 128, "key": 128, "value": 128}
SLOW = ("down", "gate")


HIDDEN_TILE = 256


def feed_kernel(
    rows, cots, gate_w, up_w, down_w, out_own, out_other, back_own, back_other, down_grad, gate_grad, grad_up, rows_t, out_sum, back_sum
):
    step = pl.program_id(0)

    @pl.when(step == 0)
    def _():
        rows_t[...] = rows[...].T
        out_sum[...] = jnp.zeros_like(out_sum)
        back_sum[...] = jnp.zeros_like(back_sum)

    gate = nn_dot(rows[...], gate_w[...])
    sigmoid = 1.0 / (1.0 + jnp.exp(-gate))
    silu = gate * sigmoid
    up = nn_dot(rows[...], up_w[...])
    hidden = (silu * up).astype(jnp.bfloat16)
    grad_hidden = nt_dot(cots[...], down_w[...])
    gate_back = (grad_hidden * up * (sigmoid * (1.0 + gate * (1.0 - sigmoid)))).astype(jnp.bfloat16)
    up_back = (grad_hidden * silu).astype(jnp.bfloat16)
    grad_up[...] = up_back
    down_grad[...] = nn_dot(hidden.T, cots[...]).astype(jnp.bfloat16)
    gate_grad[...] = nn_dot(rows_t[...], gate_back).astype(jnp.bfloat16)
    out_sum[...] += nn_dot(hidden, down_w[...])
    back_sum[...] += nt_dot(gate_back, gate_w[...]) + nt_dot(up_back, up_w[...])

    @pl.when(step == pl.num_programs(0) - 1)
    def _():
        half = rows.shape[0] // 2
        out_own[...] = out_sum[:half]
        out_other[...] = out_sum[half:].astype(jnp.bfloat16)
        back_own[...] = back_sum[:half]
        back_other[...] = back_sum[half:]


def feed_forward(rows, cots, gate_w, up_w, down_w):
    count, width = rows.shape
    hidden = gate_w.shape[1]
    whole = pl.BlockSpec((count, width), lambda tile: (0, 0))
    half = pl.BlockSpec((count // 2, width), lambda tile: (0, 0))
    columns = pl.BlockSpec((width, HIDDEN_TILE), lambda tile: (0, tile))
    lines = pl.BlockSpec((HIDDEN_TILE, width), lambda tile: (tile, 0))
    half_wide = jax.ShapeDtypeStruct((count // 2, width), jnp.float32)
    half_low = jax.ShapeDtypeStruct((count // 2, width), jnp.bfloat16)
    return pl.pallas_call(
        feed_kernel,
        grid=(hidden // HIDDEN_TILE,),
        in_specs=[whole, whole, columns, columns, lines],
        out_specs=[half, half, half, half, lines, columns, pl.BlockSpec((count, HIDDEN_TILE), lambda tile: (0, tile))],
        out_shape=[half_wide, half_low, half_wide, half_wide]
        + [
            jax.ShapeDtypeStruct((hidden, width), jnp.bfloat16),
            jax.ShapeDtypeStruct((width, hidden), jnp.bfloat16),
            jax.ShapeDtypeStruct((count, hidden), jnp.bfloat16),
        ],
        scratch_shapes=[
            pltpu.VMEM((width, count), jnp.bfloat16),
            pltpu.VMEM((count, width), jnp.float32),
            pltpu.VMEM((count, width), jnp.float32),
        ],
        compiler_params=pltpu.CompilerParams(vmem_limit_bytes=52 * 1024 * 1024),
        cost_estimate=pl.CostEstimate(
            flops=16 * count * width * hidden, bytes_accessed=12 * width * hidden + 16 * count * width, transcendentals=count * hidden
        ),
    )(rows, cots, gate_w, up_w, down_w)


def partner(values):
    return lax.ppermute(values, "narrow", [(0, 1), (1, 0)])


def rows_of(own, other):
    return jnp.concatenate([own, other], axis=0)


def rotary_pair_tables(position):
    lane = jnp.arange(LANES) % HD
    half_dim = HD // 2
    frequency = ROPE_BASE ** (-2.0 * (lane % half_dim).astype(jnp.float32) / HD)
    angles = position[:, None] * frequency[None, :]
    signs = jnp.where(lane < half_dim, -1.0, 1.0).astype(jnp.float32)
    return (jnp.cos(angles), jnp.sin(angles) * signs)


def on_device(
    tokens,
    window_span,
    valid_len,
    norm1_gain,
    norm1_shift,
    w_query,
    w_key,
    w_value,
    w_out,
    norm2_gain,
    norm2_shift,
    w_gate,
    w_up,
    w_down,
    cotangent,
):
    block_rows = tokens.shape[0]
    own_block = lax.axis_index("narrow")
    joined = window_span[0] == 2
    block_ids = jnp.stack([own_block, 1 - own_block])
    lengths = valid_len[block_ids]
    offsets = jnp.arange(2 * block_rows)
    row_block = offsets // block_rows
    position = offsets % block_rows + block_rows * jnp.repeat(block_ids, block_rows) * joined.astype(jnp.int32)
    cosine, sine = rotary_pair_tables(position.astype(jnp.float32))
    within = offsets % block_rows < jnp.repeat(lengths, block_rows)
    seen = within[:, None] & (joined | (row_block[:, None] == jnp.arange(2)[None, :]))
    mask = jnp.where(seen, 0.0, MASKED).astype(jnp.float32)

    token_values = tokens.astype(jnp.float32)
    normed_one, scaled_one, inverse_one = norm_forward(token_values, norm1_gain, norm1_shift)
    normed_one = normed_one.astype(jnp.bfloat16)
    gathered_one = rows_of(normed_one, partner(normed_one))
    cot_rows = rows_of(cotangent, partner(cotangent))
    projected = [
        jnp.dot(gathered_one, weight, preferred_element_type=jnp.float32)
        for weight in (w_query, w_key, w_value)
    ]
    query_rows, key_rows, value_rows, mixed_rows, logs = attend(*projected, cosine, sine, mask)
    other_share = jnp.dot(mixed_rows[block_rows:], w_out, preferred_element_type=jnp.float32)
    resid_values = (
        token_values
        + jnp.dot(mixed_rows[:block_rows], w_out, preferred_element_type=jnp.float32)
        + partner(other_share)
    )
    normed_two, scaled_two, inverse_two = norm_forward(resid_values, norm2_gain, norm2_shift)
    normed_two = normed_two.astype(jnp.bfloat16)
    gathered_two = rows_of(normed_two, partner(normed_two))
    out_own, out_other, grad_two_own, grad_two_other, down_grad, gate_grad, grad_up = feed_forward(
        gathered_two, cot_rows, w_gate, w_up, w_down
    )
    up_grad = transpose_times(gathered_two, grad_up).astype(jnp.bfloat16)
    out_values = resid_values + out_own + partner(out_other).astype(jnp.float32)
    grad_normed_two = grad_two_own + partner(grad_two_other)
    grad_in_two, gain_two_grad, shift_two_grad = norm_backward(
        grad_normed_two, scaled_two, inverse_two, norm2_gain
    )
    grad_resid = cotangent.astype(jnp.float32) + grad_in_two
    grad_attention = grad_resid.astype(jnp.bfloat16)
    grad_rows = rows_of(grad_attention, partner(grad_attention))
    grad_mixed = times_transpose(grad_rows, w_out).astype(jnp.bfloat16)
    out_grad = transpose_times(mixed_rows, grad_rows).astype(jnp.bfloat16)
    grad_projected = attend_back(
        query_rows, key_rows, value_rows, mixed_rows, grad_mixed, logs, cosine, sine, mask
    )
    qkv_grads = [transpose_times(gathered_one, g).astype(jnp.bfloat16) for g in grad_projected]

    def grad_one_share(rows):
        return sum(
            times_transpose(g[rows], weight)
            for g, weight in zip(grad_projected, (w_query, w_key, w_value))
        )

    grad_one_other = grad_one_share(slice(block_rows, None)).astype(jnp.bfloat16)
    grad_normed_one = grad_one_share(slice(0, block_rows)) + partner(grad_one_other).astype(
        jnp.float32
    )
    grad_in_one, gain_one_grad, shift_one_grad = norm_backward(
        grad_normed_one, scaled_one, inverse_one, norm1_gain
    )
    token_grad = grad_resid + grad_in_one
    norm_grads = jnp.stack([gain_one_grad, shift_one_grad, gain_two_grad, shift_two_grad])
    gradients = dict(zip(NAMES, [down_grad, gate_grad, up_grad, out_grad] + qkv_grads))
    fast = [name for name in NAMES if name not in SLOW]
    *fast_sums, norm_summed = summed_over_wide(
        [gradients[n] for n in fast], [CHUNK[n] for n in fast], jnp.pad(norm_grads, ((0, 4), (0, 0))), 1
    )
    sums = dict(zip(fast, fast_sums))
    for name in SLOW:
        sums[name] = lax.psum(gradients[name], "wide")
    down_summed, gate_summed, up_summed, out_summed, query_summed, key_summed, value_summed = [
        sums[name].astype(jnp.float32) for name in NAMES
    ]
    return (
        out_values,
        token_grad,
        norm_summed[0],
        norm_summed[1],
        query_summed,
        key_summed,
        value_summed,
        out_summed,
        norm_summed[2],
        norm_summed[3],
        gate_summed,
        up_summed,
        down_summed,
    )


def solution(mesh):
    fits = mesh.shape["wide"] == PLANES * 4 and mesh.shape["narrow"] == 2
    in_specs = (
        P(("wide", "narrow"), None),
        P("wide"),
        P("wide"),
        P(),
        P(),
        P(None, "narrow"),
        P(None, "narrow"),
        P(None, "narrow"),
        P("narrow", None),
        P(),
        P(),
        P(None, "narrow"),
        P(None, "narrow"),
        P("narrow", None),
        P(("wide", "narrow"), None),
    )
    out_specs = (
        P(("wide", "narrow"), None),
        P(("wide", "narrow"), None),
        P(),
        P(),
        P(None, "narrow"),
        P(None, "narrow"),
        P(None, "narrow"),
        P("narrow", None),
        P(),
        P(),
        P(None, "narrow"),
        P(None, "narrow"),
        P("narrow", None),
    )
    return jax.shard_map(
        on_device if fits else on_device_any_mesh, mesh=mesh, in_specs=in_specs, out_specs=out_specs, check_vma=False
    )
```

```python
import functools

import jax
import jax.numpy as jnp
from jax import lax
from jax.experimental import pallas as pl
from jax.experimental.pallas import tpu as pltpu
from jax.sharding import PartitionSpec as P

MESH = pl.DeviceIdType.MESH

HD = 64


EPSILON = 1e-05
MASKED = -1e30
ROPE_BASE = 10000.0


def times_transpose(left, right):
    return lax.dot_general(
        left, right, (((1,), (1,)), ((), ())), preferred_element_type=jnp.float32
    )


def transpose_times(left, right):
    return lax.dot_general(
        left, right, (((0,), (0,)), ((), ())), preferred_element_type=jnp.float32
    )


def norm_forward(values, norm_gain, norm_shift):
    average = jnp.mean(values, axis=-1, keepdims=True)
    centred = values - average
    inverse = lax.rsqrt(jnp.mean(centred * centred, axis=-1, keepdims=True) + EPSILON)
    scaled = centred * inverse
    return (scaled * norm_gain + norm_shift, scaled, inverse)


def norm_backward(grad_out, scaled, inverse, norm_gain):
    grad_scaled = grad_out * norm_gain
    first_term = jnp.mean(grad_scaled, axis=-1, keepdims=True)
    second_term = jnp.mean(grad_scaled * scaled, axis=-1, keepdims=True)
    grad_in = inverse * (grad_scaled - first_term - scaled * second_term)
    return (grad_in, jnp.sum(grad_out * scaled, axis=0), jnp.sum(grad_out, axis=0))


def rotary_tables(span_table, block_rows, width):
    row_count = span_table.shape[0] * block_rows
    row_ids = jnp.arange(row_count)
    block_ids = row_ids // block_rows
    span_rows = jnp.repeat(span_table, block_rows)
    position = (row_ids % block_rows + block_rows * (block_ids % 2) * (span_rows == 2)).astype(
        jnp.float32
    )
    columns = jnp.arange(width) % HD
    half_dim = HD // 2
    freq_index = (columns % half_dim).astype(jnp.float32)
    frequency = ROPE_BASE ** (-2.0 * freq_index / HD)
    angles = position[:, None] * frequency[None, :]
    signs = jnp.where(columns < half_dim, -1.0, 1.0).astype(jnp.float32)
    return (jnp.cos(angles), jnp.sin(angles) * signs)


def swap_halves(values):
    row_count = values.shape[0]
    width = values.shape[1]
    parts = values.reshape(row_count, width // HD, 2, HD // 2)
    return jnp.flip(parts, axis=2).reshape(row_count, width)


def rotate(values, cosine, sine_signed):
    return values * cosine + swap_halves(values) * sine_signed


def rotate_back(grads_in, cosine, sine_signed):
    return grads_in * cosine + swap_halves(grads_in * sine_signed)


def pair_mask(block_index, span_table, valid_table, block_rows):
    pair_first = block_index // 2 * 2
    offsets = jnp.arange(2 * block_rows)
    key_block = pair_first + offsets // block_rows
    within = offsets % block_rows
    first_len = lax.dynamic_index_in_dim(valid_table, pair_first, keepdims=False)
    second_len = lax.dynamic_index_in_dim(valid_table, pair_first + 1, keepdims=False)
    own_span = lax.dynamic_index_in_dim(span_table, block_index, keepdims=False)
    length_bound = jnp.where(offsets < block_rows, first_len, second_len)
    return (within < length_bound) & ((own_span == 2) | (key_block == block_index))


def on_device_any_mesh(
    tokens,
    window_span,
    valid_len,
    norm1_gain,
    norm1_shift,
    w_query,
    w_key,
    w_value,
    w_out,
    norm2_gain,
    norm2_shift,
    w_gate,
    w_up,
    w_down,
    cotangent,
):
    local_rows = tokens.shape[0]
    group_rows = local_rows * lax.axis_size("narrow")
    block_count = window_span.shape[0]
    block_rows = group_rows // block_count
    local_width = w_query.shape[1]
    local_heads = local_width // HD
    local_hidden = w_gate.shape[1]
    softmax_scale = HD ** (-0.5)
    token_values = tokens.astype(jnp.float32)
    normed_one, scaled_one, inverse_one = norm_forward(token_values, norm1_gain, norm1_shift)
    normed_one = normed_one.astype(jnp.bfloat16)
    gathered_one = lax.all_gather(normed_one, "narrow", axis=0, tiled=True)
    joined_qkv = jnp.concatenate([w_query, w_key, w_value], axis=1)
    projected = jnp.dot(gathered_one, joined_qkv, preferred_element_type=jnp.float32)
    cosine, sine_signed = rotary_tables(window_span, block_rows, local_width)
    query_rows = (rotate(projected[:, :local_width], cosine, sine_signed) * softmax_scale).astype(
        jnp.bfloat16
    )
    key_rows = rotate(projected[:, local_width : 2 * local_width], cosine, sine_signed).astype(
        jnp.bfloat16
    )
    value_rows = projected[:, 2 * local_width :].astype(jnp.bfloat16)

    def block_slices(block_index):
        query_block = lax.dynamic_slice_in_dim(query_rows, block_index * block_rows, block_rows, 0)
        pair_start = block_index // 2 * 2 * block_rows
        return (
            query_block.reshape(block_rows, local_heads, HD),
            key_rows.reshape(2 * block_rows, local_heads, HD),
            value_rows.reshape(2 * block_rows, local_heads, HD),
            pair_start,
        )

    def masked_scores(block_index, query_block, key_pair):
        scores = jnp.einsum(
            "qhd,khd->hqk", query_block, key_pair, preferred_element_type=jnp.float32
        )
        key_mask = pair_mask(block_index, window_span, valid_len, block_rows)
        return jnp.where(key_mask[None, None, :], scores, MASKED)

    def attend_forward(block_index):
        query_block, key_pair, value_pair, pair_start = block_slices(block_index)
        scores = masked_scores(block_index, query_block, key_pair)
        highest = jnp.max(scores, axis=-1, keepdims=True)
        weights = jnp.exp(scores - highest)
        weight_total = jnp.sum(weights, axis=-1, keepdims=True)
        attention_probs = (weights / weight_total).astype(jnp.bfloat16)
        mixed_block = jnp.einsum(
            "hqk,khd->qhd", attention_probs, value_pair, preferred_element_type=jnp.float32
        )
        return (
            mixed_block.reshape(block_rows, local_width).astype(jnp.bfloat16),
            (highest + jnp.log(weight_total))[:, :, 0],
        )

    mixed_blocks, log_totals = lax.map(attend_forward, jnp.arange(block_count))
    mixed_rows = mixed_blocks.reshape(group_rows, local_width)
    resid_values = token_values + lax.psum_scatter(
        jnp.dot(mixed_rows, w_out, preferred_element_type=jnp.float32),
        "narrow",
        scatter_dimension=0,
        tiled=True,
    )
    normed_two, scaled_two, inverse_two = norm_forward(resid_values, norm2_gain, norm2_shift)
    normed_two = normed_two.astype(jnp.bfloat16)
    gathered_two = lax.all_gather(normed_two, "narrow", axis=0, tiled=True)
    joined_gate_up = jnp.concatenate([w_gate, w_up], axis=1)
    gate_up = jnp.dot(gathered_two, joined_gate_up, preferred_element_type=jnp.float32)
    gate_values = gate_up[:, :local_hidden]
    up_values = gate_up[:, local_hidden:]
    sigmoid_gate = jax.nn.sigmoid(gate_values)
    hidden_rows = (gate_values * sigmoid_gate * up_values).astype(jnp.bfloat16)
    out_values = resid_values + lax.psum_scatter(
        jnp.dot(hidden_rows, w_down, preferred_element_type=jnp.float32).astype(jnp.bfloat16),
        "narrow",
        scatter_dimension=0,
        tiled=True,
    ).astype(jnp.float32)
    shard_rows = lax.all_gather(cotangent, "narrow", axis=0, tiled=True)
    grad_hidden = times_transpose(shard_rows, w_down)
    grad_down_w, grad_hidden = (transpose_times(hidden_rows, shard_rows), grad_hidden)
    silu_grad = sigmoid_gate * (1.0 + gate_values * (1.0 - sigmoid_gate))
    grad_gate_up = jnp.concatenate(
        [grad_hidden * up_values * silu_grad, grad_hidden * gate_values * sigmoid_gate], axis=1
    ).astype(jnp.bfloat16)
    grad_normed_two = lax.psum_scatter(
        times_transpose(grad_gate_up, joined_gate_up), "narrow", scatter_dimension=0, tiled=True
    )
    grad_gate_up_w = transpose_times(gathered_two, grad_gate_up)
    grad_in_two, gain_two_grad, shift_two_grad = norm_backward(
        grad_normed_two, scaled_two, inverse_two, norm2_gain
    )
    grad_resid = cotangent.astype(jnp.float32) + grad_in_two
    shard_rows = lax.all_gather(grad_resid.astype(jnp.bfloat16), "narrow", axis=0, tiled=True)
    grad_mixed_sum = times_transpose(shard_rows, w_out)
    grad_out_w, grad_mixed_sum = (transpose_times(mixed_rows, shard_rows), grad_mixed_sum)
    grad_mixed = grad_mixed_sum.astype(jnp.bfloat16)

    def attend_backward(block_index, running):
        grad_query, grad_key, grad_value = running
        query_block, key_pair, value_pair, pair_start = block_slices(block_index)
        grad_rows = lax.dynamic_slice_in_dim(
            grad_mixed, block_index * block_rows, block_rows, 0
        ).reshape(block_rows, local_heads, HD)
        scores = masked_scores(block_index, query_block, key_pair)
        log_total = lax.dynamic_index_in_dim(log_totals, block_index, keepdims=False)
        attention_probs = jnp.exp(scores - log_total[:, :, None])
        grad_probs = jnp.einsum(
            "qhd,khd->hqk", grad_rows, value_pair, preferred_element_type=jnp.float32
        )
        centre = jnp.sum(attention_probs * grad_probs, axis=-1, keepdims=True)
        grad_scores = (attention_probs * (grad_probs - centre)).astype(jnp.bfloat16)
        block_query = jnp.einsum(
            "hqk,khd->qhd", grad_scores, key_pair, preferred_element_type=jnp.float32
        ).reshape(block_rows, local_width)
        pair_key = jnp.einsum(
            "hqk,qhd->khd", grad_scores, query_block, preferred_element_type=jnp.float32
        ).reshape(2 * block_rows, local_width)
        pair_value = jnp.einsum(
            "hqk,qhd->khd",
            attention_probs.astype(jnp.bfloat16),
            grad_rows,
            preferred_element_type=jnp.float32,
        ).reshape(2 * block_rows, local_width)
        grad_query = lax.dynamic_update_slice_in_dim(
            grad_query, block_query, block_index * block_rows, 0
        )
        grad_key = grad_key + pair_key
        grad_value = grad_value + pair_value
        return (grad_query, grad_key, grad_value)

    zero_rows = jnp.zeros((group_rows, local_width), jnp.float32)
    grad_query, grad_key, grad_value = lax.fori_loop(
        0, block_count, attend_backward, (zero_rows, zero_rows, zero_rows)
    )
    grad_query_raw = rotate_back(grad_query * softmax_scale, cosine, sine_signed)
    grad_key_raw = rotate_back(grad_key, cosine, sine_signed)
    grad_qkv = jnp.concatenate([grad_query_raw, grad_key_raw, grad_value], axis=1).astype(
        jnp.bfloat16
    )
    grad_normed_one = lax.psum_scatter(
        times_transpose(grad_qkv, joined_qkv).astype(jnp.bfloat16),
        "narrow",
        scatter_dimension=0,
        tiled=True,
    ).astype(jnp.float32)
    grad_qkv_w = transpose_times(gathered_one, grad_qkv)
    grad_in_one, gain_one_grad, shift_one_grad = norm_backward(
        grad_normed_one, scaled_one, inverse_one, norm1_gain
    )
    token_grad = grad_resid + grad_in_one
    qkv_summed, out_summed, gate_up_summed, down_summed = (
        lax.psum(grad_qkv_w.astype(jnp.bfloat16), "wide").astype(jnp.float32),
        lax.psum(grad_out_w.astype(jnp.bfloat16), "wide").astype(jnp.float32),
        lax.psum(grad_gate_up_w.astype(jnp.bfloat16), "wide").astype(jnp.float32),
        lax.psum(grad_down_w.astype(jnp.bfloat16), "wide").astype(jnp.float32),
    )
    norm_summed = lax.psum(
        (gain_one_grad, shift_one_grad, gain_two_grad, shift_two_grad), ("wide", "narrow")
    )
    return (
        out_values,
        token_grad,
        norm_summed[0],
        norm_summed[1],
        qkv_summed[:, :local_width],
        qkv_summed[:, local_width : 2 * local_width],
        qkv_summed[:, 2 * local_width :],
        out_summed,
        norm_summed[2],
        norm_summed[3],
        gate_up_summed[:, :local_hidden],
        gate_up_summed[:, local_hidden:],
        down_summed,
    )


PLANES = 4


class Job:
    def __init__(self, rows, cols, chunk_rows):
        self.rows, self.cols, self.chunk_rows = rows, cols, chunk_rows
        self.count = rows // (2 * chunk_rows)


def scratch_for(job):
    half, quarter = job.chunk_rows // 2, job.chunk_rows // 4

    def slots(rows):
        return pltpu.VMEM((job.count, 2, rows, job.cols), jnp.bfloat16)

    return [
        pltpu.VMEM((job.rows, job.cols), jnp.bfloat16),
        slots(half),
        slots(half),
        slots(quarter),
        slots(quarter),
        slots(quarter),
        slots(half),
        pltpu.SemaphoreType.DMA((job.count, 2, 9)),
        pltpu.SemaphoreType.DMA((job.count, 2, 9)),
        pltpu.SemaphoreType.DMA((job.count,)),
        pltpu.SemaphoreType.DMA((job.count, 2, 3)),
    ]


OUTER, INWARD, ACROSS, CROSS, BACK, OUT_A, OUT_B, GATHER_A, GATHER_B = range(9)


class Links:
    def __init__(self):
        position = lax.axis_index("wide")
        self.x = lax.rem(position, 2)
        self.y = lax.rem(position // 2, 2)
        self.z = position // 4
        self.middle = jnp.logical_and(self.z >= 1, self.z <= 2)
        self.edge = jnp.logical_or(self.z == 0, self.z == PLANES - 1)
        self.upper = self.z // 2
        self.across = self.at(self.x, self.y, 3 - self.z)
        step = 1 - 2 * self.upper
        self.inward = self.at(self.x, self.y, lax.rem(self.z + step + PLANES, PLANES))
        self.outward = self.at(self.x, self.y, lax.rem(self.z - step + PLANES, PLANES))
        self.flips = [self.at(1 - self.x, self.y, self.z), self.at(self.x, 1 - self.y, self.z)]
        self.bits = [self.x, self.y]

    def at(self, x, y, z):
        return z * 4 + y * 2 + x

    def greet(self):
        barrier = pltpu.get_barrier_semaphore()

        def signal(target):
            pl.semaphore_signal(barrier, inc=1, device_id={"wide": target}, device_id_type=MESH)

        pl.semaphore_signal(
            barrier, inc=1, device_id={"narrow": 1 - lax.axis_index("narrow")}, device_id_type=MESH
        )
        for target in self.flips:
            signal(target)

        @pl.when(self.edge)
        def _():
            signal(self.inward)
            pl.semaphore_wait(barrier, 4)

        @pl.when(self.middle)
        def _():
            signal(self.across)
            signal(self.outward)
            pl.semaphore_wait(barrier, 5)


ADD_ROWS = 16


def add_rows(held, start, other, rows):
    def add(index, carry):
        own = pl.ds(pl.multiple_of(start + index * ADD_ROWS, ADD_ROWS), ADD_ROWS)
        arrived = other[pl.ds(pl.multiple_of(index * ADD_ROWS, ADD_ROWS), ADD_ROWS), :]
        held[own, :] = (held[own, :].astype(jnp.float32) + arrived.astype(jnp.float32)).astype(jnp.bfloat16)
        return carry

    lax.fori_loop(0, rows // ADD_ROWS, add, 0)


class Vectors:
    STEPS = 7

    def __init__(self, links, source, output, stages, arrived, sent, got):
        self.links, self.source, self.output = links, source, output
        self.stages, self.arrived, self.sent, self.got = stages, arrived, sent, got

    def copy(self, number, source, target):
        return pltpu.make_async_remote_copy(
            src_ref=source,
            dst_ref=self.arrived.at[number],
            send_sem=self.sent.at[number],
            recv_sem=self.got.at[number],
            device_id=target,
            device_id_type=MESH,
        )

    def exchange(self, number):
        links = self.links
        targets = [
            {"narrow": 1 - lax.axis_index("narrow")},
            {"wide": links.flips[0]},
            {"wide": links.flips[1]},
            {"wide": links.inward},
            {"wide": links.across},
            {"wide": links.outward},
        ]
        source = self.source if number == 0 else self.stages.at[number]
        return self.copy(number, source, targets[number])

    def add(self, number):
        source = self.source if number == 0 else self.stages.at[number]
        self.stages[number + 1] = source[...] + self.arrived[number]

    def step(self, number):
        links = self.links
        if number in (1, 2, 3):
            self.exchange(number - 1).wait_recv()
            self.add(number - 1)
        if number < 3:
            self.exchange(number).start()
        if number == 3:

            @pl.when(links.edge)
            def _():
                self.exchange(3).start()

        if number in (4, 5):

            @pl.when(links.middle)
            def _():
                self.exchange(number - 1).wait_recv()
                self.add(number - 1)
                self.exchange(number).start()

        if number == 6:

            @pl.when(links.middle)
            def _():
                self.output[...] = self.stages[5]

            @pl.when(links.edge)
            def _():
                self.exchange(5).wait_recv()
                self.output[...] = self.arrived[5]

    def close(self):
        for number in range(3):
            self.exchange(number).wait_send()

        @pl.when(self.links.edge)
        def _():
            self.exchange(3).wait_send()

        @pl.when(self.links.middle)
        def _():
            self.exchange(4).wait_send()
            self.exchange(5).wait_send()


class Chunk:
    STEPS = 8

    def __init__(self, links, job, refs, output, index, colour):
        self.links, self.colour, self.index, self.output = links, colour, index, output
        self.held = refs[0]
        self.pair_in, self.column_in, self.across_in, self.cross_in, self.back_in, self.gather_in = [
            ref.at[index, colour] for ref in refs[1:7]
        ]
        self.sent, self.got, self.loaded, self.stored = refs[7:11]
        self.half, self.quarter = job.chunk_rows // 2, job.chunk_rows // 4
        self.base = (2 * index + colour) * job.chunk_rows
        bit = links.bits[colour]
        self.keep = pl.multiple_of(self.base + bit * self.half, self.quarter)
        self.away = pl.multiple_of(self.base + (1 - bit) * self.half, self.quarter)
        self.near = pl.multiple_of(links.upper * self.quarter, self.quarter)
        self.far = pl.multiple_of((1 - links.upper) * self.quarter, self.quarter)
        self.kept = pl.multiple_of(self.keep + self.near, self.quarter)
        self.given = pl.multiple_of(self.keep + self.far, self.quarter)
        self.outer_peer = links.flips[colour]
        self.inner_peer = links.flips[1 - colour]

    def rows(self, start, size):
        return self.held.at[pl.ds(start, size), :]

    def part(self, ref, start):
        return ref.at[pl.ds(start, self.quarter), :]

    def copy(self, step, source, target, peer):
        return pltpu.make_async_remote_copy(
            src_ref=source,
            dst_ref=target,
            send_sem=self.sent.at[self.index, self.colour, step],
            recv_sem=self.got.at[self.index, self.colour, step],
            device_id={"wide": peer},
            device_id_type=MESH,
        )

    def outer(self):
        return self.copy(OUTER, self.rows(self.away, self.half), self.pair_in, self.outer_peer)

    def inward(self):
        return self.copy(INWARD, self.rows(self.keep, self.half), self.column_in, self.links.inward)

    def across(self):
        return self.copy(ACROSS, self.rows(self.given, self.quarter), self.across_in, self.links.across)

    def cross(self):
        return self.copy(CROSS, self.rows(self.kept, self.quarter), self.cross_in, self.inner_peer)

    def back(self):
        return self.copy(BACK, self.rows(self.kept, self.quarter), self.back_in, self.links.across)

    def out_a(self):
        target = self.part(self.column_in, self.near)
        return self.copy(OUT_A, self.rows(self.kept, self.quarter), target, self.links.outward)

    def out_b(self):
        return self.copy(OUT_B, self.back_in, self.part(self.column_in, self.far), self.links.outward)

    def gather_a(self, source):
        return self.copy(GATHER_A, source, self.part(self.gather_in, self.near), self.outer_peer)

    def gather_b(self, source):
        return self.copy(GATHER_B, source, self.part(self.gather_in, self.far), self.outer_peer)

    def store(self, place, source, start, size):
        target = self.output.at[pl.ds(start, size), :]
        return pltpu.make_async_copy(source, target, self.stored.at[self.index, self.colour, place])

    def totals(self, near, far):
        return self.store(0, near, self.kept, self.quarter), self.store(1, far, self.given, self.quarter)

    def partner_total(self):
        return self.store(2, self.gather_in, self.away, self.half)

    def step(self, number):
        links = self.links
        near_total = self.rows(self.kept, self.quarter)
        edge_near, edge_far = self.part(self.column_in, self.near), self.part(self.column_in, self.far)
        if number == 0:
            self.outer().start()
        if number == 1:
            self.outer().wait_recv()
            add_rows(self.held, self.keep, self.pair_in, self.half)

            @pl.when(links.edge)
            def _():
                self.inward().start()

        if number == 2:

            @pl.when(links.middle)
            def _():
                self.inward().wait_recv()
                add_rows(self.held, self.keep, self.column_in, self.half)
                self.across().start()

        if number == 3:

            @pl.when(links.middle)
            def _():
                self.across().wait_recv()
                add_rows(self.held, self.kept, self.across_in, self.quarter)
                self.cross().start()

        if number == 4:

            @pl.when(links.middle)
            def _():
                self.cross().wait()
                add_rows(self.held, self.kept, self.cross_in, self.quarter)
                self.back().start()
                self.out_a().start()
                self.gather_a(near_total).start()

        if number == 5:

            @pl.when(links.middle)
            def _():
                self.back().wait_recv()
                self.out_b().start()
                self.gather_b(self.back_in).start()
                for store in self.totals(near_total, self.back_in):
                    store.start()

            @pl.when(links.edge)
            def _():
                self.out_a().wait_recv()
                self.gather_a(edge_near).start()

        if number == 6:

            @pl.when(links.edge)
            def _():
                self.out_b().wait_recv()
                self.gather_b(edge_far).start()
                for store in self.totals(edge_near, edge_far):
                    store.start()

        if number == 7:
            self.gather_a(near_total).wait_recv()
            self.gather_b(self.back_in).wait_recv()
            self.partner_total().start()

    def close(self):
        near_total = self.rows(self.kept, self.quarter)
        self.outer().wait_send()
        self.gather_a(near_total).wait_send()
        self.gather_b(self.back_in).wait_send()

        @pl.when(self.links.middle)
        def _():
            self.across().wait_send()
            self.back().wait_send()
            self.out_a().wait_send()
            self.out_b().wait_send()

        @pl.when(self.links.edge)
        def _():
            self.inward().wait_send()

        for store in self.totals(near_total, self.back_in):
            store.wait()
        self.partner_total().wait()


def sum_kernel(jobs, *refs):
    count = len(jobs)
    inputs, refs = refs[: count + 1], refs[count + 1 :]
    outputs, scratch = refs[: count + 1], refs[count + 1 :]
    scratch, vector_scratch = scratch[:-4], scratch[-4:]
    per_job = len(scratch) // count
    links = Links()
    vectors = Vectors(links, inputs[count], outputs[count], *vector_scratch)
    items = []
    for number, job in enumerate(jobs):
        own = scratch[number * per_job : (number + 1) * per_job]
        for index in range(job.count):
            pair = [Chunk(links, job, own, outputs[number], index, colour) for colour in range(2)]
            span = pl.ds(2 * index * job.chunk_rows, 2 * job.chunk_rows)
            load = pltpu.make_async_copy(inputs[number].at[span, :], own[0].at[span, :], own[9].at[index])
            load.start()
            items.append((pair, load))
    links.greet()
    for tick in range(len(items) + Chunk.STEPS - 1):
        if tick < Vectors.STEPS:
            vectors.step(tick)
        for place, (pair, load) in enumerate(items):
            step = tick - place
            if 0 <= step < Chunk.STEPS:
                if step == 0:
                    load.wait()
                for chunk in pair:
                    chunk.step(step)
    for pair, _ in items:
        for chunk in pair:
            chunk.close()
    vectors.close()


def summed_over_wide(gradients, chunk_rows, vectors, collective_id):
    jobs = [Job(g.shape[0], g.shape[1], r) for g, r in zip(gradients, chunk_rows)]
    scratch = []
    for job in jobs:
        scratch += scratch_for(job)
    scratch += [
        pltpu.VMEM((6, *vectors.shape), jnp.float32),
        pltpu.VMEM((6, *vectors.shape), jnp.float32),
        pltpu.SemaphoreType.DMA((6,)),
        pltpu.SemaphoreType.DMA((6,)),
    ]
    sent = sum(2 * g.size * 5 // 4 for g in gradients)
    return pl.pallas_call(
        functools.partial(sum_kernel, jobs),
        out_shape=[jax.ShapeDtypeStruct(g.shape, jnp.bfloat16) for g in gradients]
        + [jax.ShapeDtypeStruct(vectors.shape, jnp.float32)],
        in_specs=[pl.BlockSpec(memory_space=pl.ANY)] * len(jobs) + [pl.BlockSpec(memory_space=pltpu.VMEM)],
        out_specs=[pl.BlockSpec(memory_space=pl.ANY)] * len(jobs) + [pl.BlockSpec(memory_space=pltpu.VMEM)],
        scratch_shapes=scratch,
        compiler_params=pltpu.CompilerParams(
            collective_id=collective_id, has_side_effects=True, vmem_limit_bytes=60 * 1024 * 1024
        ),
        cost_estimate=pl.CostEstimate(flops=0, bytes_accessed=2 * sent, transcendentals=0),
    )(*gradients, vectors)


LANES = 128
QUERY_TILE = 512
BACK_TILE = 256


def nt_dot(left, right):
    return lax.dot_general(
        left, right, (((1,), (1,)), ((), ())), preferred_element_type=jnp.float32
    )


def nn_dot(left, right):
    return jnp.dot(left, right, preferred_element_type=jnp.float32)


def swap_lanes(values):
    lane = lax.broadcasted_iota(jnp.int32, values.shape, 1)
    half_dim = HD // 2
    ahead = pltpu.roll(values, LANES - half_dim, axis=1)
    behind = pltpu.roll(values, half_dim, axis=1)
    return jnp.where(lane % HD < half_dim, ahead, behind)


def head_lanes(rows, head):
    return lax.broadcasted_iota(jnp.int32, (rows, LANES), 1) // HD == head


def masked_keys(keys, mask, head):
    lane = lax.broadcasted_iota(jnp.int32, keys.shape, 1)
    spare = (1 - head) * HD
    keys = jnp.where(lane // HD == head, keys, jnp.zeros_like(keys))
    for block in range(2):
        keys = jnp.where(lane == spare + block, mask[:, block : block + 1], keys)
    return keys


def head_queries(queries, head, block):
    lane = lax.broadcasted_iota(jnp.int32, queries.shape, 1)
    spare = (1 - head) * HD
    queries = jnp.where(lane // HD == head, queries, jnp.zeros_like(queries))
    return jnp.where(lane == spare + block, jnp.ones_like(queries), queries)


def attend_kernel(
    query_raw, key_raw, value_raw, cosine, sine, mask, query_out, key_out, value_out, mixed_out, log_out, mixed_t
):
    rows = query_raw.shape[0]
    block_rows = rows // 2
    cos, sin = cosine[...], sine[...]
    queries = query_raw[...]
    query_out[...] = ((queries * cos + swap_lanes(queries) * sin) * HD ** (-0.5)).astype(jnp.bfloat16)
    keys = key_raw[...]
    key_out[...] = (keys * cos + swap_lanes(keys) * sin).astype(jnp.bfloat16)
    value_out[...] = value_raw[...].astype(jnp.bfloat16)
    values_t = value_out[...].T
    mask_low = mask[...].astype(jnp.bfloat16)
    keys_of = [masked_keys(key_out[...], mask_low, head) for head in range(2)]

    def tile(index, carry):
        span = pl.ds(pl.multiple_of(index * QUERY_TILE, QUERY_TILE), QUERY_TILE)
        block = index * QUERY_TILE // block_rows
        for head in range(2):
            scores = nt_dot(keys_of[head], head_queries(query_out[span, :], head, block))
            highest = jnp.max(scores, axis=0, keepdims=True)
            weights = jnp.exp(scores - highest)
            total = jnp.sum(weights, axis=0, keepdims=True)
            mixed = nn_dot(values_t[head * HD : (head + 1) * HD], weights.astype(jnp.bfloat16)) / total
            mixed_t[pl.ds(head * HD, HD), span] = mixed
            log_out[0, pl.ds(head, 1), span] = highest + jnp.log(total)
        return carry

    lax.fori_loop(0, rows // QUERY_TILE, tile, 0, unroll=True)
    mixed_out[...] = mixed_t[...].T.astype(jnp.bfloat16)


def attend(query_raw, key_raw, value_raw, cosine, sine, mask):
    rows, width = query_raw.shape
    pairs = width // LANES
    wide_block = pl.BlockSpec((rows, LANES), lambda pair: (0, pair))
    table = pl.BlockSpec((rows, LANES), lambda pair: (0, 0))
    low = jax.ShapeDtypeStruct((rows, width), jnp.bfloat16)
    return pl.pallas_call(
        attend_kernel,
        grid=(pairs,),
        in_specs=[wide_block] * 3 + [table, table, pl.BlockSpec((rows, 2), lambda pair: (0, 0))],
        out_specs=[wide_block] * 4 + [pl.BlockSpec((1, 2, rows), lambda pair: (pair, 0, 0))],
        out_shape=[low] * 4 + [jax.ShapeDtypeStruct((pairs, 2, rows), jnp.float32)],
        scratch_shapes=[pltpu.VMEM((LANES, rows), jnp.float32)],
        compiler_params=pltpu.CompilerParams(vmem_limit_bytes=32 * 1024 * 1024),
        cost_estimate=pl.CostEstimate(
            flops=4 * rows * rows * width, bytes_accessed=20 * rows * width, transcendentals=rows * rows * width // HD
        ),
    )(query_raw, key_raw, value_raw, cosine, sine, mask)


def attend_back_pair(
    query_rows, key_rows, value_rows, mixed_rows, grad_mixed, logs, cos, sin, mask, outs, grad_query_t, grad_key, grad_value, grad_t
):
    rows = query_rows.shape[0]
    block_rows = rows // 2
    mask_low = mask[...].astype(jnp.bfloat16)
    keys_t = key_rows[...].T
    values = value_rows[...]
    grad_t[...] = (grad_mixed[...].astype(jnp.float32) * mixed_rows[...].astype(jnp.float32)).T
    grad_key[...] = jnp.zeros_like(grad_key)
    grad_value[...] = jnp.zeros_like(grad_value)
    keys_of = [masked_keys(key_rows[...], mask_low, head) for head in range(2)]

    def tile(index, carry):
        span = pl.ds(pl.multiple_of(index * BACK_TILE, BACK_TILE), BACK_TILE)
        block = index * BACK_TILE // block_rows
        for head in range(2):
            inside = head_lanes(BACK_TILE, head)
            queries = query_rows[span, :]
            grads = grad_mixed[span, :]
            grads = jnp.where(inside, grads, jnp.zeros_like(grads))
            centre = jnp.sum(grad_t[pl.ds(head * HD, HD), span], axis=0, keepdims=True)
            scores = nt_dot(keys_of[head], head_queries(queries, head, block))
            probs = jnp.exp(scores - logs[0, pl.ds(head, 1), span])
            grad_probs = nt_dot(values, grads)
            grad_scores = (probs * (grad_probs - centre)).astype(jnp.bfloat16)
            grad_value[...] += nn_dot(probs.astype(jnp.bfloat16), grads)
            grad_key[...] += nn_dot(grad_scores, jnp.where(inside, queries, jnp.zeros_like(queries)))
            grad_query_t[pl.ds(head * HD, HD), span] = nn_dot(keys_t[head * HD : (head + 1) * HD], grad_scores)
        return carry

    lax.fori_loop(0, rows // BACK_TILE, tile, 0, unroll=True)
    grad_query = grad_query_t[...].T * HD ** (-0.5)
    outs[0][...] = (grad_query * cos[...] + swap_lanes(grad_query * sin[...])).astype(jnp.bfloat16)
    grad_keys = grad_key[...]
    outs[1][...] = (grad_keys * cos[...] + swap_lanes(grad_keys * sin[...])).astype(jnp.bfloat16)
    outs[2][...] = grad_value[...].astype(jnp.bfloat16)


def attend_back_kernel(
    query_rows, key_rows, value_rows, mixed_rows, grad_mixed, logs, cos, sin, mask, normed, w_query, w_key, w_value,
    query_grad, key_grad, value_grad, share_own, share_other, normed_t, share_sum, grads, *scratch
):
    pair = pl.program_id(0)

    @pl.when(pair == 0)
    def _():
        normed_t[...] = normed[...].T
        share_sum[...] = jnp.zeros_like(share_sum)

    parts = tuple(grads.at[:, pl.ds(part * LANES, LANES)] for part in range(3))
    attend_back_pair(
        query_rows, key_rows, value_rows, mixed_rows, grad_mixed, logs, cos, sin, mask, parts, *scratch
    )
    weight_grads = nn_dot(normed_t[...], grads[...]).astype(jnp.bfloat16)
    for part, output in enumerate((query_grad, key_grad, value_grad)):
        output[...] = weight_grads[:, part * LANES : (part + 1) * LANES]
    weights = jnp.concatenate([w_query[...], w_key[...], w_value[...]], axis=1)
    share_sum[...] += nt_dot(grads[...], weights)

    @pl.when(pair == pl.num_programs(0) - 1)
    def _():
        half = share_own.shape[0]
        share_own[...] = share_sum[:half]
        share_other[...] = share_sum[half:].astype(jnp.bfloat16)


def attend_back(query_rows, key_rows, value_rows, mixed_rows, grad_mixed, logs, cosine, sine, mask, normed, w_query, w_key, w_value):
    rows, width = query_rows.shape
    features = normed.shape[1]
    pairs = width // LANES
    wide_block = pl.BlockSpec((rows, LANES), lambda pair: (0, pair))
    table = pl.BlockSpec((rows, LANES), lambda pair: (0, 0))
    columns = pl.BlockSpec((features, LANES), lambda pair: (0, pair))
    half = pl.BlockSpec((rows // 2, features), lambda pair: (0, 0))
    return pl.pallas_call(
        attend_back_kernel,
        grid=(pairs,),
        in_specs=[wide_block] * 5
        + [pl.BlockSpec((1, 2, rows), lambda pair: (pair, 0, 0)), table, table, pl.BlockSpec((rows, 2), lambda pair: (0, 0))]
        + [pl.BlockSpec((rows, features), lambda pair: (0, 0))]
        + [columns] * 3,
        out_specs=[columns] * 3 + [half, half],
        out_shape=[jax.ShapeDtypeStruct((features, width), jnp.bfloat16)] * 3
        + [
            jax.ShapeDtypeStruct((rows // 2, features), jnp.float32),
            jax.ShapeDtypeStruct((rows // 2, features), jnp.bfloat16),
        ],
        scratch_shapes=[
            pltpu.VMEM((features, rows), jnp.bfloat16),
            pltpu.VMEM((rows, features), jnp.float32),
            pltpu.VMEM((rows, 3 * LANES), jnp.bfloat16),
            pltpu.VMEM((LANES, rows), jnp.float32),
            pltpu.VMEM((rows, LANES), jnp.float32),
            pltpu.VMEM((rows, LANES), jnp.float32),
            pltpu.VMEM((LANES, rows), jnp.float32),
        ],
        compiler_params=pltpu.CompilerParams(vmem_limit_bytes=48 * 1024 * 1024),
        cost_estimate=pl.CostEstimate(
            flops=10 * rows * rows * width + 12 * rows * features * width, bytes_accessed=16 * rows * width, transcendentals=rows * rows * width // HD
        ),
    )(query_rows, key_rows, value_rows, mixed_rows, grad_mixed, logs, cosine, sine, mask, normed, w_query, w_key, w_value)


NAMES = ("down", "gate", "up", "out", "query", "key", "value")
CHUNK = {"down": 128, "gate": 64, "up": 64, "out": 128, "query": 128, "key": 128, "value": 128}
SLOW = ("down", "gate")


HIDDEN_TILE = 256


def feed_kernel(
    rows, cots, gate_w, up_w, down_w, out_own, out_other, back_own, back_other, down_grad, gate_grad, grad_up, rows_t, out_sum, back_sum
):
    step = pl.program_id(0)

    @pl.when(step == 0)
    def _():
        rows_t[...] = rows[...].T
        out_sum[...] = jnp.zeros_like(out_sum)
        back_sum[...] = jnp.zeros_like(back_sum)

    gate = nn_dot(rows[...], gate_w[...])
    sigmoid = 1.0 / (1.0 + jnp.exp(-gate))
    silu = gate * sigmoid
    up = nn_dot(rows[...], up_w[...])
    hidden = (silu * up).astype(jnp.bfloat16)
    grad_hidden = nt_dot(cots[...], down_w[...])
    gate_back = (grad_hidden * up * (sigmoid * (1.0 + gate * (1.0 - sigmoid)))).astype(jnp.bfloat16)
    up_back = (grad_hidden * silu).astype(jnp.bfloat16)
    grad_up[...] = up_back
    down_grad[...] = nn_dot(hidden.T, cots[...]).astype(jnp.bfloat16)
    gate_grad[...] = nn_dot(rows_t[...], gate_back).astype(jnp.bfloat16)
    out_sum[...] += nn_dot(hidden, down_w[...])
    back_sum[...] += nt_dot(gate_back, gate_w[...]) + nt_dot(up_back, up_w[...])

    @pl.when(step == pl.num_programs(0) - 1)
    def _():
        half = rows.shape[0] // 2
        out_own[...] = out_sum[:half]
        out_other[...] = out_sum[half:].astype(jnp.bfloat16)
        back_own[...] = back_sum[:half]
        back_other[...] = back_sum[half:]


def feed_forward(rows, cots, gate_w, up_w, down_w):
    count, width = rows.shape
    hidden = gate_w.shape[1]
    whole = pl.BlockSpec((count, width), lambda tile: (0, 0))
    half = pl.BlockSpec((count // 2, width), lambda tile: (0, 0))
    columns = pl.BlockSpec((width, HIDDEN_TILE), lambda tile: (0, tile))
    lines = pl.BlockSpec((HIDDEN_TILE, width), lambda tile: (tile, 0))
    half_wide = jax.ShapeDtypeStruct((count // 2, width), jnp.float32)
    half_low = jax.ShapeDtypeStruct((count // 2, width), jnp.bfloat16)
    return pl.pallas_call(
        feed_kernel,
        grid=(hidden // HIDDEN_TILE,),
        in_specs=[whole, whole, columns, columns, lines],
        out_specs=[half, half, half, half, lines, columns, pl.BlockSpec((count, HIDDEN_TILE), lambda tile: (0, tile))],
        out_shape=[half_wide, half_low, half_wide, half_wide]
        + [
            jax.ShapeDtypeStruct((hidden, width), jnp.bfloat16),
            jax.ShapeDtypeStruct((width, hidden), jnp.bfloat16),
            jax.ShapeDtypeStruct((count, hidden), jnp.bfloat16),
        ],
        scratch_shapes=[
            pltpu.VMEM((width, count), jnp.bfloat16),
            pltpu.VMEM((count, width), jnp.float32),
            pltpu.VMEM((count, width), jnp.float32),
        ],
        compiler_params=pltpu.CompilerParams(vmem_limit_bytes=52 * 1024 * 1024),
        cost_estimate=pl.CostEstimate(
            flops=16 * count * width * hidden, bytes_accessed=12 * width * hidden + 16 * count * width, transcendentals=count * hidden
        ),
    )(rows, cots, gate_w, up_w, down_w)


def partner(values):
    return lax.ppermute(values, "narrow", [(0, 1), (1, 0)])


def rows_of(own, other):
    return jnp.concatenate([own, other], axis=0)


def rotary_pair_tables(position):
    lane = jnp.arange(LANES) % HD
    half_dim = HD // 2
    frequency = ROPE_BASE ** (-2.0 * (lane % half_dim).astype(jnp.float32) / HD)
    angles = position[:, None] * frequency[None, :]
    signs = jnp.where(lane < half_dim, -1.0, 1.0).astype(jnp.float32)
    return (jnp.cos(angles), jnp.sin(angles) * signs)


def on_device(
    tokens,
    window_span,
    valid_len,
    norm1_gain,
    norm1_shift,
    w_query,
    w_key,
    w_value,
    w_out,
    norm2_gain,
    norm2_shift,
    w_gate,
    w_up,
    w_down,
    cotangent,
):
    block_rows = tokens.shape[0]
    own_block = lax.axis_index("narrow")
    joined = window_span[0] == 2
    block_ids = jnp.stack([own_block, 1 - own_block])
    lengths = valid_len[block_ids]
    offsets = jnp.arange(2 * block_rows)
    row_block = offsets // block_rows
    position = offsets % block_rows + block_rows * jnp.repeat(block_ids, block_rows) * joined.astype(jnp.int32)
    cosine, sine = rotary_pair_tables(position.astype(jnp.float32))
    within = offsets % block_rows < jnp.repeat(lengths, block_rows)
    seen = within[:, None] & (joined | (row_block[:, None] == jnp.arange(2)[None, :]))
    mask = jnp.where(seen, 0.0, MASKED).astype(jnp.float32)

    token_values = tokens.astype(jnp.float32)
    normed_one, scaled_one, inverse_one = norm_forward(token_values, norm1_gain, norm1_shift)
    normed_one = normed_one.astype(jnp.bfloat16)
    gathered_one = rows_of(normed_one, partner(normed_one))
    cot_rows = rows_of(cotangent, partner(cotangent))
    projected = [
        jnp.dot(gathered_one, weight, preferred_element_type=jnp.float32)
        for weight in (w_query, w_key, w_value)
    ]
    query_rows, key_rows, value_rows, mixed_rows, logs = attend(*projected, cosine, sine, mask)
    other_share = jnp.dot(mixed_rows[block_rows:], w_out, preferred_element_type=jnp.float32)
    resid_values = (
        token_values
        + jnp.dot(mixed_rows[:block_rows], w_out, preferred_element_type=jnp.float32)
        + partner(other_share)
    )
    normed_two, scaled_two, inverse_two = norm_forward(resid_values, norm2_gain, norm2_shift)
    normed_two = normed_two.astype(jnp.bfloat16)
    gathered_two = rows_of(normed_two, partner(normed_two))
    out_own, out_other, grad_two_own, grad_two_other, down_grad, gate_grad, grad_up = feed_forward(
        gathered_two, cot_rows, w_gate, w_up, w_down
    )
    up_grad = transpose_times(gathered_two, grad_up).astype(jnp.bfloat16)
    out_values = resid_values + out_own + partner(out_other).astype(jnp.float32)
    grad_normed_two = grad_two_own + partner(grad_two_other)
    grad_in_two, gain_two_grad, shift_two_grad = norm_backward(
        grad_normed_two, scaled_two, inverse_two, norm2_gain
    )
    grad_resid = cotangent.astype(jnp.float32) + grad_in_two
    grad_attention = grad_resid.astype(jnp.bfloat16)
    grad_rows = rows_of(grad_attention, partner(grad_attention))
    grad_mixed = times_transpose(grad_rows, w_out).astype(jnp.bfloat16)
    out_grad = transpose_times(mixed_rows, grad_rows).astype(jnp.bfloat16)
    *qkv_grads, grad_one_own, grad_one_other = attend_back(
        query_rows, key_rows, value_rows, mixed_rows, grad_mixed, logs, cosine, sine, mask, gathered_one, w_query, w_key, w_value
    )
    grad_normed_one = grad_one_own + partner(grad_one_other).astype(jnp.float32)
    grad_in_one, gain_one_grad, shift_one_grad = norm_backward(
        grad_normed_one, scaled_one, inverse_one, norm1_gain
    )
    token_grad = grad_resid + grad_in_one
    norm_grads = jnp.stack([gain_one_grad, shift_one_grad, gain_two_grad, shift_two_grad])
    gradients = dict(zip(NAMES, [down_grad, gate_grad, up_grad, out_grad] + qkv_grads))
    fast = [name for name in NAMES if name not in SLOW]
    *fast_sums, norm_summed = summed_over_wide(
        [gradients[n] for n in fast], [CHUNK[n] for n in fast], jnp.pad(norm_grads, ((0, 4), (0, 0))), 1
    )
    sums = dict(zip(fast, fast_sums))
    for name in SLOW:
        sums[name] = lax.psum(gradients[name], "wide")
    down_summed, gate_summed, up_summed, out_summed, query_summed, key_summed, value_summed = [
        sums[name].astype(jnp.float32) for name in NAMES
    ]
    return (
        out_values,
        token_grad,
        norm_summed[0],
        norm_summed[1],
        query_summed,
        key_summed,
        value_summed,
        out_summed,
        norm_summed[2],
        norm_summed[3],
        gate_summed,
        up_summed,
        down_summed,
    )


def solution(mesh):
    fits = mesh.shape["wide"] == PLANES * 4 and mesh.shape["narrow"] == 2
    in_specs = (
        P(("wide", "narrow"), None),
        P("wide"),
        P("wide"),
        P(),
        P(),
        P(None, "narrow"),
        P(None, "narrow"),
        P(None, "narrow"),
        P("narrow", None),
        P(),
        P(),
        P(None, "narrow"),
        P(None, "narrow"),
        P("narrow", None),
        P(("wide", "narrow"), None),
    )
    out_specs = (
        P(("wide", "narrow"), None),
        P(("wide", "narrow"), None),
        P(),
        P(),
        P(None, "narrow"),
        P(None, "narrow"),
        P(None, "narrow"),
        P("narrow", None),
        P(),
        P(),
        P(None, "narrow"),
        P(None, "narrow"),
        P("narrow", None),
    )
    return jax.shard_map(
        on_device if fits else on_device_any_mesh, mesh=mesh, in_specs=in_specs, out_specs=out_specs, check_vma=False
    )
```

```python
import functools

import jax
import jax.numpy as jnp
from jax import lax
from jax.experimental import pallas as pl
from jax.experimental.pallas import tpu as pltpu
from jax.sharding import PartitionSpec as P

MESH = pl.DeviceIdType.MESH

HD = 64


EPSILON = 1e-05
MASKED = -1e30
ROPE_BASE = 10000.0


def times_transpose(left, right):
    return lax.dot_general(
        left, right, (((1,), (1,)), ((), ())), preferred_element_type=jnp.float32
    )


def transpose_times(left, right):
    return lax.dot_general(
        left, right, (((0,), (0,)), ((), ())), preferred_element_type=jnp.float32
    )


def norm_forward(values, norm_gain, norm_shift):
    average = jnp.mean(values, axis=-1, keepdims=True)
    centred = values - average
    inverse = lax.rsqrt(jnp.mean(centred * centred, axis=-1, keepdims=True) + EPSILON)
    scaled = centred * inverse
    return (scaled * norm_gain + norm_shift, scaled, inverse)


def norm_backward(grad_out, scaled, inverse, norm_gain):
    grad_scaled = grad_out * norm_gain
    first_term = jnp.mean(grad_scaled, axis=-1, keepdims=True)
    second_term = jnp.mean(grad_scaled * scaled, axis=-1, keepdims=True)
    grad_in = inverse * (grad_scaled - first_term - scaled * second_term)
    return (grad_in, jnp.sum(grad_out * scaled, axis=0), jnp.sum(grad_out, axis=0))


def rotary_tables(span_table, block_rows, width):
    row_count = span_table.shape[0] * block_rows
    row_ids = jnp.arange(row_count)
    block_ids = row_ids // block_rows
    span_rows = jnp.repeat(span_table, block_rows)
    position = (row_ids % block_rows + block_rows * (block_ids % 2) * (span_rows == 2)).astype(
        jnp.float32
    )
    columns = jnp.arange(width) % HD
    half_dim = HD // 2
    freq_index = (columns % half_dim).astype(jnp.float32)
    frequency = ROPE_BASE ** (-2.0 * freq_index / HD)
    angles = position[:, None] * frequency[None, :]
    signs = jnp.where(columns < half_dim, -1.0, 1.0).astype(jnp.float32)
    return (jnp.cos(angles), jnp.sin(angles) * signs)


def swap_halves(values):
    row_count = values.shape[0]
    width = values.shape[1]
    parts = values.reshape(row_count, width // HD, 2, HD // 2)
    return jnp.flip(parts, axis=2).reshape(row_count, width)


def rotate(values, cosine, sine_signed):
    return values * cosine + swap_halves(values) * sine_signed


def rotate_back(grads_in, cosine, sine_signed):
    return grads_in * cosine + swap_halves(grads_in * sine_signed)


def pair_mask(block_index, span_table, valid_table, block_rows):
    pair_first = block_index // 2 * 2
    offsets = jnp.arange(2 * block_rows)
    key_block = pair_first + offsets // block_rows
    within = offsets % block_rows
    first_len = lax.dynamic_index_in_dim(valid_table, pair_first, keepdims=False)
    second_len = lax.dynamic_index_in_dim(valid_table, pair_first + 1, keepdims=False)
    own_span = lax.dynamic_index_in_dim(span_table, block_index, keepdims=False)
    length_bound = jnp.where(offsets < block_rows, first_len, second_len)
    return (within < length_bound) & ((own_span == 2) | (key_block == block_index))


def on_device_any_mesh(
    tokens,
    window_span,
    valid_len,
    norm1_gain,
    norm1_shift,
    w_query,
    w_key,
    w_value,
    w_out,
    norm2_gain,
    norm2_shift,
    w_gate,
    w_up,
    w_down,
    cotangent,
):
    local_rows = tokens.shape[0]
    group_rows = local_rows * lax.axis_size("narrow")
    block_count = window_span.shape[0]
    block_rows = group_rows // block_count
    local_width = w_query.shape[1]
    local_heads = local_width // HD
    local_hidden = w_gate.shape[1]
    softmax_scale = HD ** (-0.5)
    token_values = tokens.astype(jnp.float32)
    normed_one, scaled_one, inverse_one = norm_forward(token_values, norm1_gain, norm1_shift)
    normed_one = normed_one.astype(jnp.bfloat16)
    gathered_one = lax.all_gather(normed_one, "narrow", axis=0, tiled=True)
    joined_qkv = jnp.concatenate([w_query, w_key, w_value], axis=1)
    projected = jnp.dot(gathered_one, joined_qkv, preferred_element_type=jnp.float32)
    cosine, sine_signed = rotary_tables(window_span, block_rows, local_width)
    query_rows = (rotate(projected[:, :local_width], cosine, sine_signed) * softmax_scale).astype(
        jnp.bfloat16
    )
    key_rows = rotate(projected[:, local_width : 2 * local_width], cosine, sine_signed).astype(
        jnp.bfloat16
    )
    value_rows = projected[:, 2 * local_width :].astype(jnp.bfloat16)

    def block_slices(block_index):
        query_block = lax.dynamic_slice_in_dim(query_rows, block_index * block_rows, block_rows, 0)
        pair_start = block_index // 2 * 2 * block_rows
        return (
            query_block.reshape(block_rows, local_heads, HD),
            key_rows.reshape(2 * block_rows, local_heads, HD),
            value_rows.reshape(2 * block_rows, local_heads, HD),
            pair_start,
        )

    def masked_scores(block_index, query_block, key_pair):
        scores = jnp.einsum(
            "qhd,khd->hqk", query_block, key_pair, preferred_element_type=jnp.float32
        )
        key_mask = pair_mask(block_index, window_span, valid_len, block_rows)
        return jnp.where(key_mask[None, None, :], scores, MASKED)

    def attend_forward(block_index):
        query_block, key_pair, value_pair, pair_start = block_slices(block_index)
        scores = masked_scores(block_index, query_block, key_pair)
        highest = jnp.max(scores, axis=-1, keepdims=True)
        weights = jnp.exp(scores - highest)
        weight_total = jnp.sum(weights, axis=-1, keepdims=True)
        attention_probs = (weights / weight_total).astype(jnp.bfloat16)
        mixed_block = jnp.einsum(
            "hqk,khd->qhd", attention_probs, value_pair, preferred_element_type=jnp.float32
        )
        return (
            mixed_block.reshape(block_rows, local_width).astype(jnp.bfloat16),
            (highest + jnp.log(weight_total))[:, :, 0],
        )

    mixed_blocks, log_totals = lax.map(attend_forward, jnp.arange(block_count))
    mixed_rows = mixed_blocks.reshape(group_rows, local_width)
    resid_values = token_values + lax.psum_scatter(
        jnp.dot(mixed_rows, w_out, preferred_element_type=jnp.float32),
        "narrow",
        scatter_dimension=0,
        tiled=True,
    )
    normed_two, scaled_two, inverse_two = norm_forward(resid_values, norm2_gain, norm2_shift)
    normed_two = normed_two.astype(jnp.bfloat16)
    gathered_two = lax.all_gather(normed_two, "narrow", axis=0, tiled=True)
    joined_gate_up = jnp.concatenate([w_gate, w_up], axis=1)
    gate_up = jnp.dot(gathered_two, joined_gate_up, preferred_element_type=jnp.float32)
    gate_values = gate_up[:, :local_hidden]
    up_values = gate_up[:, local_hidden:]
    sigmoid_gate = jax.nn.sigmoid(gate_values)
    hidden_rows = (gate_values * sigmoid_gate * up_values).astype(jnp.bfloat16)
    out_values = resid_values + lax.psum_scatter(
        jnp.dot(hidden_rows, w_down, preferred_element_type=jnp.float32).astype(jnp.bfloat16),
        "narrow",
        scatter_dimension=0,
        tiled=True,
    ).astype(jnp.float32)
    shard_rows = lax.all_gather(cotangent, "narrow", axis=0, tiled=True)
    grad_hidden = times_transpose(shard_rows, w_down)
    grad_down_w, grad_hidden = (transpose_times(hidden_rows, shard_rows), grad_hidden)
    silu_grad = sigmoid_gate * (1.0 + gate_values * (1.0 - sigmoid_gate))
    grad_gate_up = jnp.concatenate(
        [grad_hidden * up_values * silu_grad, grad_hidden * gate_values * sigmoid_gate], axis=1
    ).astype(jnp.bfloat16)
    grad_normed_two = lax.psum_scatter(
        times_transpose(grad_gate_up, joined_gate_up), "narrow", scatter_dimension=0, tiled=True
    )
    grad_gate_up_w = transpose_times(gathered_two, grad_gate_up)
    grad_in_two, gain_two_grad, shift_two_grad = norm_backward(
        grad_normed_two, scaled_two, inverse_two, norm2_gain
    )
    grad_resid = cotangent.astype(jnp.float32) + grad_in_two
    shard_rows = lax.all_gather(grad_resid.astype(jnp.bfloat16), "narrow", axis=0, tiled=True)
    grad_mixed_sum = times_transpose(shard_rows, w_out)
    grad_out_w, grad_mixed_sum = (transpose_times(mixed_rows, shard_rows), grad_mixed_sum)
    grad_mixed = grad_mixed_sum.astype(jnp.bfloat16)

    def attend_backward(block_index, running):
        grad_query, grad_key, grad_value = running
        query_block, key_pair, value_pair, pair_start = block_slices(block_index)
        grad_rows = lax.dynamic_slice_in_dim(
            grad_mixed, block_index * block_rows, block_rows, 0
        ).reshape(block_rows, local_heads, HD)
        scores = masked_scores(block_index, query_block, key_pair)
        log_total = lax.dynamic_index_in_dim(log_totals, block_index, keepdims=False)
        attention_probs = jnp.exp(scores - log_total[:, :, None])
        grad_probs = jnp.einsum(
            "qhd,khd->hqk", grad_rows, value_pair, preferred_element_type=jnp.float32
        )
        centre = jnp.sum(attention_probs * grad_probs, axis=-1, keepdims=True)
        grad_scores = (attention_probs * (grad_probs - centre)).astype(jnp.bfloat16)
        block_query = jnp.einsum(
            "hqk,khd->qhd", grad_scores, key_pair, preferred_element_type=jnp.float32
        ).reshape(block_rows, local_width)
        pair_key = jnp.einsum(
            "hqk,qhd->khd", grad_scores, query_block, preferred_element_type=jnp.float32
        ).reshape(2 * block_rows, local_width)
        pair_value = jnp.einsum(
            "hqk,qhd->khd",
            attention_probs.astype(jnp.bfloat16),
            grad_rows,
            preferred_element_type=jnp.float32,
        ).reshape(2 * block_rows, local_width)
        grad_query = lax.dynamic_update_slice_in_dim(
            grad_query, block_query, block_index * block_rows, 0
        )
        grad_key = grad_key + pair_key
        grad_value = grad_value + pair_value
        return (grad_query, grad_key, grad_value)

    zero_rows = jnp.zeros((group_rows, local_width), jnp.float32)
    grad_query, grad_key, grad_value = lax.fori_loop(
        0, block_count, attend_backward, (zero_rows, zero_rows, zero_rows)
    )
    grad_query_raw = rotate_back(grad_query * softmax_scale, cosine, sine_signed)
    grad_key_raw = rotate_back(grad_key, cosine, sine_signed)
    grad_qkv = jnp.concatenate([grad_query_raw, grad_key_raw, grad_value], axis=1).astype(
        jnp.bfloat16
    )
    grad_normed_one = lax.psum_scatter(
        times_transpose(grad_qkv, joined_qkv).astype(jnp.bfloat16),
        "narrow",
        scatter_dimension=0,
        tiled=True,
    ).astype(jnp.float32)
    grad_qkv_w = transpose_times(gathered_one, grad_qkv)
    grad_in_one, gain_one_grad, shift_one_grad = norm_backward(
        grad_normed_one, scaled_one, inverse_one, norm1_gain
    )
    token_grad = grad_resid + grad_in_one
    qkv_summed, out_summed, gate_up_summed, down_summed = (
        lax.psum(grad_qkv_w.astype(jnp.bfloat16), "wide").astype(jnp.float32),
        lax.psum(grad_out_w.astype(jnp.bfloat16), "wide").astype(jnp.float32),
        lax.psum(grad_gate_up_w.astype(jnp.bfloat16), "wide").astype(jnp.float32),
        lax.psum(grad_down_w.astype(jnp.bfloat16), "wide").astype(jnp.float32),
    )
    norm_summed = lax.psum(
        (gain_one_grad, shift_one_grad, gain_two_grad, shift_two_grad), ("wide", "narrow")
    )
    return (
        out_values,
        token_grad,
        norm_summed[0],
        norm_summed[1],
        qkv_summed[:, :local_width],
        qkv_summed[:, local_width : 2 * local_width],
        qkv_summed[:, 2 * local_width :],
        out_summed,
        norm_summed[2],
        norm_summed[3],
        gate_up_summed[:, :local_hidden],
        gate_up_summed[:, local_hidden:],
        down_summed,
    )


PLANES = 4


class Job:
    def __init__(self, rows, cols, chunk_rows):
        self.rows, self.cols, self.chunk_rows = rows, cols, chunk_rows
        self.count = rows // (2 * chunk_rows)


def scratch_for(job):
    half, quarter = job.chunk_rows // 2, job.chunk_rows // 4

    def slots(rows):
        return pltpu.VMEM((job.count, 2, rows, job.cols), jnp.bfloat16)

    return [
        pltpu.VMEM((job.rows, job.cols), jnp.bfloat16),
        slots(half),
        slots(half),
        slots(quarter),
        slots(quarter),
        slots(quarter),
        slots(half),
        pltpu.SemaphoreType.DMA((job.count, 2, 9)),
        pltpu.SemaphoreType.DMA((job.count, 2, 9)),
        pltpu.SemaphoreType.DMA((job.count,)),
        pltpu.SemaphoreType.DMA((job.count, 2, 3)),
    ]


OUTER, INWARD, ACROSS, CROSS, BACK, OUT_A, OUT_B, GATHER_A, GATHER_B = range(9)


class Links:
    def __init__(self):
        position = lax.axis_index("wide")
        self.x = lax.rem(position, 2)
        self.y = lax.rem(position // 2, 2)
        self.z = position // 4
        self.middle = jnp.logical_and(self.z >= 1, self.z <= 2)
        self.edge = jnp.logical_or(self.z == 0, self.z == PLANES - 1)
        self.upper = self.z // 2
        self.across = self.at(self.x, self.y, 3 - self.z)
        step = 1 - 2 * self.upper
        self.inward = self.at(self.x, self.y, lax.rem(self.z + step + PLANES, PLANES))
        self.outward = self.at(self.x, self.y, lax.rem(self.z - step + PLANES, PLANES))
        self.flips = [self.at(1 - self.x, self.y, self.z), self.at(self.x, 1 - self.y, self.z)]
        self.bits = [self.x, self.y]

    def at(self, x, y, z):
        return z * 4 + y * 2 + x

    def greet(self):
        barrier = pltpu.get_barrier_semaphore()

        def signal(target):
            pl.semaphore_signal(barrier, inc=1, device_id={"wide": target}, device_id_type=MESH)

        pl.semaphore_signal(
            barrier, inc=1, device_id={"narrow": 1 - lax.axis_index("narrow")}, device_id_type=MESH
        )
        for target in self.flips:
            signal(target)

        @pl.when(self.edge)
        def _():
            signal(self.inward)
            pl.semaphore_wait(barrier, 4)

        @pl.when(self.middle)
        def _():
            signal(self.across)
            signal(self.outward)
            pl.semaphore_wait(barrier, 5)


ADD_ROWS = 16


def add_rows(held, start, other, rows):
    def add(index, carry):
        own = pl.ds(pl.multiple_of(start + index * ADD_ROWS, ADD_ROWS), ADD_ROWS)
        arrived = other[pl.ds(pl.multiple_of(index * ADD_ROWS, ADD_ROWS), ADD_ROWS), :]
        held[own, :] = (held[own, :].astype(jnp.float32) + arrived.astype(jnp.float32)).astype(jnp.bfloat16)
        return carry

    lax.fori_loop(0, rows // ADD_ROWS, add, 0)


class Vectors:
    STEPS = 7

    def __init__(self, links, source, output, stages, arrived, sent, got):
        self.links, self.source, self.output = links, source, output
        self.stages, self.arrived, self.sent, self.got = stages, arrived, sent, got

    def copy(self, number, source, target):
        return pltpu.make_async_remote_copy(
            src_ref=source,
            dst_ref=self.arrived.at[number],
            send_sem=self.sent.at[number],
            recv_sem=self.got.at[number],
            device_id=target,
            device_id_type=MESH,
        )

    def exchange(self, number):
        links = self.links
        targets = [
            {"narrow": 1 - lax.axis_index("narrow")},
            {"wide": links.flips[0]},
            {"wide": links.flips[1]},
            {"wide": links.inward},
            {"wide": links.across},
            {"wide": links.outward},
        ]
        source = self.source if number == 0 else self.stages.at[number]
        return self.copy(number, source, targets[number])

    def add(self, number):
        source = self.source if number == 0 else self.stages.at[number]
        self.stages[number + 1] = source[...] + self.arrived[number]

    def step(self, number):
        links = self.links
        if number in (1, 2, 3):
            self.exchange(number - 1).wait_recv()
            self.add(number - 1)
        if number < 3:
            self.exchange(number).start()
        if number == 3:

            @pl.when(links.edge)
            def _():
                self.exchange(3).start()

        if number in (4, 5):

            @pl.when(links.middle)
            def _():
                self.exchange(number - 1).wait_recv()
                self.add(number - 1)
                self.exchange(number).start()

        if number == 6:

            @pl.when(links.middle)
            def _():
                self.output[...] = self.stages[5]

            @pl.when(links.edge)
            def _():
                self.exchange(5).wait_recv()
                self.output[...] = self.arrived[5]

    def close(self):
        for number in range(3):
            self.exchange(number).wait_send()

        @pl.when(self.links.edge)
        def _():
            self.exchange(3).wait_send()

        @pl.when(self.links.middle)
        def _():
            self.exchange(4).wait_send()
            self.exchange(5).wait_send()


class Chunk:
    STEPS = 8

    def __init__(self, links, job, refs, output, index, colour):
        self.links, self.colour, self.index, self.output = links, colour, index, output
        self.held = refs[0]
        self.pair_in, self.column_in, self.across_in, self.cross_in, self.back_in, self.gather_in = [
            ref.at[index, colour] for ref in refs[1:7]
        ]
        self.sent, self.got, self.loaded, self.stored = refs[7:11]
        self.half, self.quarter = job.chunk_rows // 2, job.chunk_rows // 4
        self.base = (2 * index + colour) * job.chunk_rows
        bit = links.bits[colour]
        self.keep = pl.multiple_of(self.base + bit * self.half, self.quarter)
        self.away = pl.multiple_of(self.base + (1 - bit) * self.half, self.quarter)
        self.near = pl.multiple_of(links.upper * self.quarter, self.quarter)
        self.far = pl.multiple_of((1 - links.upper) * self.quarter, self.quarter)
        self.kept = pl.multiple_of(self.keep + self.near, self.quarter)
        self.given = pl.multiple_of(self.keep + self.far, self.quarter)
        self.outer_peer = links.flips[colour]
        self.inner_peer = links.flips[1 - colour]

    def rows(self, start, size):
        return self.held.at[pl.ds(start, size), :]

    def part(self, ref, start):
        return ref.at[pl.ds(start, self.quarter), :]

    def copy(self, step, source, target, peer):
        return pltpu.make_async_remote_copy(
            src_ref=source,
            dst_ref=target,
            send_sem=self.sent.at[self.index, self.colour, step],
            recv_sem=self.got.at[self.index, self.colour, step],
            device_id={"wide": peer},
            device_id_type=MESH,
        )

    def outer(self):
        return self.copy(OUTER, self.rows(self.away, self.half), self.pair_in, self.outer_peer)

    def inward(self):
        return self.copy(INWARD, self.rows(self.keep, self.half), self.column_in, self.links.inward)

    def across(self):
        return self.copy(ACROSS, self.rows(self.given, self.quarter), self.across_in, self.links.across)

    def cross(self):
        return self.copy(CROSS, self.rows(self.kept, self.quarter), self.cross_in, self.inner_peer)

    def back(self):
        return self.copy(BACK, self.rows(self.kept, self.quarter), self.back_in, self.links.across)

    def out_a(self):
        target = self.part(self.column_in, self.near)
        return self.copy(OUT_A, self.rows(self.kept, self.quarter), target, self.links.outward)

    def out_b(self):
        return self.copy(OUT_B, self.back_in, self.part(self.column_in, self.far), self.links.outward)

    def gather_a(self, source):
        return self.copy(GATHER_A, source, self.part(self.gather_in, self.near), self.outer_peer)

    def gather_b(self, source):
        return self.copy(GATHER_B, source, self.part(self.gather_in, self.far), self.outer_peer)

    def store(self, place, source, start, size):
        target = self.output.at[pl.ds(start, size), :]
        return pltpu.make_async_copy(source, target, self.stored.at[self.index, self.colour, place])

    def totals(self, near, far):
        return self.store(0, near, self.kept, self.quarter), self.store(1, far, self.given, self.quarter)

    def partner_total(self):
        return self.store(2, self.gather_in, self.away, self.half)

    def step(self, number):
        links = self.links
        near_total = self.rows(self.kept, self.quarter)
        edge_near, edge_far = self.part(self.column_in, self.near), self.part(self.column_in, self.far)
        if number == 0:
            self.outer().start()
        if number == 1:
            self.outer().wait_recv()
            add_rows(self.held, self.keep, self.pair_in, self.half)

            @pl.when(links.edge)
            def _():
                self.inward().start()

        if number == 2:

            @pl.when(links.middle)
            def _():
                self.inward().wait_recv()
                add_rows(self.held, self.keep, self.column_in, self.half)
                self.across().start()

        if number == 3:

            @pl.when(links.middle)
            def _():
                self.across().wait_recv()
                add_rows(self.held, self.kept, self.across_in, self.quarter)
                self.cross().start()

        if number == 4:

            @pl.when(links.middle)
            def _():
                self.cross().wait()
                add_rows(self.held, self.kept, self.cross_in, self.quarter)
                self.back().start()
                self.out_a().start()
                self.gather_a(near_total).start()

        if number == 5:

            @pl.when(links.middle)
            def _():
                self.back().wait_recv()
                self.out_b().start()
                self.gather_b(self.back_in).start()
                for store in self.totals(near_total, self.back_in):
                    store.start()

            @pl.when(links.edge)
            def _():
                self.out_a().wait_recv()
                self.gather_a(edge_near).start()

        if number == 6:

            @pl.when(links.edge)
            def _():
                self.out_b().wait_recv()
                self.gather_b(edge_far).start()
                for store in self.totals(edge_near, edge_far):
                    store.start()

        if number == 7:
            self.gather_a(near_total).wait_recv()
            self.gather_b(self.back_in).wait_recv()
            self.partner_total().start()

    def close(self):
        near_total = self.rows(self.kept, self.quarter)
        self.outer().wait_send()
        self.gather_a(near_total).wait_send()
        self.gather_b(self.back_in).wait_send()

        @pl.when(self.links.middle)
        def _():
            self.across().wait_send()
            self.back().wait_send()
            self.out_a().wait_send()
            self.out_b().wait_send()

        @pl.when(self.links.edge)
        def _():
            self.inward().wait_send()

        for store in self.totals(near_total, self.back_in):
            store.wait()
        self.partner_total().wait()


def sum_kernel(jobs, *refs):
    count = len(jobs)
    inputs, refs = refs[: count + 1], refs[count + 1 :]
    outputs, scratch = refs[: count + 1], refs[count + 1 :]
    scratch, vector_scratch = scratch[:-4], scratch[-4:]
    per_job = len(scratch) // count
    links = Links()
    vectors = Vectors(links, inputs[count], outputs[count], *vector_scratch)
    items = []
    for number, job in enumerate(jobs):
        own = scratch[number * per_job : (number + 1) * per_job]
        for index in range(job.count):
            pair = [Chunk(links, job, own, outputs[number], index, colour) for colour in range(2)]
            span = pl.ds(2 * index * job.chunk_rows, 2 * job.chunk_rows)
            load = pltpu.make_async_copy(inputs[number].at[span, :], own[0].at[span, :], own[9].at[index])
            load.start()
            items.append((pair, load))
    links.greet()
    for tick in range(len(items) + Chunk.STEPS - 1):
        if tick < Vectors.STEPS:
            vectors.step(tick)
        for place, (pair, load) in enumerate(items):
            step = tick - place
            if 0 <= step < Chunk.STEPS:
                if step == 0:
                    load.wait()
                for chunk in pair:
                    chunk.step(step)
    for pair, _ in items:
        for chunk in pair:
            chunk.close()
    vectors.close()


def summed_over_wide(gradients, chunk_rows, vectors, collective_id):
    jobs = [Job(g.shape[0], g.shape[1], r) for g, r in zip(gradients, chunk_rows)]
    scratch = []
    for job in jobs:
        scratch += scratch_for(job)
    scratch += [
        pltpu.VMEM((6, *vectors.shape), jnp.float32),
        pltpu.VMEM((6, *vectors.shape), jnp.float32),
        pltpu.SemaphoreType.DMA((6,)),
        pltpu.SemaphoreType.DMA((6,)),
    ]
    sent = sum(2 * g.size * 5 // 4 for g in gradients)
    return pl.pallas_call(
        functools.partial(sum_kernel, jobs),
        out_shape=[jax.ShapeDtypeStruct(g.shape, jnp.bfloat16) for g in gradients]
        + [jax.ShapeDtypeStruct(vectors.shape, jnp.float32)],
        in_specs=[pl.BlockSpec(memory_space=pl.ANY)] * len(jobs) + [pl.BlockSpec(memory_space=pltpu.VMEM)],
        out_specs=[pl.BlockSpec(memory_space=pl.ANY)] * len(jobs) + [pl.BlockSpec(memory_space=pltpu.VMEM)],
        scratch_shapes=scratch,
        compiler_params=pltpu.CompilerParams(
            collective_id=collective_id, has_side_effects=True, vmem_limit_bytes=60 * 1024 * 1024
        ),
        cost_estimate=pl.CostEstimate(flops=0, bytes_accessed=2 * sent, transcendentals=0),
    )(*gradients, vectors)


LANES = 128
QUERY_TILE = 512
BACK_TILE = 256


def nt_dot(left, right):
    return lax.dot_general(
        left, right, (((1,), (1,)), ((), ())), preferred_element_type=jnp.float32
    )


def nn_dot(left, right):
    return jnp.dot(left, right, preferred_element_type=jnp.float32)


def swap_lanes(values):
    lane = lax.broadcasted_iota(jnp.int32, values.shape, 1)
    half_dim = HD // 2
    ahead = pltpu.roll(values, LANES - half_dim, axis=1)
    behind = pltpu.roll(values, half_dim, axis=1)
    return jnp.where(lane % HD < half_dim, ahead, behind)


def head_lanes(rows, head):
    return lax.broadcasted_iota(jnp.int32, (rows, LANES), 1) // HD == head


def masked_keys(keys, mask, head):
    lane = lax.broadcasted_iota(jnp.int32, keys.shape, 1)
    spare = (1 - head) * HD
    keys = jnp.where(lane // HD == head, keys, jnp.zeros_like(keys))
    for block in range(2):
        keys = jnp.where(lane == spare + block, mask[:, block : block + 1], keys)
    return keys


def head_queries(queries, head, block):
    lane = lax.broadcasted_iota(jnp.int32, queries.shape, 1)
    spare = (1 - head) * HD
    queries = jnp.where(lane // HD == head, queries, jnp.zeros_like(queries))
    return jnp.where(lane == spare + block, jnp.ones_like(queries), queries)


def attend_kernel(
    query_raw, key_raw, value_raw, cosine, sine, mask, query_out, key_out, value_out, mixed_out, log_out, mixed_t
):
    rows = query_raw.shape[0]
    block_rows = rows // 2
    cos, sin = cosine[...], sine[...]
    queries = query_raw[...]
    query_out[...] = ((queries * cos + swap_lanes(queries) * sin) * HD ** (-0.5)).astype(jnp.bfloat16)
    keys = key_raw[...]
    key_out[...] = (keys * cos + swap_lanes(keys) * sin).astype(jnp.bfloat16)
    value_out[...] = value_raw[...].astype(jnp.bfloat16)
    values_t = value_out[...].T
    mask_low = mask[...].astype(jnp.bfloat16)
    keys_of = [masked_keys(key_out[...], mask_low, head) for head in range(2)]

    def tile(index, carry):
        span = pl.ds(pl.multiple_of(index * QUERY_TILE, QUERY_TILE), QUERY_TILE)
        block = index * QUERY_TILE // block_rows
        for head in range(2):
            scores = nt_dot(keys_of[head], head_queries(query_out[span, :], head, block))
            highest = jnp.max(scores, axis=0, keepdims=True)
            weights = jnp.exp(scores - highest)
            total = jnp.sum(weights, axis=0, keepdims=True)
            mixed = nn_dot(values_t[head * HD : (head + 1) * HD], weights.astype(jnp.bfloat16)) / total
            mixed_t[pl.ds(head * HD, HD), span] = mixed
            log_out[0, pl.ds(head, 1), span] = highest + jnp.log(total)
        return carry

    lax.fori_loop(0, rows // QUERY_TILE, tile, 0, unroll=True)
    mixed_out[...] = mixed_t[...].T.astype(jnp.bfloat16)


def attend(query_raw, key_raw, value_raw, cosine, sine, mask):
    rows, width = query_raw.shape
    pairs = width // LANES
    wide_block = pl.BlockSpec((rows, LANES), lambda pair: (0, pair))
    table = pl.BlockSpec((rows, LANES), lambda pair: (0, 0))
    low = jax.ShapeDtypeStruct((rows, width), jnp.bfloat16)
    return pl.pallas_call(
        attend_kernel,
        grid=(pairs,),
        in_specs=[wide_block] * 3 + [table, table, pl.BlockSpec((rows, 2), lambda pair: (0, 0))],
        out_specs=[wide_block] * 4 + [pl.BlockSpec((1, 2, rows), lambda pair: (pair, 0, 0))],
        out_shape=[low] * 4 + [jax.ShapeDtypeStruct((pairs, 2, rows), jnp.float32)],
        scratch_shapes=[pltpu.VMEM((LANES, rows), jnp.float32)],
        compiler_params=pltpu.CompilerParams(vmem_limit_bytes=32 * 1024 * 1024),
        cost_estimate=pl.CostEstimate(
            flops=4 * rows * rows * width, bytes_accessed=20 * rows * width, transcendentals=rows * rows * width // HD
        ),
    )(query_raw, key_raw, value_raw, cosine, sine, mask)


def attend_back_pair(
    query_rows, key_rows, value_rows, mixed_rows, grad_mixed, logs, cos, sin, mask, outs, grad_query_t, grad_key, grad_value, grad_t
):
    rows = query_rows.shape[0]
    block_rows = rows // 2
    mask_low = mask[...].astype(jnp.bfloat16)
    keys_t = key_rows[...].T
    values = value_rows[...]
    grad_t[...] = (grad_mixed[...].astype(jnp.float32) * mixed_rows[...].astype(jnp.float32)).T
    grad_key[...] = jnp.zeros_like(grad_key)
    grad_value[...] = jnp.zeros_like(grad_value)
    keys_of = [masked_keys(key_rows[...], mask_low, head) for head in range(2)]

    def tile(index, carry):
        span = pl.ds(pl.multiple_of(index * BACK_TILE, BACK_TILE), BACK_TILE)
        block = index * BACK_TILE // block_rows
        for head in range(2):
            inside = head_lanes(BACK_TILE, head)
            queries = query_rows[span, :]
            grads = grad_mixed[span, :]
            grads = jnp.where(inside, grads, jnp.zeros_like(grads))
            centre = jnp.sum(grad_t[pl.ds(head * HD, HD), span], axis=0, keepdims=True)
            scores = nt_dot(keys_of[head], head_queries(queries, head, block))
            probs = jnp.exp(scores - logs[0, pl.ds(head, 1), span])
            grad_probs = nt_dot(values, grads)
            grad_scores = (probs * (grad_probs - centre)).astype(jnp.bfloat16)
            grad_value[...] += nn_dot(probs.astype(jnp.bfloat16), grads)
            grad_key[...] += nn_dot(grad_scores, jnp.where(inside, queries, jnp.zeros_like(queries)))
            grad_query_t[pl.ds(head * HD, HD), span] = nn_dot(keys_t[head * HD : (head + 1) * HD], grad_scores)
        return carry

    lax.fori_loop(0, rows // BACK_TILE, tile, 0, unroll=True)
    grad_query = grad_query_t[...].T * HD ** (-0.5)
    outs[0][...] = (grad_query * cos[...] + swap_lanes(grad_query * sin[...])).astype(jnp.bfloat16)
    grad_keys = grad_key[...]
    outs[1][...] = (grad_keys * cos[...] + swap_lanes(grad_keys * sin[...])).astype(jnp.bfloat16)
    outs[2][...] = grad_value[...].astype(jnp.bfloat16)


def attend_back_kernel(
    query_rows, key_rows, value_rows, mixed_rows, grad_mixed, logs, cos, sin, mask, normed, w_query, w_key, w_value,
    query_grad, key_grad, value_grad, share_own, share_other, normed_t, share_sum, grads, *scratch
):
    pair = pl.program_id(0)

    @pl.when(pair == 0)
    def _():
        normed_t[...] = normed[...].T
        share_sum[...] = jnp.zeros_like(share_sum)

    parts = tuple(grads.at[:, pl.ds(part * LANES, LANES)] for part in range(3))
    attend_back_pair(
        query_rows, key_rows, value_rows, mixed_rows, grad_mixed, logs, cos, sin, mask, parts, *scratch
    )
    weight_grads = nn_dot(normed_t[...], grads[...]).astype(jnp.bfloat16)
    for part, output in enumerate((query_grad, key_grad, value_grad)):
        output[...] = weight_grads[:, part * LANES : (part + 1) * LANES]
    weights = jnp.concatenate([w_query[...], w_key[...], w_value[...]], axis=1)
    share_sum[...] += nt_dot(grads[...], weights)

    @pl.when(pair == pl.num_programs(0) - 1)
    def _():
        half = share_own.shape[0]
        share_own[...] = share_sum[:half]
        share_other[...] = share_sum[half:].astype(jnp.bfloat16)


def attend_back(query_rows, key_rows, value_rows, mixed_rows, grad_mixed, logs, cosine, sine, mask, normed, w_query, w_key, w_value):
    rows, width = query_rows.shape
    features = normed.shape[1]
    pairs = width // LANES
    wide_block = pl.BlockSpec((rows, LANES), lambda pair: (0, pair))
    table = pl.BlockSpec((rows, LANES), lambda pair: (0, 0))
    columns = pl.BlockSpec((features, LANES), lambda pair: (0, pair))
    half = pl.BlockSpec((rows // 2, features), lambda pair: (0, 0))
    return pl.pallas_call(
        attend_back_kernel,
        grid=(pairs,),
        in_specs=[wide_block] * 5
        + [pl.BlockSpec((1, 2, rows), lambda pair: (pair, 0, 0)), table, table, pl.BlockSpec((rows, 2), lambda pair: (0, 0))]
        + [pl.BlockSpec((rows, features), lambda pair: (0, 0))]
        + [columns] * 3,
        out_specs=[columns] * 3 + [half, half],
        out_shape=[jax.ShapeDtypeStruct((features, width), jnp.bfloat16)] * 3
        + [
            jax.ShapeDtypeStruct((rows // 2, features), jnp.float32),
            jax.ShapeDtypeStruct((rows // 2, features), jnp.bfloat16),
        ],
        scratch_shapes=[
            pltpu.VMEM((features, rows), jnp.bfloat16),
            pltpu.VMEM((rows, features), jnp.float32),
            pltpu.VMEM((rows, 3 * LANES), jnp.bfloat16),
            pltpu.VMEM((LANES, rows), jnp.float32),
            pltpu.VMEM((rows, LANES), jnp.float32),
            pltpu.VMEM((rows, LANES), jnp.float32),
            pltpu.VMEM((LANES, rows), jnp.float32),
        ],
        compiler_params=pltpu.CompilerParams(vmem_limit_bytes=48 * 1024 * 1024),
        cost_estimate=pl.CostEstimate(
            flops=10 * rows * rows * width + 12 * rows * features * width, bytes_accessed=16 * rows * width, transcendentals=rows * rows * width // HD
        ),
    )(query_rows, key_rows, value_rows, mixed_rows, grad_mixed, logs, cosine, sine, mask, normed, w_query, w_key, w_value)


NAMES = ("down", "gate", "up", "out", "query", "key", "value")
CHUNK = {"down": 128, "gate": 64, "up": 64, "out": 128, "query": 128, "key": 128, "value": 128}
SLOW = ("down", "gate")


HIDDEN_TILE = 256


def feed_kernel(
    rows, cots, gate_w, up_w, down_w, out_other, back_other, down_grad, gate_grad, hidden_out, grad_gate, grad_up, rows_t, out_sum, back_sum
):
    step = pl.program_id(0)
    half = out_sum.shape[0]

    @pl.when(step == 0)
    def _():
        rows_t[...] = rows[...].T
        out_sum[...] = jnp.zeros_like(out_sum)
        back_sum[...] = jnp.zeros_like(back_sum)

    gate = nn_dot(rows[...], gate_w[...])
    sigmoid = 1.0 / (1.0 + jnp.exp(-gate))
    silu = gate * sigmoid
    up = nn_dot(rows[...], up_w[...])
    hidden = (silu * up).astype(jnp.bfloat16)
    grad_hidden = nt_dot(cots[...], down_w[...])
    gate_back = (grad_hidden * up * (sigmoid * (1.0 + gate * (1.0 - sigmoid)))).astype(jnp.bfloat16)
    hidden_out[...] = hidden
    grad_gate[...] = gate_back
    up_back = (grad_hidden * silu).astype(jnp.bfloat16)
    grad_up[...] = up_back
    down_grad[...] = nn_dot(hidden.T, cots[...]).astype(jnp.bfloat16)
    gate_grad[...] = nn_dot(rows_t[...], gate_back).astype(jnp.bfloat16)
    out_sum[...] += nn_dot(hidden[half:], down_w[...])
    back_sum[...] += nt_dot(gate_back[half:], gate_w[...]) + nt_dot(up_back[half:], up_w[...])

    @pl.when(step == pl.num_programs(0) - 1)
    def _():
        out_other[...] = out_sum[...].astype(jnp.bfloat16)
        back_other[...] = back_sum[...]


def feed_forward(rows, cots, gate_w, up_w, down_w):
    count, width = rows.shape
    hidden = gate_w.shape[1]
    whole = pl.BlockSpec((count, width), lambda tile: (0, 0))
    half = pl.BlockSpec((count // 2, width), lambda tile: (0, 0))
    columns = pl.BlockSpec((width, HIDDEN_TILE), lambda tile: (0, tile))
    lines = pl.BlockSpec((HIDDEN_TILE, width), lambda tile: (tile, 0))
    units = pl.BlockSpec((count, HIDDEN_TILE), lambda tile: (0, tile))
    return pl.pallas_call(
        feed_kernel,
        grid=(hidden // HIDDEN_TILE,),
        in_specs=[whole, whole, columns, columns, lines],
        out_specs=[half, half, lines, columns, units, units, units],
        out_shape=[
            jax.ShapeDtypeStruct((count // 2, width), jnp.bfloat16),
            jax.ShapeDtypeStruct((count // 2, width), jnp.float32),
            jax.ShapeDtypeStruct((hidden, width), jnp.bfloat16),
            jax.ShapeDtypeStruct((width, hidden), jnp.bfloat16),
        ]
        + [jax.ShapeDtypeStruct((count, hidden), jnp.bfloat16)] * 3,
        scratch_shapes=[
            pltpu.VMEM((width, count), jnp.bfloat16),
            pltpu.VMEM((count // 2, width), jnp.float32),
            pltpu.VMEM((count // 2, width), jnp.float32),
        ],
        compiler_params=pltpu.CompilerParams(vmem_limit_bytes=44 * 1024 * 1024),
        cost_estimate=pl.CostEstimate(
            flops=13 * count * width * hidden, bytes_accessed=10 * width * hidden + 10 * count * width, transcendentals=count * hidden
        ),
    )(rows, cots, gate_w, up_w, down_w)


def partner(values):
    return lax.ppermute(values, "narrow", [(0, 1), (1, 0)])


def rows_of(own, other):
    return jnp.concatenate([own, other], axis=0)


def rotary_pair_tables(position):
    lane = jnp.arange(LANES) % HD
    half_dim = HD // 2
    frequency = ROPE_BASE ** (-2.0 * (lane % half_dim).astype(jnp.float32) / HD)
    angles = position[:, None] * frequency[None, :]
    signs = jnp.where(lane < half_dim, -1.0, 1.0).astype(jnp.float32)
    return (jnp.cos(angles), jnp.sin(angles) * signs)


def on_device(
    tokens,
    window_span,
    valid_len,
    norm1_gain,
    norm1_shift,
    w_query,
    w_key,
    w_value,
    w_out,
    norm2_gain,
    norm2_shift,
    w_gate,
    w_up,
    w_down,
    cotangent,
):
    block_rows = tokens.shape[0]
    own_block = lax.axis_index("narrow")
    joined = window_span[0] == 2
    block_ids = jnp.stack([own_block, 1 - own_block])
    lengths = valid_len[block_ids]
    offsets = jnp.arange(2 * block_rows)
    row_block = offsets // block_rows
    position = offsets % block_rows + block_rows * jnp.repeat(block_ids, block_rows) * joined.astype(jnp.int32)
    cosine, sine = rotary_pair_tables(position.astype(jnp.float32))
    within = offsets % block_rows < jnp.repeat(lengths, block_rows)
    seen = within[:, None] & (joined | (row_block[:, None] == jnp.arange(2)[None, :]))
    mask = jnp.where(seen, 0.0, MASKED).astype(jnp.float32)

    token_values = tokens.astype(jnp.float32)
    normed_one, scaled_one, inverse_one = norm_forward(token_values, norm1_gain, norm1_shift)
    normed_one = normed_one.astype(jnp.bfloat16)
    gathered_one = rows_of(normed_one, partner(normed_one))
    cot_rows = rows_of(cotangent, partner(cotangent))
    projected = [
        jnp.dot(gathered_one, weight, preferred_element_type=jnp.float32)
        for weight in (w_query, w_key, w_value)
    ]
    query_rows, key_rows, value_rows, mixed_rows, logs = attend(*projected, cosine, sine, mask)
    other_share = jnp.dot(mixed_rows[block_rows:], w_out, preferred_element_type=jnp.float32)
    resid_values = (
        token_values
        + jnp.dot(mixed_rows[:block_rows], w_out, preferred_element_type=jnp.float32)
        + partner(other_share)
    )
    normed_two, scaled_two, inverse_two = norm_forward(resid_values, norm2_gain, norm2_shift)
    normed_two = normed_two.astype(jnp.bfloat16)
    gathered_two = rows_of(normed_two, partner(normed_two))
    out_other, grad_two_other, down_grad, gate_grad, hidden_rows, grad_gate, grad_up = feed_forward(
        gathered_two, cot_rows, w_gate, w_up, w_down
    )
    up_grad = transpose_times(gathered_two, grad_up).astype(jnp.bfloat16)
    out_values = (
        resid_values
        + jnp.dot(hidden_rows[:block_rows], w_down, preferred_element_type=jnp.float32)
        + partner(out_other).astype(jnp.float32)
    )
    grad_normed_two = (
        times_transpose(grad_gate[:block_rows], w_gate)
        + times_transpose(grad_up[:block_rows], w_up)
        + partner(grad_two_other)
    )
    grad_normed_two, up_grad = lax.optimization_barrier((grad_normed_two, up_grad))
    grad_in_two, gain_two_grad, shift_two_grad = norm_backward(
        grad_normed_two, scaled_two, inverse_two, norm2_gain
    )
    grad_resid = cotangent.astype(jnp.float32) + grad_in_two
    grad_attention = grad_resid.astype(jnp.bfloat16)
    grad_rows = rows_of(grad_attention, partner(grad_attention))
    grad_mixed = times_transpose(grad_rows, w_out).astype(jnp.bfloat16)
    out_grad = transpose_times(mixed_rows, grad_rows).astype(jnp.bfloat16)
    *qkv_grads, grad_one_own, grad_one_other = attend_back(
        query_rows, key_rows, value_rows, mixed_rows, grad_mixed, logs, cosine, sine, mask, gathered_one, w_query, w_key, w_value
    )
    grad_normed_one = grad_one_own + partner(grad_one_other).astype(jnp.float32)
    grad_in_one, gain_one_grad, shift_one_grad = norm_backward(
        grad_normed_one, scaled_one, inverse_one, norm1_gain
    )
    token_grad = grad_resid + grad_in_one
    norm_grads = jnp.stack([gain_one_grad, shift_one_grad, gain_two_grad, shift_two_grad])
    gradients = dict(zip(NAMES, [down_grad, gate_grad, up_grad, out_grad] + qkv_grads))
    fast = [name for name in NAMES if name not in SLOW]
    *fast_sums, norm_summed = summed_over_wide(
        [gradients[n] for n in fast], [CHUNK[n] for n in fast], jnp.pad(norm_grads, ((0, 4), (0, 0))), 1
    )
    sums = dict(zip(fast, fast_sums))
    for name in SLOW:
        sums[name] = lax.psum(gradients[name], "wide")
    down_summed, gate_summed, up_summed, out_summed, query_summed, key_summed, value_summed = [
        sums[name].astype(jnp.float32) for name in NAMES
    ]
    return (
        out_values,
        token_grad,
        norm_summed[0],
        norm_summed[1],
        query_summed,
        key_summed,
        value_summed,
        out_summed,
        norm_summed[2],
        norm_summed[3],
        gate_summed,
        up_summed,
        down_summed,
    )


def solution(mesh):
    fits = mesh.shape["wide"] == PLANES * 4 and mesh.shape["narrow"] == 2
    in_specs = (
        P(("wide", "narrow"), None),
        P("wide"),
        P("wide"),
        P(),
        P(),
        P(None, "narrow"),
        P(None, "narrow"),
        P(None, "narrow"),
        P("narrow", None),
        P(),
        P(),
        P(None, "narrow"),
        P(None, "narrow"),
        P("narrow", None),
        P(("wide", "narrow"), None),
    )
    out_specs = (
        P(("wide", "narrow"), None),
        P(("wide", "narrow"), None),
        P(),
        P(),
        P(None, "narrow"),
        P(None, "narrow"),
        P(None, "narrow"),
        P("narrow", None),
        P(),
        P(),
        P(None, "narrow"),
        P(None, "narrow"),
        P("narrow", None),
    )
    return jax.shard_map(
        on_device if fits else on_device_any_mesh, mesh=mesh, in_specs=in_specs, out_specs=out_specs, check_vma=False
    )
```
